32 devices in a mesh: ctx: 8 (over z, x), wa: 4 (over y, core).
Axes of the slice: x: 2, y: 2, z: 4, core: 2. Of those that a mesh axis runs over, the one named last changes fastest.
Arguments:
- tokens: bfloat16 [4, 1024, 768], P('wa', 'ctx'), may hold values from -6 to 6
- lengths: int32 [4], P('wa'), may hold values from 513 to 1024, as said below
- qkv_weight: bfloat16 [768, 2304], P('wa'), may hold values from -0.21875 to 0.21875
- out_weight: bfloat16 [768, 768], P('wa'), may hold values from -6 to 6
- up_weight: bfloat16 [768, 3072], P('wa'), may hold values from -0.21875 to 0.21875
- down_weight: bfloat16 [3072, 768], P('wa'), may hold values from -0.109375 to 0.109375
- qv_bias: bfloat16 [1536], P('wa'), may hold values from -3 to 3
- out_bias: bfloat16 [768], P('wa'), may hold values from -3 to 3
- up_bias: bfloat16 [3072], P('wa'), may hold values from -3 to 3
- down_bias: bfloat16 [768], P('wa'), may hold values from -3 to 3
- gain_one: bfloat16 [768], P('wa'), may hold values from 0.25 to 1.75
- shift_one: bfloat16 [768], P('wa'), may hold values from -3 to 3
- gain_two: bfloat16 [768], P('wa'), may hold values from 0.25 to 1.75
- shift_two: bfloat16 [768], P('wa'), may hold values from -3 to 3
- cotangent: bfloat16 [4, 1024, 768], P('wa', 'ctx'), may hold values from -6 to 6
Outputs:
- output: bfloat16 [4, 1024, 768], P('wa', 'ctx')
- grad_tokens: bfloat16 [4, 1024, 768], P('wa', 'ctx')
- grad_qkv_weight: float32 [768, 2304], P('wa')
- grad_out_weight: float32 [768, 768], P('wa')
- grad_up_weight: float32 [768, 3072], P('wa')
- grad_down_weight: float32 [3072, 768], P('wa')
- grad_qv_bias: float32 [1536], P('wa')
- grad_out_bias: float32 [768], P('wa')
- grad_up_bias: float32 [3072], P('wa')
- grad_down_bias: float32 [768], P('wa')
- grad_gain_one: float32 [768], P('wa')
- grad_shift_one: float32 [768], P('wa')
- grad_gain_two: float32 [768], P('wa')
- grad_shift_two: float32 [768], P('wa')
The draws below stay inside these ranges and needn't reach their ends.
Inputs may be any that keep to these rules, and one draw needn't show every extreme that they name: `lengths`: each sequence's count of valid tokens is more than half of its 1024 slots; in every draw some sequence has all 1024 valid.
All inputs are finite; a program needn't handle non-finite values.
Results may differ from the reference program's by a relative error of at most 0.015.
Values may be sent and summed in bfloat16 or wider, within the bound.
A program may use at most 192 MiB of HBM per device.

```python
import math
import jax
import jax.numpy as jnp
from jax import lax

D = 768
HEADS = 12
HEAD = 64
FF = 3072
SLOTS = 1024
SEQS = 4


def draw_lengths(key, part):
    base_len = jax.random.randint(key, (SEQS,), SLOTS // 2 + 1, SLOTS + 1)
    chosen = jax.random.randint(jax.random.fold_in(key, 7), (), 0, SEQS)
    return jnp.where(jnp.arange(SEQS) == chosen, SLOTS, base_len).astype(jnp.int32)


def level_of(rng, shape, split, smallest, high):
    level = 1.0
    for axis_at, shards_of in split:
        steps = jax.random.uniform(jax.random.fold_in(jax.random.fold_in(rng, 6), axis_at), (shards_of,), jnp.float32, smallest / len(split), high / len(split))
        level = level * jnp.repeat(jnp.exp(steps), shape[axis_at] // shards_of).reshape((-1,) + (1,) * (len(shape) - 1 - axis_at))
    return level


def bell_draw(rng, dims, deviation, reach, cuts=(), dtype=jnp.bfloat16):
    gain = level_of(rng, dims, cuts, -0.22, 0.18) if cuts else 1.0
    values = jax.random.normal(rng, dims, jnp.float32) * deviation * gain
    return jnp.minimum(jnp.maximum(values, -reach), reach).astype(dtype)


def setup_inputs(seed: int = 0) -> dict:
    arg_keys = jax.random.split(jax.random.key(seed), 16)
    return {
        "tokens": bell_draw(arg_keys[0], (SEQS, SLOTS, D), 1.0, 6.0, ((0, 4), (1, 8))),
        "lengths": draw_lengths(jax.random.fold_in(arg_keys[15], 71), 0),
        "qkv_weight": bell_draw(arg_keys[2], (D, 3 * D), D ** -0.5, 0.21875, ((0, 4),)),
        "out_weight": bell_draw(arg_keys[3], (D, D), 1 ** -0.5, 6.0, ((0, 4),)),
        "up_weight": bell_draw(arg_keys[4], (D, FF), D ** -0.5, 0.21875, ((0, 4),)),
        "down_weight": bell_draw(arg_keys[5], (FF, D), FF ** -0.5, 0.109375, ((0, 4),)),
        "qv_bias": bell_draw(arg_keys[6], (2 * D,), 0.5, 3.0, ((0, 4),)),
        "out_bias": bell_draw(arg_keys[7], (D,), 0.5, 3.0, ((0, 4),)),
        "up_bias": bell_draw(arg_keys[8], (FF,), 0.5, 3.0, ((0, 4),)),
        "down_bias": bell_draw(arg_keys[9], (D,), 0.5, 3.0, ((0, 4),)),
        "gain_one": jnp.clip(1.0 + 0.15 * jax.random.normal(arg_keys[10], (D,), jnp.float32), 0.25, 1.75).astype(jnp.bfloat16),
        "shift_one": bell_draw(arg_keys[11], (D,), 0.5, 3.0, ((0, 4),)),
        "gain_two": jnp.clip(1.0 + 0.15 * jax.random.normal(arg_keys[12], (D,), jnp.float32), 0.25, 1.75).astype(jnp.bfloat16),
        "shift_two": bell_draw(arg_keys[13], (D,), 0.5, 3.0, ((0, 4),)),
        "cotangent": bell_draw(arg_keys[14], (SEQS, SLOTS, D), 1.0, 6.0, ((0, 4), (1, 8))),
    }


eps_norm = 1e-12
floor_score = -1e+30
highest = lax.Precision.HIGHEST

@jax.custom_vjp
def low(v):
    return lax.optimization_barrier(v.astype(jnp.bfloat16)).astype(jnp.float32)

@jax.custom_vjp
def low_back(v):
    return v

def low_keep(v):
    return (low(v), None)

def low_pass(kept, grad):
    return (grad,)

def back_keep(v):
    return (v, None)

def back_low(kept, grad):
    return (low(grad),)
low.defvjp(low_keep, low_pass)
low_back.defvjp(back_keep, back_low)

def layer_norm(summed, gain_vec, shift_vec):
    center = summed - lax.optimization_barrier(jnp.mean(summed, -1, keepdims=True))
    spread = lax.optimization_barrier(jnp.mean(center * center, -1, keepdims=True))
    return center * lax.rsqrt(spread + eps_norm) * gain_vec + shift_vec

def attend_block(query_block, key_heads, value_heads, alive_keys):
    score_scale = HEAD ** (-0.5)
    scores = jnp.einsum('qhe,khe->hqk', query_block, key_heads, precision=highest) * score_scale
    scores = low_back(jnp.where(alive_keys[None, None, :], scores, floor_score))
    attn_prob = jax.nn.softmax(scores, axis=-1)
    return jnp.einsum('hqk,khe->qhe', attn_prob, value_heads, precision=highest)

def sequence(seq_rows, length, weights):
    qkv_w, out_w, up_w, down_w, qv_b, out_b, up_b, down_b, gain_a, shift_a, gain_b, shift_b = weights
    model_width = seq_rows.shape[1]
    block_rows = math.gcd(SLOTS, 512)
    projected = jnp.dot(seq_rows, qkv_w, precision=highest)
    queries = low_back(low(projected[:, :model_width] + qv_b[:model_width]))
    key_rows = low_back(low(projected[:, model_width:2 * model_width]))
    values = low_back(low(projected[:, 2 * model_width:] + qv_b[model_width:]))
    alive_keys = jnp.arange(SLOTS) < length
    key_heads = key_rows.reshape(SLOTS, HEADS, HEAD)
    value_heads = values.reshape(SLOTS, HEADS, HEAD)
    query_blocks = queries.reshape(SLOTS // block_rows, block_rows, HEADS, HEAD)
    attended = lax.map(jax.checkpoint(lambda query_block: attend_block(query_block, key_heads, value_heads, alive_keys)), query_blocks)
    mixed = low_back(low(attended.reshape(SLOTS, model_width)))
    branch = low_back(jnp.dot(mixed, out_w, precision=highest) + out_b)
    normed = layer_norm(seq_rows + branch, gain_a, shift_a)
    hidden = low_back(jnp.dot(low(normed), up_w, precision=highest) + up_b)
    activated = low(jax.nn.gelu(hidden, approximate=False))
    ffn_out = low_back(jnp.dot(activated, down_w, precision=highest) + down_b)
    return layer_norm(normed + ffn_out, gain_b, shift_b)

def reference(tokens, lengths, qkv_weight, out_weight, up_weight, down_weight, qv_bias, out_bias, up_bias, down_bias, gain_one, shift_one, gain_two, shift_two, cotangent):
    params = (qkv_weight.astype(jnp.float32), out_weight.astype(jnp.float32), up_weight.astype(jnp.float32), down_weight.astype(jnp.float32), qv_bias.astype(jnp.float32), out_bias.astype(jnp.float32), up_bias.astype(jnp.float32), down_bias.astype(jnp.float32), gain_one.astype(jnp.float32), shift_one.astype(jnp.float32), gain_two.astype(jnp.float32), shift_two.astype(jnp.float32))
    inputs = tokens.astype(jnp.float32)

    def forward(inputs_all, weights):

        def per_seq(member):
            return jax.checkpoint(sequence)(member[0], member[1], weights)
        return lax.map(per_seq, (inputs_all, lengths))
    outputs, back_fn = jax.vjp(forward, inputs, params)
    positions = jnp.arange(SLOTS)
    live_rows = (positions[None, :] < lengths[:, None]).astype(jnp.float32)
    grad_out = cotangent.astype(jnp.float32) * live_rows[:, :, None]
    grad_inputs, grad_params = back_fn(grad_out)
    return (outputs.astype(jnp.bfloat16), grad_inputs.astype(jnp.bfloat16), grad_params[0], grad_params[1], grad_params[2], grad_params[3], grad_params[4], grad_params[5], grad_params[6], grad_params[7], grad_params[8], grad_params[9], grad_params[10], grad_params[11])
```

```python
import functools
import math
from types import SimpleNamespace

import jax
import jax.numpy as jnp
from jax import lax
from jax.experimental import pallas as pl
from jax.experimental.pallas import tpu as pltpu
from jax.sharding import PartitionSpec as P

HEADS = 12
HEAD = 64
EPS = 1e-12
FLOOR = -1e30
MESH = pl.DeviceIdType.MESH
BF = jnp.bfloat16
F32 = jnp.float32

OUTB, DOWNB, GAIN1, SHIFT1, GAIN2, SHIFT2, LEN = range(7)
VROWS = 16
GROWS = 8


def dot(a, b):
    return lax.dot_general(a, b, (((1,), (0,)), ((), ())), preferred_element_type=F32)


def dot_nt(a, b):
    return lax.dot_general(a, b, (((1,), (1,)), ((), ())), preferred_element_type=F32)


def dot_tn(a, b):
    return lax.dot_general(a, b, (((0,), (0,)), ((), ())), preferred_element_type=F32)


def norm_stats(v):
    center = v - jnp.mean(v, -1, keepdims=True)
    rstd = lax.rsqrt(jnp.mean(center * center, -1, keepdims=True) + EPS)
    return center * rstd, rstd


def norm_back(dy, normed, rstd, gain):
    dn = dy * gain
    return rstd * (
        dn - jnp.mean(dn, -1, keepdims=True) - normed * jnp.mean(dn * normed, -1, keepdims=True)
    )


def col_sum(v):
    return jnp.sum(v, 0, keepdims=True)


def make_plan(cfg):
    C, W, B, D, FW, DW, DP, KVW, MW, R = (
        cfg.C, cfg.W, cfg.B, cfg.D, cfg.FW, cfg.DW, cfg.DP, cfg.KVW, cfg.MW, cfg.R)
    V = pltpu.VMEM
    dma = pltpu.SemaphoreType.DMA
    Q = W * B
    plan = dict(
        Xall=V((W, B, D), BF), Wc=V((D, MW), BF), Bb=V((W, 16, MW), BF), Vv=V((W, VROWS, D), F32),
        Vs=V((VROWS, D), F32), Outp=V((W, DP, D), BF), Upc=V((D, FW), BF), Dn=V((FW, D), BF), Cot=V((B, D), BF),
        QKVs=V((W, B, MW), BF), Rq=V((W, B, MW), BF), KV=V((R * Q, KVW), BF),
        Qm=V((cfg.HW, Q, DP), BF), Dm=V((cfg.HW, Q, DP), BF),
        mrow=V((8, Q), F32), lrow=V((8, Q), F32), drow=V((8, Q), F32), OT=V((DP, Q), F32), dQT=V((DP, Q), F32),
        Osend=V((W, B, DP), BF), Mix=V((W, B, DP), BF), MixT=V((W, B, DP), BF),
        N1f=V((B, D), F32), n1=V((B, D), F32), n2=V((B, D), F32), r1=V((B, 1), F32),
        N1all=V((W, B, D), BF), Hp=V((W, B, FW), F32), Gs=V((W, B, FW), BF),
        Fs=V((W, B, D), BF), Fr=V((3, B, D), BF), dR2=V((B, D), F32), dFall=V((W, B, D), BF),
        dHs=V((W, B, FW), BF), dNs=V((W, B, D), BF), dNr=V((3, B, D), BF), dR1=V((B, D), F32),
        dAall=V((W, B, D), BF), dOs=V((W, B, DP), BF), dOr=V((W, B, DP), BF),
        dKVf=V((R * Q, KVW), F32), dKVs=V((R, Q, KVW), BF), dKVr=V((R, Q, KVW), BF),
        dqs=V((W, B, MW), BF), dqr=V((W, B, MW), BF), dxs=V((W, B, D), BF), dxr=V((3, B, D), BF),
        gv=V((GROWS, D), F32),
    )
    sems = dict(
        x=4, wq=4, bb=4, vv=4, ow=4, uw=4, own=8,
        q=W, kv=(R - 1) * W, o=W, mt=4, n=4, f=4, df=4, dn=4, da=4, do=W, dkv=R - 1, dq=W, dx=4,
    )
    recvs = dict(sems, kv=R * W, dkv=R, q=W)
    if cfg.fused:
        NZ = C // 2
        for name, (ch, cols, to_rows) in cfg.grads.items():
            plan["G" + name] = V((NZ, 2, ch, cols), BF)
            plan["X" + name] = V((NZ, ch, cols), BF)
            plan["S" + name] = V((NZ, ch, cols), BF)
            plan["Z" + name] = V((NZ, ch, cols), BF)
            plan["R" + name] = V((ch, cols), BF)
            plan["F" + name] = V((2, W, ch, cols) if to_rows else (NZ, 2, ch, cols), BF)
            for kind in ("gx", "gz", "ga", "gf"):
                sems[kind + name] = NZ + 1
                recvs[kind + name] = NZ + 1
            sems["gw" + name] = 1
            recvs["gw" + name] = W
        plan.update(Vx=V((GROWS, D), F32), Vy=V((GROWS, D), F32), Vz=V((NZ, GROWS, D), F32),
                    Vw=V((W, GROWS, D), F32))
        sems.update(vx=1, vz=NZ, vw=4)
        recvs.update(vx=1, vz=NZ, vw=4)
    for name, n in sems.items():
        plan["s_" + name] = dma((n,))
    for name, n in recvs.items():
        plan["r_" + name] = dma((n,))
    return plan


def layer_kernel(cfg, names, n_in, *refs):
    (x_ref, cot_ref, wq_ref, bias_ref, vec_ref, upb_ref, out_ref, up_ref, down_ref) = refs[:n_in]
    y_ref, gx_ref, gqkv_ref, gout_ref, gup_ref, gdown_ref, gvec_ref = refs[n_in : n_in + 7]
    m = SimpleNamespace(**dict(zip(names, refs[n_in + 7 :])))
    C, W, B, D, DW, DP, KVW, MW, R, HW = (
        cfg.C, cfg.W, cfg.B, cfg.D, cfg.DW, cfg.DP, cfg.KVW, cfg.MW, cfg.R, cfg.HW)
    OFF = DP - DW
    Q = W * B
    c = lax.axis_index("ctx")
    w = lax.axis_index("wa")
    block_part = lax.rem(c, R)
    block_slot = lax.div(c, R)
    s = lax.div(c, R)
    low = lax.rem(c, R)
    g_att = lax.div(w, 2) * 2 + lax.rem(low, 2)
    r_att = lax.div(low, 2) * 2 + lax.rem(w, 2)

    def att_device(t, g, r):
        return (t * R + lax.div(r, 2) * 2 + lax.rem(g, 2), lax.div(g, 2) * 2 + lax.rem(r, 2))

    def is_me(dev):
        return jnp.logical_and(dev[0] == c, dev[1] == w)

    drains = []

    def remote(src, dst, ss, rs, dev):
        return pltpu.make_async_remote_copy(
            src_ref=src, dst_ref=dst, send_sem=ss, recv_sem=rs, device_id=dev, device_id_type=MESH)

    def send(src, dst, ss, rs, dev, pred=None):
        def go():
            remote(src, dst, ss, rs, dev).start()

        def end():
            remote(src, dst, ss, rs, dev).wait_send()

        if pred is None:
            go()
        else:
            pl.when(pred)(go)
        drains.append((pred, end))

    def arrive(dst, rs, pred=None):
        def go():
            remote(dst, dst, rs, rs, (c, w)).wait_recv()

        if pred is None:
            go()
        else:
            pl.when(pred)(go)

    barrier = pltpu.get_barrier_semaphore()

    def greet(i, carry):
        ci, wi = lax.div(i, W), lax.rem(i, W)

        @pl.when(jnp.logical_not(is_me((ci, wi))))
        def _():
            pl.semaphore_signal(barrier, inc=1, device_id=(ci, wi), device_id_type=MESH)

        return carry

    lax.fori_loop(0, C * W, greet, 0)
    pl.semaphore_wait(barrier, C * W - 1)

    def peer(k):
        return (c, jnp.bitwise_xor(w, k))

    def gather_start(buf, ss, rs):
        send(buf.at[w], buf.at[w], ss.at[2], rs.at[2], peer(2))
        send(buf.at[w], buf.at[w], ss.at[1], rs.at[1], peer(1))

    def gather_wait(buf, ss, rs, k):
        if k == 1:
            arrive(buf.at[jnp.bitwise_xor(w, 1)], rs.at[1])
        if k == 2:
            t = jnp.bitwise_xor(w, 2)
            arrive(buf.at[t], rs.at[2])
            send(buf.at[t], buf.at[t], ss.at[3], rs.at[3], peer(1))
        if k == 3:
            arrive(buf.at[jnp.bitwise_xor(w, 3)], rs.at[3])

    def scatter_sum(part, stage, recv, ss, rs):
        t3, t2, t1 = (jnp.bitwise_xor(w, k) for k in (3, 2, 1))
        stage[t3] = part(t3).astype(BF)
        send(stage.at[t3], recv.at[1], ss.at[1], rs.at[1], peer(1))
        mine2 = part(t2)
        arrive(recv.at[1], rs.at[1])
        stage[t2] = (mine2 + recv[1].astype(F32)).astype(BF)
        send(stage.at[t2], recv.at[2], ss.at[2], rs.at[2], peer(2))
        stage[t1] = part(t1).astype(BF)
        send(stage.at[t1], recv.at[0], ss.at[0], rs.at[0], peer(1))
        own = part(w)
        arrive(recv.at[0], rs.at[0])
        own = own + recv[0].astype(F32)
        arrive(recv.at[2], rs.at[2])
        return own + recv[2].astype(F32)

    def local(src, dst, sem):
        cp = pltpu.make_async_copy(src, dst, sem)
        cp.start()
        return cp

    rows_w = pl.ds(w * DW, DW)
    own = [
        local(x_ref, m.Xall.at[w], m.s_own.at[0]),
        local(wq_ref.at[w], m.Wc.at[rows_w], m.s_own.at[1]),
        local(bias_ref.at[w], m.Bb.at[w], m.s_own.at[2]),
        local(vec_ref, m.Vv.at[w], m.s_own.at[3]),
        local(out_ref, m.Outp.at[w, pl.ds(OFF, DW)], m.s_own.at[4]),
        local(up_ref.at[:, pl.ds(pl.multiple_of(w * cfg.FW, cfg.FW), cfg.FW)], m.Upc.at[rows_w], m.s_own.at[5]),
        local(down_ref, m.Dn, m.s_own.at[6]),
        local(cot_ref, m.Cot, m.s_own.at[7]),
    ]
    for k in (2, 3, 1):
        t = jnp.bitwise_xor(w, k)
        send(wq_ref.at[t], m.Wc.at[rows_w], m.s_wq.at[k], m.r_wq.at[k], peer(k))
        send(bias_ref.at[t], m.Bb.at[w], m.s_bb.at[k], m.r_bb.at[k], peer(k))
        send(vec_ref, m.Vv.at[w], m.s_vv.at[k], m.r_vv.at[k], peer(k))
    own[0].wait()
    gather_start(m.Xall, m.s_x, m.r_x)
    for t in range(W):
        m.Outp[t, 0:OFF, :] = jnp.zeros((OFF, D), BF)
    for cp in own[1:]:
        cp.wait()
    for k in (1, 2, 3):
        t = jnp.bitwise_xor(w, k)
        arrive(m.Wc.at[pl.ds(t * DW, DW)], m.r_wq.at[k])
        arrive(m.Bb.at[t], m.r_bb.at[k])
        arrive(m.Vv.at[t], m.r_vv.at[k])
        gather_wait(m.Xall, m.s_x, m.r_x, k)
    for k in (2, 3, 1):
        t = jnp.bitwise_xor(w, k)
        send(out_ref, m.Outp.at[w, pl.ds(OFF, DW)], m.s_ow.at[k], m.r_ow.at[k], peer(k))
    for k in (2, 3, 1):
        t = jnp.bitwise_xor(w, k)
        send(up_ref.at[:, pl.ds(pl.multiple_of(t * cfg.FW, cfg.FW), cfg.FW)], m.Upc.at[rows_w],
             m.s_uw.at[k], m.r_uw.at[k], peer(k))

    vsum = m.Vv[0]
    bias = m.Bb[0, 0:1, :].astype(F32)
    for t in range(1, W):
        vsum = vsum + m.Vv[t]
        bias = bias + m.Bb[t, 0:1, :].astype(F32)
    m.Vs[...] = vsum

    def vec(row):
        return m.Vs[row : row + 1, :]

    for k in range(W):
        t = lax.rem(s + 1 + k, W)
        m.QKVs[t] = (dot(m.Xall[t], m.Wc[...]) + bias).astype(BF)
        dev = att_device(t, w, block_part)
        send(m.QKVs.at[t], m.Rq.at[block_slot], m.s_q.at[k], m.r_q.at[block_slot], dev,
             jnp.logical_not(is_me(dev)))

        @pl.when(is_me(dev))
        def _():
            m.Rq[block_slot] = m.QKVs[t]

    lanes = lax.broadcasted_iota(jnp.int32, (1, DP), 1)

    def q_lane(h):
        return jnp.logical_and(lanes >= h * HEAD, lanes < (h + 1) * HEAD)

    def v_lane(h):
        return jnp.logical_and(lanes >= OFF + h * HEAD, lanes < OFF + (h + 1) * HEAD)

    for j in range(W):
        src = (j * R + r_att, g_att)
        arrive(m.Rq.at[j], m.r_q.at[j], jnp.logical_not(is_me(src)))
        kv_rows = pl.ds(pl.multiple_of(r_att * Q + j * B, B), B)
        for k in range(1, R):
            dev = att_device(s, g_att, lax.rem(r_att + k, R))
            send(m.Rq.at[j, :, pl.ds(0, KVW)], m.KV.at[kv_rows], m.s_kv.at[(k - 1) * W + j],
                 m.r_kv.at[r_att * W + j], dev)
        m.KV[kv_rows, :] = m.Rq[j, :, 0:KVW]
        q = m.Rq[j, :, KVW:MW] * jnp.asarray(HEAD**-0.5, BF)
        for h in range(HW):
            m.Qm[h, j * B : (j + 1) * B, :] = jnp.where(q_lane(h), q, jnp.zeros_like(q))
    for k in range(1, R):
        r = lax.rem(r_att + k, R)
        for j in range(W):
            arrive(m.KV.at[pl.ds(pl.multiple_of(r * Q + j * B, B), B)], m.r_kv.at[r * W + j])

    KC = 2 * B
    PER_SET = Q // KC
    len_s = m.Vs[pl.ds(LEN + s, 1), 0:Q]

    def alive(chunk):
        r, half = lax.div(chunk, PER_SET), lax.rem(chunk, PER_SET)
        row = lax.broadcasted_iota(jnp.int32, (KC, Q), 0)
        later = (row >= B).astype(jnp.int32)
        place = ((2 * half + later) * R + r) * B + row - later * B
        return place.astype(F32) < len_s

    m.mrow[...] = jnp.full(m.mrow.shape, FLOOR, F32)
    m.lrow[...] = jnp.zeros(m.lrow.shape, F32)
    m.OT[...] = jnp.zeros(m.OT.shape, F32)

    def attend(chunk, carry):
        rows = pl.ds(pl.multiple_of(chunk * KC, KC), KC)
        keys = m.KV[rows, 0:DP]
        values_t = m.KV[rows, KVW - DP : KVW].T
        live = alive(chunk)
        for h in range(HW):
            scores = jnp.where(live, dot_nt(keys, m.Qm[h]), FLOOR)
            top = m.mrow[h : h + 1, :]
            new_top = jnp.maximum(top, jnp.max(scores, 0, keepdims=True))
            prob = jnp.exp(scores - new_top)
            factor = jnp.exp(top - new_top)
            m.mrow[h : h + 1, :] = new_top
            m.lrow[h : h + 1, :] = m.lrow[h : h + 1, :] * factor + col_sum(prob)
            a, b = OFF + h * HEAD, OFF + (h + 1) * HEAD
            m.OT[a:b, :] = m.OT[a:b, :] * factor + dot(values_t[a:b, :], prob.astype(BF))
        return carry

    lax.fori_loop(0, R * PER_SET, attend, 0)
    for h in range(HW):
        a, b = OFF + h * HEAD, OFF + (h + 1) * HEAD
        m.OT[a:b, :] = m.OT[a:b, :] / m.lrow[h : h + 1, :]
    m.lrow[0:HW, :] = m.mrow[0:HW, :] + jnp.log(m.lrow[0:HW, :])
    for j in range(W):
        m.Osend[j] = m.OT[:, j * B : (j + 1) * B].T.astype(BF)
        dev = (j * R + r_att, s)
        send(m.Osend.at[j], m.Mix.at[g_att], m.s_o.at[j], m.r_o.at[g_att], dev, jnp.logical_not(is_me(dev)))

        @pl.when(is_me(dev))
        def _():
            m.Mix[g_att] = m.Osend[j]

    for k in (1, 2, 3):
        arrive(m.Outp.at[jnp.bitwise_xor(w, k), pl.ds(OFF, DW)], m.r_ow.at[k])
    resid = m.Xall[w].astype(F32) + vec(OUTB)
    for g in range(W):
        arrive(m.Mix.at[g], m.r_o.at[g], jnp.logical_not(is_me(att_device(w, g, block_part))))
        resid = resid + dot(m.Mix[g], m.Outp[g])
    n1, r1 = norm_stats(resid)
    m.n1[...] = n1
    m.r1[...] = r1
    n1_full = n1 * vec(GAIN1) + vec(SHIFT1)
    m.N1f[...] = n1_full
    m.N1all[w] = n1_full.astype(BF)
    gather_start(m.N1all, m.s_n, m.r_n)

    for k in (1, 2, 3):
        arrive(m.Upc.at[pl.ds(jnp.bitwise_xor(w, k) * DW, DW)], m.r_uw.at[k])
    up_bias = upb_ref[...]

    def expand(t):
        h = dot(m.N1all[t], m.Upc[...]) + up_bias
        phi = 0.5 * (1.0 + lax.erf(h * (2.0**-0.5)))
        m.Gs[t] = (h * phi).astype(BF)
        m.Hp[t] = phi + h * ((2.0 * math.pi) ** -0.5) * jnp.exp(-0.5 * h * h)

    expand(w)
    for k in (1, 2, 3):
        gather_wait(m.N1all, m.s_n, m.r_n, k)
        expand(jnp.bitwise_xor(w, k))

    ffn = scatter_sum(lambda t: dot(m.Gs[t], m.Dn[...]), m.Fs, m.Fr, m.s_f, m.r_f)
    n2, r2 = norm_stats(m.N1f[...] + ffn + vec(DOWNB))
    m.n2[...] = n2
    y_ref[...] = (n2 * vec(GAIN2) + vec(SHIFT2)).astype(BF)

    place = c * B + lax.broadcasted_iota(jnp.int32, (B, D), 0)
    dy = jnp.where(place.astype(F32) < m.Vs[pl.ds(LEN + w, 1), :], m.Cot[...].astype(F32), 0.0)
    d_r2 = norm_back(dy, n2, r2, vec(GAIN2))
    m.dR2[...] = d_r2
    m.dFall[w] = d_r2.astype(BF)
    gather_start(m.dFall, m.s_df, m.r_df)
    m.gv[2:3, :] = col_sum(dy * n2)
    m.gv[3:4, :] = col_sum(dy)
    m.gv[5:6, :] = col_sum(m.dFall[w].astype(F32))

    def shrink(t):
        m.dHs[t] = (dot_nt(m.dFall[t], m.Dn[...]) * m.Hp[t]).astype(BF)

    shrink(w)
    for k in (1, 2, 3):
        gather_wait(m.dFall, m.s_df, m.r_df, k)
        shrink(jnp.bitwise_xor(w, k))
    d_n1 = scatter_sum(lambda t: dot_nt(m.dHs[t], m.Upc[...]), m.dNs, m.dNr, m.s_dn, m.r_dn) + m.dR2[...]
    n1 = m.n1[...]
    d_r1 = norm_back(d_n1, n1, m.r1[...], vec(GAIN1))
    m.dR1[...] = d_r1
    d_a = d_r1.astype(BF)
    m.dAall[w] = d_a
    for g in range(W):
        m.dOs[g] = dot_nt(d_a, m.Outp[g]).astype(BF)
        dev = att_device(w, g, block_part)
        send(m.dOs.at[g], m.dOr.at[block_slot], m.s_do.at[g], m.r_do.at[block_slot], dev,
             jnp.logical_not(is_me(dev)))

        @pl.when(is_me(dev))
        def _():
            m.dOr[block_slot] = m.dOs[g]

    gather_start(m.dAall, m.s_da, m.r_da)
    for k in (2, 3, 1):
        send(m.Mix.at[jnp.bitwise_xor(w, k)], m.MixT.at[w], m.s_mt.at[k], m.r_mt.at[k], peer(k))
    m.MixT[w] = m.Mix[w]
    m.gv[0:1, :] = col_sum(d_n1 * n1)
    m.gv[1:2, :] = col_sum(d_n1)
    m.gv[4:5, :] = col_sum(d_a.astype(F32))

    def flat(ref):
        return ref[...].reshape(Q, ref.shape[-1])

    def put_grad(name, dest, index, lhs, rhs, parts):
        rows = lhs.shape[-1] // parts
        for i in range(parts):
            val = dot_tn(lhs[:, :, i * rows : (i + 1) * rows].reshape(Q, rows), flat(rhs)).astype(BF)
            if cfg.fused:
                ch = cfg.grads[name][0]
                n = rows // (2 * ch)
                dest[i * n : (i + 1) * n] = val.reshape(n, 2, ch, val.shape[-1])
            else:
                dest[i * rows : (i + 1) * rows, :] = val

    put_grad("down", m.Gdown if cfg.fused else gdown_ref, 0, m.Gs, m.dFall, 2)
    put_grad("up", m.Gup if cfg.fused else gup_ref, 1, m.N1all, m.dHs, 2)
    m.gv[6:7, :] = col_sum(flat(m.dHs).astype(F32))

    for j in range(W):
        arrive(m.dOr.at[j], m.r_do.at[j], jnp.logical_not(is_me((j * R + r_att, s))))
        d_o = m.dOr[j]
        cols = slice(j * B, (j + 1) * B)
        for h in range(HW):
            m.Dm[h, cols, :] = jnp.where(v_lane(h), d_o, jnp.zeros_like(d_o))
        prod = m.OT[:, cols] * d_o.astype(F32).T
        for h in range(HW):
            m.drow[h : h + 1, cols] = col_sum(prod[OFF + h * HEAD : OFF + (h + 1) * HEAD, :])
    m.dQT[...] = jnp.zeros(m.dQT.shape, F32)

    def attend_back(step, carry):
        chunk = lax.rem((r_att + 1) * PER_SET + step, R * PER_SET)
        rows = pl.ds(pl.multiple_of(chunk * KC, KC), KC)
        keys = m.KV[rows, 0:DP]
        values = m.KV[rows, KVW - DP : KVW]
        keys_t = keys.T
        live = alive(chunk)
        d_k = jnp.zeros((KC, DP), F32)
        d_v = jnp.zeros((KC, DP), F32)
        for h in range(HW):
            scores = dot_nt(keys, m.Qm[h])
            prob = jnp.where(live, jnp.exp(scores - m.lrow[h : h + 1, :]), 0.0)
            d_prob = dot_nt(values, m.Dm[h])
            d_s = (prob * (d_prob - m.drow[h : h + 1, :])).astype(BF)
            d_k = d_k + dot(d_s, m.Qm[h])
            d_v = d_v + dot(prob.astype(BF), m.Dm[h])
            a, b = h * HEAD, (h + 1) * HEAD
            m.dQT[a:b, :] = m.dQT[a:b, :] + dot(keys_t[a:b, :], d_s)
        lead = KVW - DP
        m.dKVf[rows, 0:lead] = d_k[:, 0:lead]
        m.dKVf[rows, lead:DP] = d_k[:, lead:] + d_v[:, 0 : DP - lead]
        m.dKVf[rows, DP:KVW] = d_v[:, DP - lead :]
        return carry

    lax.fori_loop(0, (R - 1) * PER_SET, attend_back, 0)
    for k in range(1, R):
        r = lax.rem(r_att + k, R)
        m.dKVs[r] = m.dKVf[pl.ds(pl.multiple_of(r * Q, Q), Q), :].astype(BF)
        send(m.dKVs.at[r], m.dKVr.at[r_att], m.s_dkv.at[k - 1], m.r_dkv.at[r_att], att_device(s, g_att, r))
    lax.fori_loop((R - 1) * PER_SET, R * PER_SET, attend_back, 0)
    for k in range(1, R):
        arrive(m.dKVr.at[lax.rem(r_att + k, R)], m.r_dkv.at[lax.rem(r_att + k, R)])
    for j in range(W):
        d_kv = m.dKVf[pl.ds(pl.multiple_of(r_att * Q + j * B, B), B), :]
        for k in range(1, R):
            d_kv = d_kv + m.dKVr[lax.rem(r_att + k, R), j * B : (j + 1) * B, :].astype(F32)
        m.dqs[j, :, 0:KVW] = d_kv.astype(BF)
        d_q = m.dQT[:, j * B : (j + 1) * B].T * (HEAD**-0.5)
        m.dqs[j, :, KVW:MW] = jnp.where(lanes < DW, d_q, 0.0).astype(BF)
        dev = (j * R + r_att, g_att)
        send(m.dqs.at[j], m.dqr.at[s], m.s_dq.at[j], m.r_dq.at[s], dev, jnp.logical_not(is_me(dev)))

        @pl.when(is_me(dev))
        def _():
            m.dqr[s] = m.dqs[j]

    for k in (1, 2, 3):
        gather_wait(m.dAall, m.s_da, m.r_da, k)
        arrive(m.MixT.at[jnp.bitwise_xor(w, k)], m.r_mt.at[k])
    put_grad("out", m.Gout if cfg.fused else gout_ref, 2, m.MixT, m.dAall, 1)

    for t in range(W):
        arrive(m.dqr.at[t], m.r_dq.at[t], jnp.logical_not(is_me(att_device(t, w, block_part))))
    d_x = scatter_sum(lambda t: dot_nt(m.dqr[t], m.Wc[...]), m.dxs, m.dxr, m.s_dx, m.r_dx)
    gx_ref[...] = (m.dR1[...] + d_x).astype(BF)
    put_grad("qkv", m.Gqkv if cfg.fused else gqkv_ref, 3, m.Xall, m.dqr, 2)
    m.gv[7:8, 0:MW] = col_sum(flat(m.dqr).astype(F32))
    m.gv[7:8, MW:D] = jnp.zeros((1, D - MW), F32)

    if not cfg.fused:
        gvec_ref[0] = m.gv[...]
    else:
        NZ = C // 2
        z, x = lax.div(c, 2), lax.rem(c, 2)
        beside = (c + 1 - 2 * x, w)
        G = SimpleNamespace(**{k: getattr(m, k) for k in vars(m)})

        def buf(kind, name):
            return getattr(G, kind + name)

        def zpeer(k):
            return lax.rem(z + k, NZ)

        def halves_start(name):
            for k in list(range(1, NZ)) + [0]:
                zi = zpeer(k)
                send(buf("G", name).at[zi, 1 - x], buf("X", name).at[zi], buf("s_gx", name).at[k],
                     buf("r_gx", name).at[k], beside)

        def planes_start(name):
            for k in range(1, NZ):
                zi = zpeer(k)
                arrive(buf("X", name).at[zi], buf("r_gx", name).at[k])
                buf("S", name)[zi] = (buf("G", name)[zi, x].astype(F32) + buf("X", name)[zi].astype(F32)).astype(BF)
                send(buf("S", name).at[zi], buf("Z", name).at[z], buf("s_gz", name).at[k], buf("r_gz", name).at[k],
                     (zi * 2 + x, w))

        def reduce_end(name):
            to_rows = cfg.grads[name][2]
            arrive(buf("X", name).at[z], buf("r_gx", name).at[0])
            acc = buf("G", name)[z, x].astype(F32) + buf("X", name)[z].astype(F32)
            for k in range(1, NZ):
                zi = lax.rem(z + NZ - k, NZ)
                arrive(buf("Z", name).at[zi], buf("r_gz", name).at[k])
                acc = acc + buf("Z", name)[zi].astype(F32)
            if to_rows:
                buf("R", name)[...] = acc.astype(BF)
                home = block_slot

                @pl.when(home == w)
                def _():
                    buf("F", name)[x, w] = buf("R", name)[...]

                send(buf("R", name), buf("F", name).at[x, w], buf("s_gw", name).at[0], buf("r_gw", name).at[w],
                     (c, home), home != w)
            else:
                buf("F", name)[z, x] = acc.astype(BF)
                fin = buf("F", name)
                for k in range(1, NZ):
                    send(fin.at[z, x], fin.at[z, x], buf("s_ga", name).at[k], buf("r_ga", name).at[k],
                         (zpeer(k) * 2 + x, w))
                send(fin.at[z, x], fin.at[z, x], buf("s_gf", name).at[0], buf("r_gf", name).at[0], beside)

        def spread(name):
            fin = buf("F", name)
            if cfg.grads[name][2]:
                at_home = block_slot == w
                for k in range(1, W):
                    t = jnp.bitwise_xor(w, k)
                    arrive(fin.at[x, t], buf("r_gw", name).at[t], at_home)
                for k in range(1, NZ):
                    send(fin.at[x], fin.at[x], buf("s_ga", name).at[k], buf("r_ga", name).at[0],
                         (zpeer(k) * 2 + x, w), at_home)
                arrive(fin.at[x], buf("r_ga", name).at[0], jnp.logical_not(at_home))
                send(fin.at[x], fin.at[x], buf("s_gf", name).at[0], buf("r_gf", name).at[0], beside)
            else:
                for k in range(1, NZ):
                    zi = lax.rem(z + NZ - k, NZ)
                    arrive(fin.at[zi, x], buf("r_ga", name).at[k])
                    send(fin.at[zi, x], fin.at[zi, x], buf("s_gf", name).at[k], buf("r_gf", name).at[k], beside)

        def finish(name, dest):
            fin = buf("F", name)
            ch, cols, to_rows = cfg.grads[name]
            if to_rows:
                arrive(fin.at[1 - x], buf("r_gf", name).at[0])
                for i in range(2):
                    for t in range(W):
                        dest[i * ch : (i + 1) * ch, t * cols : (t + 1) * cols] = fin[i, t]
            else:
                for k in range(NZ):
                    zi = lax.rem(z + NZ - k, NZ)
                    arrive(fin.at[zi, 1 - x], buf("r_gf", name).at[k])
                dest[...] = fin[...].reshape(dest.shape)

        order = ("up", "down", "qkv", "out")
        send(m.gv, m.Vx, m.s_vx.at[0], m.r_vx.at[0], beside)
        for name in order:
            halves_start(name)
        arrive(m.Vx, m.r_vx.at[0])
        m.Vy[...] = m.gv[...] + m.Vx[...]
        for k in range(1, NZ):
            send(m.Vy, m.Vz.at[z], m.s_vz.at[k], m.r_vz.at[k], (zpeer(k) * 2 + x, w))
        for name in order:
            planes_start(name)
        total = m.Vy[...]
        for k in range(1, NZ):
            zi = lax.rem(z + NZ - k, NZ)
            arrive(m.Vz.at[zi], m.r_vz.at[k])
            total = total + m.Vz[zi]
        m.Vw[w] = total
        for k in (1, 2, 3):
            send(m.Vw.at[w], m.Vw.at[w], m.s_vw.at[k], m.r_vw.at[k], peer(k))
        for name in order:
            reduce_end(name)
        for name in order:
            spread(name)
        for k in (1, 2, 3):
            arrive(m.Vw.at[jnp.bitwise_xor(w, k)], m.r_vw.at[k])
        gvec_ref[...] = m.Vw[...]
        for name, dest in zip(order, (gup_ref, gdown_ref, gqkv_ref, gout_ref)):
            finish(name, dest)

    for pred, end in drains:
        if pred is None:
            end()
        else:
            pl.when(pred)(end)


def body(C, W, tokens, lengths, qkv_weight, out_weight, up_weight, down_weight, qv_bias, out_bias, up_bias,
         down_bias, gain_one, shift_one, gain_two, shift_two, cotangent):
    _, B, D = tokens.shape
    FW = down_weight.shape[0]
    DW = D // W
    DP = -(-DW // 128) * 128
    KVW = 2 * DW
    MW = KVW + DP
    R = C // W
    cfg = SimpleNamespace(C=C, W=W, B=B, D=D, FW=FW, DW=DW, DP=DP, KVW=KVW, MW=MW, R=R, HW=HEADS // W)
    cfg.fused = R == 2 and D % (16 * C) == 0
    cfg.grads = dict(up=(D // C, FW, True), down=(FW // C, D, False), qkv=(D // C, MW, True), out=(DP // C, D, False))
    w = lax.axis_index("wa")

    thirds = qkv_weight.reshape(DW, 3, W, DW)
    pad = jnp.zeros((W, DW, DP - DW), BF)
    wq = jnp.concatenate([thirds[:, i].transpose(1, 0, 2) for i in (1, 2, 0)] + [pad], 2)
    qv = lax.dynamic_update_slice(jnp.zeros((2 * D,), BF), qv_bias, (w * (2 * D // W),)).reshape(2, W, 1, DW)
    bias = jnp.concatenate([jnp.zeros((W, 1, DW), BF), qv[1], qv[0], jnp.zeros((W, 1, DP - DW), BF)], 2)
    bias = jnp.pad(bias, ((0, 0), (0, 15), (0, 0)))
    small = jnp.stack([out_bias, down_bias, gain_one, shift_one, gain_two, shift_two]).astype(F32)
    vec = lax.dynamic_update_slice(jnp.zeros((VROWS, D), F32), small, (0, w * DW))
    vec = lax.dynamic_update_slice(vec, jnp.broadcast_to(lengths.astype(F32)[:, None], (1, D)), (LEN + w, 0))

    plan = make_plan(cfg)
    names = list(plan)
    vm = pl.BlockSpec(memory_space=pltpu.VMEM)
    hbm = pl.BlockSpec(memory_space=pl.ANY)
    shape = jax.ShapeDtypeStruct
    if cfg.fused:
        outs = [shape((DW, W * MW), BF), shape((DP, D), BF), shape((DW, W * FW), BF), shape((FW, D), BF),
                shape((W, GROWS, D), F32)]
    else:
        outs = [shape((D, MW), BF), shape((DP, D), BF), shape((D, FW), BF), shape((FW, D), BF),
                shape((1, GROWS, D), F32)]
    outs = [shape((B, D), BF), shape((B, D), BF)] + outs
    args = (tokens.reshape(B, D), cotangent.reshape(B, D), wq, bias, vec, up_bias.astype(F32).reshape(1, FW),
            out_weight, up_weight, down_weight)
    y, gx, gqkv, gout, gup, gdown, gvec = pl.pallas_call(
        functools.partial(layer_kernel, cfg, names, len(args)),
        out_shape=outs,
        in_specs=[hbm, hbm, hbm, hbm, hbm, vm, hbm, hbm, hbm],
        out_specs=[vm] * len(outs),
        scratch_shapes=[plan[n] for n in names],
        compiler_params=pltpu.CompilerParams(collective_id=0, has_side_effects=True, vmem_limit_bytes=60 << 20),
        name="layer",
    )(*args)
    if not cfg.fused:
        def to_rows(g):
            g = lax.psum(g, "ctx").reshape(W, DW, g.shape[1])
            return lax.all_to_all(g, "wa", 0, 0, tiled=True).transpose(1, 0, 2).reshape(DW, -1)

        gqkv, gup = to_rows(gqkv), to_rows(gup)
        gout, gdown, gvec = lax.psum((gout, gdown, gvec), "ctx")
        gvec = lax.all_gather(gvec, "wa", axis=0, tiled=True)
    gq = gqkv.reshape(DW, W, MW).astype(F32)
    gqkv = jnp.concatenate(
        [gq[:, :, a : a + DW].reshape(DW, D) for a in (KVW, 0, DW)], 1)
    own = lax.dynamic_slice_in_dim(jnp.sum(gvec, 0)[0:6], w * DW, DW, 1)
    g_upb = lax.dynamic_slice_in_dim(gvec, w, 1, 0)[0, 6]
    g_qv = jnp.concatenate([gvec[:, 7, KVW : KVW + DW].reshape(D), gvec[:, 7, DW:KVW].reshape(D)])
    g_qv = lax.dynamic_slice_in_dim(g_qv, w * (2 * D // W), 2 * D // W)
    return (
        y.reshape(1, B, D),
        gx.reshape(1, B, D),
        gqkv,
        gout[DP - DW :].astype(F32),
        gup.astype(F32),
        gdown.astype(F32),
        g_qv,
        own[4],
        g_upb,
        own[5],
        own[0],
        own[1],
        own[2],
        own[3],
    )


def solution(mesh):
    tok, vec, mat = P("wa", "ctx", None), P("wa"), P("wa", None)
    return jax.shard_map(
        functools.partial(body, mesh.shape["ctx"], mesh.shape["wa"]),
        mesh=mesh,
        in_specs=(tok, vec, mat, mat, mat, mat) + (vec,) * 8 + (tok,),
        out_specs=(tok, tok, mat, mat, mat, mat) + (vec,) * 8,
        check_vma=False,
    )
```

```python
import functools
import math
from types import SimpleNamespace

import jax
import jax.numpy as jnp
from jax import lax
from jax.experimental import pallas as pl
from jax.experimental.pallas import tpu as pltpu
from jax.sharding import PartitionSpec as P

HEADS = 12
HEAD = 64
EPS = 1e-12
FLOOR = -1e30
MESH = pl.DeviceIdType.MESH
BF = jnp.bfloat16
F32 = jnp.float32

OUTB, DOWNB, GAIN1, SHIFT1, GAIN2, SHIFT2, QVB = range(7)
UPB, LEN = 8, 12
VROWS = 16
GROWS = 8


def dot(a, b):
    return lax.dot_general(a, b, (((1,), (0,)), ((), ())), preferred_element_type=F32)


def dot_nt(a, b):
    return lax.dot_general(a, b, (((1,), (1,)), ((), ())), preferred_element_type=F32)


def dot_tn(a, b):
    return lax.dot_general(a, b, (((0,), (0,)), ((), ())), preferred_element_type=F32)


def norm_stats(v):
    center = v - jnp.mean(v, -1, keepdims=True)
    rstd = lax.rsqrt(jnp.mean(center * center, -1, keepdims=True) + EPS)
    return center * rstd, rstd


def norm_back(dy, normed, rstd, gain):
    dn = dy * gain
    return rstd * (
        dn - jnp.mean(dn, -1, keepdims=True) - normed * jnp.mean(dn * normed, -1, keepdims=True)
    )


def col_sum(v):
    return jnp.sum(v, 0, keepdims=True)


def make_plan(cfg):
    C, W, B, D, FW, DW, DP, KVW, MW, R = (
        cfg.C, cfg.W, cfg.B, cfg.D, cfg.FW, cfg.DW, cfg.DP, cfg.KVW, cfg.MW, cfg.R)
    V = pltpu.VMEM
    dma = pltpu.SemaphoreType.DMA
    Q = W * B
    plan = dict(
        Xall=V((W, B, D), BF), Wc=V((D, MW), BF), Wq=V((DW, 3 * D), BF), Ws=V((W, DW, MW), BF), Vv=V((W, VROWS, DW), F32),
        Vs=V((8, D), F32), Outp=V((W, DP, D), BF), Upc=V((D, FW), BF), Dn=V((FW, D), BF), Cot=V((B, D), BF),
        QKVs=V((W, B, MW), BF), Rq=V((W, B, MW), BF), KV=V((R * Q, KVW), BF),
        Qm=V((cfg.HW, Q, DP), BF), Dm=V((cfg.HW, Q, DP), BF),
        mrow=V((8, Q), F32), lrow=V((8, Q), F32), bias=V((8, MW), F32), upb=V((8, cfg.FW), F32), drow=V((8, Q), F32), OT=V((DP, Q), F32), dQT=V((DP, Q), F32),
        Osend=V((W, B, DP), BF), Mix=V((W, B, DP), BF), MixT=V((W, B, DP), BF),
        N1f=V((B, D), F32), n1=V((B, D), F32), n2=V((B, D), F32), r1=V((B, 1), F32),
        N1all=V((W, B, D), BF), Hp=V((W, B, FW), F32), Gs=V((W, B, FW), BF),
        Fs=V((W, B, D), BF), Fr=V((3, B, D), BF), dR2=V((B, D), F32), dFall=V((W, B, D), BF),
        dHs=V((W, B, FW), BF), dNs=V((W, B, D), BF), dNr=V((3, B, D), BF), dR1=V((B, D), F32),
        dAall=V((W, B, D), BF), dOs=V((W, B, DP), BF), dOr=V((W, B, DP), BF),
        dKVf=V((Q, KVW), F32), dKVs=V((R - 1, Q, KVW), BF), dKVr=V((R - 1, Q, KVW), BF),
        dqs=V((W, B, MW), BF), dqr=V((W, B, MW), BF), dxs=V((W, B, D), BF), dxr=V((3, B, D), BF),
        gv=V((GROWS, D), F32),
    )
    sems = dict(
        x=4, wq=4, vv=4, ow=4, uw=4, own=7,
        q=W, kv=(R - 1) * W, o=W, mt=4, n=4, f=4, df=4, dn=4, da=4, do=W, dkv=R - 1, dq=W, dx=4,
    )
    recvs = dict(sems, kv=R * W)
    if cfg.fused:
        for name, (pieces, ch, cols, to_rows) in cfg.grads.items():
            plan["G" + name] = V((pieces, 2, 2, ch, cols), BF)
            plan["X" + name] = V((pieces, 2, ch, cols), BF)
            plan["T" + name] = V((pieces, ch, cols), BF)
            plan["Y" + name] = V((pieces, ch, cols), BF)
            plan["U" + name] = V((pieces, ch, cols), BF)
            plan["Z" + name] = V((pieces, ch, cols), BF)
            for kind in ("g1", "g2", "g3", "g4", "g5", "g6"):
                sems[kind + name] = pieces
                recvs[kind + name] = pieces
            if to_rows:
                plan["R" + name] = V((pieces, ch, cols), BF)
        plan.update(Va=V((3, GROWS, D), F32), Vb=V((3, GROWS, D), F32), Vt=V((W, GROWS, DW), F32),
                    Vw=V((W, GROWS, DW), F32))
        sems.update(v1=3, vw=W)
        recvs.update(v1=3, vw=W)
    for name, n in sems.items():
        plan["s_" + name] = dma((n,))
    for name, n in recvs.items():
        plan["r_" + name] = dma((n,))
    return plan


class make_sums:
    def __init__(self, cfg, m, c, w, send, arrive):
        self.cfg, self.m, self.w, self.send, self.arrive = cfg, m, w, send, arrive
        self.c = c
        self.x, self.near = lax.rem(c, 2), lax.rem(lax.div(c, 2), 2)
        self.partners = [(jnp.bitwise_xor(c, k), w) for k in (1, 2, 4)]
        self.waves = []

    def start(self, names):
        if self.cfg.fused:
            for name in names:
                for p in range(self.cfg.grads[name][0]):
                    self.one(name, p)

    def add(self, names, lag):
        if not self.cfg.fused:
            return
        items = [(n, p) for n in names for p in range(self.cfg.grads[n][0])]
        stages = [self.two, self.three, self.four, self.five, self.six, self.seven]
        waves = []
        for wave in range(len(items) + lag * (len(stages) - 1)):
            steps = [functools.partial(stages[k], *items[wave - lag * k])
                     for k in reversed(range(len(stages))) if 0 <= wave - lag * k < len(items)]
            waves.append(steps)
        old, merged = self.waves, []
        for i in range(max(len(old), len(waves))):
            merged.append((old[i] if i < len(old) else []) + (waves[i] if i < len(waves) else []))
        self.waves = merged

    def run(self, n):
        for wave in self.waves[:n]:
            for step in wave:
                step()
        del self.waves[:n]

    def ref(self, kind, name):
        return getattr(self.m, kind + name)

    def go(self, kind, name, p, src, dst, dev, pred=None):
        self.send(src, dst, self.ref("s_" + kind, name).at[p], self.ref("r_" + kind, name).at[p], dev, pred)

    def got(self, kind, name, p, dst, pred=None):
        self.arrive(dst, self.ref("r_" + kind, name).at[p], pred)

    def piece(self, name, k):
        return jnp.bitwise_xor(self.w, k) if self.cfg.grads[name][3] else k

    def one(self, name, k):
        p = self.piece(name, k)
        self.go("g1", name, k, self.ref("G", name).at[p, 1 - self.x], self.ref("X", name).at[k], self.partners[0])

    def two(self, name, k):
        g, other, t = self.ref("G", name), self.ref("X", name), self.ref("T", name)
        self.got("g1", name, k, other.at[k])
        far = 1 - self.near
        mine = g[self.piece(name, k), self.x, far].astype(F32)
        t[k] = (mine + other[k, far].astype(F32)).astype(BF)
        self.go("g2", name, k, t.at[k], self.ref("Y", name).at[k], self.partners[1])

    def three(self, name, k):
        g, other, y, u = (self.ref(kind, name) for kind in "GXYU")
        self.got("g2", name, k, y.at[k])
        n = self.near
        mine = g[self.piece(name, k), self.x, n].astype(F32)
        u[k] = (mine + other[k, n].astype(F32) + y[k].astype(F32)).astype(BF)
        self.go("g3", name, k, u.at[k], self.ref("Z", name).at[k], self.partners[2])

    def four(self, name, k):
        u, z, fin = (self.ref(kind, name) for kind in "UZF")
        self.got("g3", name, k, z.at[k])
        total = (u[k].astype(F32) + z[k].astype(F32)).astype(BF)
        if not self.cfg.grads[name][3] or k == 0:
            fin[self.piece(name, k), self.x, self.near] = total
            return
        done = self.ref("R", name)
        done[k] = total
        self.go("g4", name, k, done.at[k], fin.at[self.w, self.x, self.near], (self.c, jnp.bitwise_xor(self.w, k)))

    def five(self, name, k):
        here = self.ref("F", name).at[self.piece(name, k), self.x, self.near]
        if self.cfg.grads[name][3] and k > 0:
            self.got("g4", name, k, here)
        self.go("g5", name, k, here, here, self.partners[1])

    def six(self, name, k):
        fin, p = self.ref("F", name), self.piece(name, k)
        self.got("g5", name, k, fin.at[p, self.x, 1 - self.near])
        self.go("g6", name, k, fin.at[p, self.x], fin.at[p, self.x], self.partners[0])

    def seven(self, name, k):
        self.got("g6", name, k, self.ref("F", name).at[self.piece(name, k), 1 - self.x])


def layer_kernel(cfg, names, n_in, *refs):
    (x_ref, cot_ref, qkv_ref, vec_ref, out_ref, up_ref, down_ref) = refs[:n_in]
    y_ref, gx_ref, gqkv_ref, gout_ref, gup_ref, gdown_ref, gvec_ref = refs[n_in : n_in + 7]
    m = SimpleNamespace(**dict(zip(names, refs[n_in + 7 :])))
    if cfg.fused:
        m.Fqkv, m.Fout, m.Fup, m.Fdown = gqkv_ref, gout_ref, gup_ref, gdown_ref
    C, W, B, D, DW, DP, KVW, MW, R, HW = (
        cfg.C, cfg.W, cfg.B, cfg.D, cfg.DW, cfg.DP, cfg.KVW, cfg.MW, cfg.R, cfg.HW)
    OFF = DP - DW
    Q = W * B
    c = lax.axis_index("ctx")
    w = lax.axis_index("wa")
    block_part = lax.rem(c, R)
    block_slot = lax.div(c, R)
    s = lax.div(c, R)
    low = lax.rem(c, R)
    g_att = lax.div(w, 2) * 2 + lax.rem(low, 2)
    r_att = lax.div(low, 2) * 2 + lax.rem(w, 2)

    def att_device(t, g, r):
        return (t * R + lax.div(r, 2) * 2 + lax.rem(g, 2), lax.div(g, 2) * 2 + lax.rem(r, 2))

    def is_me(dev):
        return jnp.logical_and(dev[0] == c, dev[1] == w)

    drains = []

    def remote(src, dst, ss, rs, dev):
        return pltpu.make_async_remote_copy(
            src_ref=src, dst_ref=dst, send_sem=ss, recv_sem=rs, device_id=dev, device_id_type=MESH)

    def send(src, dst, ss, rs, dev, pred=None):
        def go():
            remote(src, dst, ss, rs, dev).start()

        def end():
            remote(src, dst, ss, rs, dev).wait_send()

        if pred is None:
            go()
        else:
            pl.when(pred)(go)
        drains.append((pred, end))

    def arrive(dst, rs, pred=None):
        def go():
            remote(dst, dst, rs, rs, (c, w)).wait_recv()

        if pred is None:
            go()
        else:
            pl.when(pred)(go)

    barrier = pltpu.get_barrier_semaphore()

    def greet(i, carry):
        ci, wi = lax.div(i, W), lax.rem(i, W)

        @pl.when(jnp.logical_not(is_me((ci, wi))))
        def _():
            pl.semaphore_signal(barrier, inc=1, device_id=(ci, wi), device_id_type=MESH)

        return carry

    lax.fori_loop(0, C * W, greet, 0)

    def return_barrier():
        pl.semaphore_wait(barrier, C * W - 1)

    def peer(k):
        return (c, jnp.bitwise_xor(w, k))

    def gather_start(buf, ss, rs):
        send(buf.at[w], buf.at[w], ss.at[2], rs.at[2], peer(2))
        send(buf.at[w], buf.at[w], ss.at[1], rs.at[1], peer(1))

    def gather_wait(buf, ss, rs, k):
        if k == 1:
            arrive(buf.at[jnp.bitwise_xor(w, 1)], rs.at[1])
        if k == 2:
            t = jnp.bitwise_xor(w, 2)
            arrive(buf.at[t], rs.at[2])
            send(buf.at[t], buf.at[t], ss.at[3], rs.at[3], peer(1))
        if k == 3:
            arrive(buf.at[jnp.bitwise_xor(w, 3)], rs.at[3])

    def scatter_sum(part, stage, recv, ss, rs, early=None, late=None):
        t3, t2, t1 = (jnp.bitwise_xor(w, k) for k in (3, 2, 1))
        stage[t3] = part(t3).astype(BF)
        send(stage.at[t3], recv.at[1], ss.at[1], rs.at[1], peer(1))
        mine2 = part(t2)
        stage[t1] = part(t1).astype(BF)
        send(stage.at[t1], recv.at[0], ss.at[0], rs.at[0], peer(1))
        if early:
            early()
        arrive(recv.at[1], rs.at[1])
        stage[t2] = (mine2 + recv[1].astype(F32)).astype(BF)
        send(stage.at[t2], recv.at[2], ss.at[2], rs.at[2], peer(2))
        own = part(w)
        if late:
            late()
        arrive(recv.at[0], rs.at[0])
        own = own + recv[0].astype(F32)
        arrive(recv.at[2], rs.at[2])
        return own + recv[2].astype(F32)

    def local(src, dst, sem):
        cp = pltpu.make_async_copy(src, dst, sem)
        cp.start()
        return cp

    rows_w = pl.ds(w * DW, DW)
    own = [
        local(qkv_ref, m.Wq, m.s_own.at[1]),
        local(x_ref, m.Xall.at[w], m.s_own.at[0]),
        local(vec_ref, m.Vv.at[w], m.s_own.at[2]),
        local(out_ref, m.Outp.at[w, pl.ds(OFF, DW)], m.s_own.at[3]),
        local(up_ref.at[:, pl.ds(pl.multiple_of(w * cfg.FW, cfg.FW), cfg.FW)], m.Upc.at[rows_w], m.s_own.at[4]),
        local(down_ref, m.Dn, m.s_own.at[5]),
        local(cot_ref, m.Cot, m.s_own.at[6]),
    ]
    own[0].wait()
    for g in range(W):
        for i, third in enumerate((1, 2, 0)):
            a = third * D + g * DW
            m.Ws[g, :, i * DW : (i + 1) * DW] = m.Wq[:, a : a + DW]
        m.Ws[g, :, 3 * DW : MW] = jnp.zeros((DW, MW - 3 * DW), BF)
    own[1].wait()
    own[2].wait()
    return_barrier()
    for k in (2, 3, 1):
        t = jnp.bitwise_xor(w, k)
        send(m.Ws.at[t], m.Wc.at[rows_w], m.s_wq.at[k], m.r_wq.at[k], peer(k))
        send(m.Vv.at[w], m.Vv.at[w], m.s_vv.at[k], m.r_vv.at[k], peer(k))
    gather_start(m.Xall, m.s_x, m.r_x)
    m.Wc[rows_w, :] = m.Ws[w]
    for t in range(W):
        m.Outp[t, 0:OFF, :] = jnp.zeros((OFF, D), BF)
    m.bias[...] = jnp.zeros(m.bias.shape, F32)
    for cp in own[3:]:
        cp.wait()
    for k in (1, 2, 3):
        t = jnp.bitwise_xor(w, k)
        arrive(m.Wc.at[pl.ds(t * DW, DW)], m.r_wq.at[k])
        arrive(m.Vv.at[t], m.r_vv.at[k])
        gather_wait(m.Xall, m.s_x, m.r_x, k)
    for k in (2, 3, 1):
        t = jnp.bitwise_xor(w, k)
        send(out_ref, m.Outp.at[w, pl.ds(OFF, DW)], m.s_ow.at[k], m.r_ow.at[k], peer(k))
    for k in (2, 3, 1):
        t = jnp.bitwise_xor(w, k)
        send(up_ref.at[:, pl.ds(pl.multiple_of(t * cfg.FW, cfg.FW), cfg.FW)], m.Upc.at[rows_w],
             m.s_uw.at[k], m.r_uw.at[k], peer(k))

    for t in range(W):
        m.Vs[0:6, t * DW : (t + 1) * DW] = m.Vv[t, 0:6, :]
        m.upb[0:1, t * DW : (t + 1) * DW] = m.Vv[w, UPB + t : UPB + t + 1, :]
    half, odd = lax.div(w, 2), lax.rem(w, 2)
    m.bias[0:1, DW : 2 * DW] = m.Vv[W // 2 + half, pl.ds(QVB + odd, 1), :]
    m.bias[0:1, 2 * DW : 3 * DW] = m.Vv[half, pl.ds(QVB + odd, 1), :]
    bias = m.bias[0:1, :]

    def vec(row):
        return m.Vs[row : row + 1, :]

    for k in range(W):
        t = lax.rem(s + 1 + k, W)
        m.QKVs[t] = (dot(m.Xall[t], m.Wc[...]) + bias).astype(BF)
        dev = att_device(t, w, block_part)
        send(m.QKVs.at[t], m.Rq.at[block_slot], m.s_q.at[k], m.r_q.at[block_slot], dev,
             jnp.logical_not(is_me(dev)))

        @pl.when(is_me(dev))
        def _():
            m.Rq[block_slot] = m.QKVs[t]

    lanes = lax.broadcasted_iota(jnp.int32, (1, DP), 1)

    def q_lane(h):
        return jnp.logical_and(lanes >= h * HEAD, lanes < (h + 1) * HEAD)

    def v_lane(h):
        return jnp.logical_and(lanes >= OFF + h * HEAD, lanes < OFF + (h + 1) * HEAD)

    for j in range(W):
        src = (j * R + r_att, g_att)
        arrive(m.Rq.at[j], m.r_q.at[j], jnp.logical_not(is_me(src)))
        kv_rows = pl.ds(pl.multiple_of(r_att * Q + j * B, B), B)
        for k in range(1, R):
            dev = att_device(s, g_att, lax.rem(r_att + k, R))
            send(m.Rq.at[j, :, pl.ds(0, KVW)], m.KV.at[kv_rows], m.s_kv.at[(k - 1) * W + j],
                 m.r_kv.at[r_att * W + j], dev)
        m.KV[kv_rows, :] = m.Rq[j, :, 0:KVW]
        q = m.Rq[j, :, KVW:MW] * jnp.asarray(HEAD**-0.5, BF)
        for h in range(HW):
            m.Qm[h, j * B : (j + 1) * B, :] = jnp.where(q_lane(h), q, jnp.zeros_like(q))
    for k in range(1, R):
        r = lax.rem(r_att + k, R)
        for j in range(W):
            arrive(m.KV.at[pl.ds(pl.multiple_of(r * Q + j * B, B), B)], m.r_kv.at[r * W + j])

    KC = 2 * B
    PER_SET = Q // KC
    len_s = m.Vv[s, LEN : LEN + 1, 0:1]

    def alive(chunk):
        r, half = lax.div(chunk, PER_SET), lax.rem(chunk, PER_SET)
        row = lax.broadcasted_iota(jnp.int32, (KC, Q), 0)
        later = (row >= B).astype(jnp.int32)
        place = ((2 * half + later) * R + r) * B + row - later * B
        return place.astype(F32) < len_s

    m.mrow[...] = jnp.full(m.mrow.shape, FLOOR, F32)
    m.lrow[...] = jnp.zeros(m.lrow.shape, F32)
    m.OT[...] = jnp.zeros(m.OT.shape, F32)

    def attend(chunk, carry):
        rows = pl.ds(pl.multiple_of(chunk * KC, KC), KC)
        keys = m.KV[rows, 0:DP]
        values_t = m.KV[rows, KVW - DP : KVW].T
        live = alive(chunk)
        for h in range(HW):
            scores = jnp.where(live, dot_nt(keys, m.Qm[h]), FLOOR)
            top = m.mrow[h : h + 1, :]
            new_top = jnp.maximum(top, jnp.max(scores, 0, keepdims=True))
            prob = jnp.exp(scores - new_top)
            factor = jnp.exp(top - new_top)
            m.mrow[h : h + 1, :] = new_top
            m.lrow[h : h + 1, :] = m.lrow[h : h + 1, :] * factor + col_sum(prob)
            a, b = OFF + h * HEAD, OFF + (h + 1) * HEAD
            m.OT[a:b, :] = m.OT[a:b, :] * factor + dot(values_t[a:b, :], prob.astype(BF))
        return carry

    lax.fori_loop(0, R * PER_SET, attend, 0)
    for h in range(HW):
        a, b = OFF + h * HEAD, OFF + (h + 1) * HEAD
        m.OT[a:b, :] = m.OT[a:b, :] / m.lrow[h : h + 1, :]
    m.lrow[0:HW, :] = m.mrow[0:HW, :] + jnp.log(m.lrow[0:HW, :])
    for j in range(W):
        m.Osend[j] = m.OT[:, j * B : (j + 1) * B].T.astype(BF)
        dev = (j * R + r_att, s)
        send(m.Osend.at[j], m.Mix.at[g_att], m.s_o.at[j], m.r_o.at[g_att], dev, jnp.logical_not(is_me(dev)))

        @pl.when(is_me(dev))
        def _():
            m.Mix[g_att] = m.Osend[j]

    for k in (1, 2, 3):
        arrive(m.Outp.at[jnp.bitwise_xor(w, k), pl.ds(OFF, DW)], m.r_ow.at[k])
    resid = m.Xall[w].astype(F32) + vec(OUTB)
    for g in range(W):
        arrive(m.Mix.at[g], m.r_o.at[g], jnp.logical_not(is_me(att_device(w, g, block_part))))
        resid = resid + dot(m.Mix[g], m.Outp[g])
    n1, r1 = norm_stats(resid)
    m.n1[...] = n1
    m.r1[...] = r1
    n1_full = n1 * vec(GAIN1) + vec(SHIFT1)
    m.N1f[...] = n1_full
    m.N1all[w] = n1_full.astype(BF)
    gather_start(m.N1all, m.s_n, m.r_n)

    for k in (1, 2, 3):
        arrive(m.Upc.at[pl.ds(jnp.bitwise_xor(w, k) * DW, DW)], m.r_uw.at[k])
    up_bias = m.upb[0:1, :]

    def expand(t):
        h = dot(m.N1all[t], m.Upc[...]) + up_bias
        phi = 0.5 * (1.0 + lax.erf(h * (2.0**-0.5)))
        m.Gs[t] = (h * phi).astype(BF)
        m.Hp[t] = phi + h * ((2.0 * math.pi) ** -0.5) * jnp.exp(-0.5 * h * h)

    expand(w)
    for k in (1, 2, 3):
        gather_wait(m.N1all, m.s_n, m.r_n, k)
        expand(jnp.bitwise_xor(w, k))

    ffn = scatter_sum(lambda t: dot(m.Gs[t], m.Dn[...]), m.Fs, m.Fr, m.s_f, m.r_f)
    n2, r2 = norm_stats(m.N1f[...] + ffn + vec(DOWNB))
    m.n2[...] = n2
    y_ref[...] = (n2 * vec(GAIN2) + vec(SHIFT2)).astype(BF)

    place = c * B + lax.broadcasted_iota(jnp.int32, (B, D), 0)
    dy = jnp.where(place.astype(F32) < m.Vv[w, LEN : LEN + 1, 0:1], m.Cot[...].astype(F32), 0.0)
    d_r2 = norm_back(dy, n2, r2, vec(GAIN2))
    m.dR2[...] = d_r2
    m.dFall[w] = d_r2.astype(BF)
    gather_start(m.dFall, m.s_df, m.r_df)
    m.gv[2:3, :] = col_sum(dy * n2)
    m.gv[3:4, :] = col_sum(dy)
    m.gv[5:6, :] = col_sum(m.dFall[w].astype(F32))

    def shrink(t):
        m.dHs[t] = (dot_nt(m.dFall[t], m.Dn[...]) * m.Hp[t]).astype(BF)

    shrink(w)
    for k in (1, 2, 3):
        gather_wait(m.dFall, m.s_df, m.r_df, k)
        shrink(jnp.bitwise_xor(w, k))

    def flat(ref):
        return ref[...].reshape(Q, ref.shape[-1])

    def put_grad(name, plain, lhs, rhs, parts, lead=0):
        rows = lhs.shape[-1] // parts
        for i in range(parts):
            val = dot_tn(lhs[:, :, i * rows : (i + 1) * rows].reshape(Q, rows), flat(rhs)).astype(BF)
            if cfg.fused:
                _, ch, cols, _ = cfg.grads[name]
                n = (rows - lead) // (4 * ch)
                getattr(m, "G" + name)[i * n : (i + 1) * n] = val[lead:].reshape(n, 2, 2, ch, cols)
            else:
                plain[i * rows : (i + 1) * rows, :] = val

    pump = make_sums(cfg, m, c, w, send, arrive)

    def early():
        put_grad("down", gdown_ref, m.Gs, m.dFall, 2)
        pump.start(("down",))

    def late():
        put_grad("up", gup_ref, m.N1all, m.dHs, 2)
        m.gv[6:7, :] = col_sum(flat(m.dHs).astype(F32))
        pump.add(("down", "up"), 2)
        pump.run(cfg.pump[0])

    d_n1 = scatter_sum(
        lambda t: dot_nt(m.dHs[t], m.Upc[...]), m.dNs, m.dNr, m.s_dn, m.r_dn, early, late) + m.dR2[...]
    n1 = m.n1[...]
    d_r1 = norm_back(d_n1, n1, m.r1[...], vec(GAIN1))
    m.dR1[...] = d_r1
    d_a = d_r1.astype(BF)
    m.dAall[w] = d_a
    for g in range(W):
        m.dOs[g] = dot_nt(d_a, m.Outp[g]).astype(BF)
        dev = att_device(w, g, block_part)
        send(m.dOs.at[g], m.dOr.at[block_slot], m.s_do.at[g], m.r_do.at[block_slot], dev,
             jnp.logical_not(is_me(dev)))

        @pl.when(is_me(dev))
        def _():
            m.dOr[block_slot] = m.dOs[g]

    pump.start(("up",))
    gather_start(m.dAall, m.s_da, m.r_da)
    for k in (2, 3, 1):
        send(m.Mix.at[jnp.bitwise_xor(w, k)], m.MixT.at[w], m.s_mt.at[k], m.r_mt.at[k], peer(k))
    m.MixT[w] = m.Mix[w]
    m.gv[0:1, :] = col_sum(d_n1 * n1)
    m.gv[1:2, :] = col_sum(d_n1)
    m.gv[4:5, :] = col_sum(d_a.astype(F32))

    pump.run(cfg.pump[1])
    for j in range(W):
        arrive(m.dOr.at[j], m.r_do.at[j], jnp.logical_not(is_me((j * R + r_att, s))))
        d_o = m.dOr[j]
        cols = slice(j * B, (j + 1) * B)
        for h in range(HW):
            m.Dm[h, cols, :] = jnp.where(v_lane(h), d_o, jnp.zeros_like(d_o))
        prod = m.OT[:, cols] * d_o.astype(F32).T
        for h in range(HW):
            m.drow[h : h + 1, cols] = col_sum(prod[OFF + h * HEAD : OFF + (h + 1) * HEAD, :])
    m.dQT[...] = jnp.zeros(m.dQT.shape, F32)

    def attend_back(step, carry):
        chunk = lax.rem((r_att + 1) * PER_SET + step, R * PER_SET)
        rows = pl.ds(pl.multiple_of(chunk * KC, KC), KC)
        keys = m.KV[rows, 0:DP]
        values = m.KV[rows, KVW - DP : KVW]
        keys_t = keys.T
        live = alive(chunk)
        d_k = jnp.zeros((KC, DP), F32)
        d_v = jnp.zeros((KC, DP), F32)
        for h in range(HW):
            scores = dot_nt(keys, m.Qm[h])
            prob = jnp.where(live, jnp.exp(scores - m.lrow[h : h + 1, :]), 0.0)
            d_prob = dot_nt(values, m.Dm[h])
            d_s = (prob * (d_prob - m.drow[h : h + 1, :])).astype(BF)
            d_k = d_k + dot(d_s, m.Qm[h])
            d_v = d_v + dot(prob.astype(BF), m.Dm[h])
            a, b = h * HEAD, (h + 1) * HEAD
            m.dQT[a:b, :] = m.dQT[a:b, :] + dot(keys_t[a:b, :], d_s)
        lead = KVW - DP
        d_kv = jnp.concatenate([d_k[:, 0:lead], d_k[:, lead:] + d_v[:, 0 : DP - lead], d_v[:, DP - lead :]], 1)
        place, part = lax.div(step, PER_SET), lax.rem(step, PER_SET)
        rows = pl.ds(pl.multiple_of(part * KC, KC), KC)
        if carry is None:
            m.dKVf[rows, :] = d_kv
        else:
            m.dKVs[place, rows, :] = d_kv.astype(BF)
        return carry

    lax.fori_loop(0, (R - 1) * PER_SET, attend_back, 0)
    for k in range(1, R):
        send(m.dKVs.at[k - 1], m.dKVr.at[R - k - 1], m.s_dkv.at[k - 1], m.r_dkv.at[R - k - 1],
             att_device(s, g_att, lax.rem(r_att + k, R)))
    pump.run(cfg.pump[2])
    lax.fori_loop((R - 1) * PER_SET, R * PER_SET, attend_back, None)
    pump.run(cfg.pump[3])
    for k in range(1, R):
        arrive(m.dKVr.at[k - 1], m.r_dkv.at[k - 1])
    for j in range(W):
        d_kv = m.dKVf[j * B : (j + 1) * B, :]
        for k in range(1, R):
            d_kv = d_kv + m.dKVr[k - 1, j * B : (j + 1) * B, :].astype(F32)
        m.dqs[j, :, 0:KVW] = d_kv.astype(BF)
        d_q = m.dQT[:, j * B : (j + 1) * B].T * (HEAD**-0.5)
        m.dqs[j, :, KVW:MW] = jnp.where(lanes < DW, d_q, 0.0).astype(BF)
        dev = (j * R + r_att, g_att)
        send(m.dqs.at[j], m.dqr.at[s], m.s_dq.at[j], m.r_dq.at[s], dev, jnp.logical_not(is_me(dev)))

        @pl.when(is_me(dev))
        def _():
            m.dqr[s] = m.dqs[j]

    for k in (1, 2, 3):
        gather_wait(m.dAall, m.s_da, m.r_da, k)
        arrive(m.MixT.at[jnp.bitwise_xor(w, k)], m.r_mt.at[k])
    put_grad("out", gout_ref, m.MixT, m.dAall, 1, OFF)
    pump.start(("out",))
    pump.run(cfg.pump[4])

    for t in range(W):
        arrive(m.dqr.at[t], m.r_dq.at[t], jnp.logical_not(is_me(att_device(t, w, block_part))))

    def early():
        put_grad("qkv", gqkv_ref, m.Xall, m.dqr, 2)
        pump.start(("qkv",))

    def late():
        m.gv[7:8, 0:MW] = col_sum(flat(m.dqr).astype(F32))
        m.gv[7:8, MW:D] = jnp.zeros((1, D - MW), F32)
        pump.add(("out", "qkv"), 1)
        pump.run(cfg.pump[5])

    d_x = scatter_sum(
        lambda t: dot_nt(m.dqr[t], m.Wc[...]), m.dxs, m.dxr, m.s_dx, m.r_dx, early, late)
    gx_ref[...] = (m.dR1[...] + d_x).astype(BF)

    if not cfg.fused:
        gvec_ref[0] = m.gv[...]
    else:
        total = m.gv[...]
        for i, dev in enumerate(pump.partners):
            m.Va[i] = total
            send(m.Va.at[i], m.Vb.at[i], m.s_v1.at[i], m.r_v1.at[i], dev)
            pump.run(cfg.pump[6])
            arrive(m.Vb.at[i], m.r_v1.at[i])
            total = total + m.Vb[i]
        for t in range(W):
            m.Vt[t, 0:6, :] = total[0:6, t * DW : (t + 1) * DW]
            m.Vt[t, 6:7, :] = total[7:8, 2 * DW : 3 * DW]
            m.Vt[t, 7:8, :] = total[7:8, DW : 2 * DW]
        m.Vw[w] = m.Vt[w]
        for k in (2, 3, 1):
            send(m.Vt.at[jnp.bitwise_xor(w, k)], m.Vw.at[w], m.s_vw.at[k], m.r_vw.at[k], peer(k))
        m.gv[6:7, :] = total[6:7, :]
        pump.run(cfg.pump[6])
        for k in (1, 2, 3):
            arrive(m.Vw.at[jnp.bitwise_xor(w, k)], m.r_vw.at[k])
        gvec_ref[0:6, 0:DW] = m.Vw[0, 0:6, :] + m.Vw[1, 0:6, :] + m.Vw[2, 0:6, :] + m.Vw[3, 0:6, :]
        for i in range(2):
            gvec_ref[6:7, i * DW : (i + 1) * DW] = m.Vw[2 * odd + i, pl.ds(6 + half, 1), :]
        gvec_ref[7:8, :] = m.gv[6:7, :]
        pump.run(1000)

    for pred, end in drains:
        if pred is None:
            end()
        else:
            pl.when(pred)(end)


def body(C, W, tokens, lengths, qkv_weight, out_weight, up_weight, down_weight, qv_bias, out_bias, up_bias,
         down_bias, gain_one, shift_one, gain_two, shift_two, cotangent):
    _, B, D = tokens.shape
    FW = down_weight.shape[0]
    DW = D // W
    DP = -(-DW // 128) * 128
    KVW = 2 * DW
    MW = KVW + DP
    R = C // W
    cfg = SimpleNamespace(C=C, W=W, B=B, D=D, FW=FW, DW=DW, DP=DP, KVW=KVW, MW=MW, R=R, HW=HEADS // W)
    cfg.fused = R == 2 and C == 8 and DW % 64 == 0 and FW % (64 * W) == 0
    cfg.grads = dict(down=(W, FW // W // 4, D, False), up=(W, DW // 4, FW, True), qkv=(W, DW // 4, MW, True),
                     out=(1, DW // 4, D, False))
    cfg.pump = (2, 2, 1, 1, 2, 2, 1)
    w = lax.axis_index("wa")
    small = [v.astype(F32) for v in (out_bias, down_bias, gain_one, shift_one, gain_two, shift_two, qv_bias, up_bias)]
    small.append(jnp.broadcast_to(lengths.astype(F32), ((VROWS - LEN) * DW,)))
    vec = jnp.concatenate(small).reshape(VROWS, DW)

    plan = make_plan(cfg)
    names = list(plan)
    vm = pl.BlockSpec(memory_space=pltpu.VMEM)
    hbm = pl.BlockSpec(memory_space=pl.ANY)
    shape = jax.ShapeDtypeStruct
    if cfg.fused:
        outs = [shape((n, 2, 2, ch, cols), BF) for n, ch, cols, _ in (cfg.grads[k] for k in ("qkv", "out", "up", "down"))]
        outs.append(shape((GROWS, D), F32))
    else:
        outs = [shape((D, MW), BF), shape((DP, D), BF), shape((D, FW), BF), shape((FW, D), BF),
                shape((1, GROWS, D), F32)]
    outs = [shape((B, D), BF), shape((B, D), BF)] + outs
    args = (tokens.reshape(B, D), cotangent.reshape(B, D), qkv_weight, vec, out_weight, up_weight, down_weight)
    y, gx, gqkv, gout, gup, gdown, gvec = pl.pallas_call(
        functools.partial(layer_kernel, cfg, names, len(args)),
        out_shape=outs,
        in_specs=[hbm] * len(args),
        out_specs=[vm] * len(outs),
        scratch_shapes=[plan[n] for n in names],
        compiler_params=pltpu.CompilerParams(collective_id=0, has_side_effects=True, vmem_limit_bytes=60 << 20),
        name="layer",
    )(*args)
    if cfg.fused:
        return finish(cfg, y, gx, gqkv, gout, gup, gdown, gvec)

    def to_rows(g):
        g = lax.psum(g, "ctx").reshape(W, DW, g.shape[1])
        return lax.all_to_all(g, "wa", 0, 0, tiled=True).transpose(1, 0, 2).reshape(DW, -1)

    gq = to_rows(gqkv).reshape(DW, W, MW).astype(F32)
    gup = to_rows(gup)
    gout, gdown, gvec = lax.psum((gout, gdown, gvec), "ctx")
    gvec = lax.all_gather(gvec, "wa", axis=0, tiled=True)
    gqkv = jnp.concatenate([gq[:, :, a : a + DW].reshape(DW, D) for a in (KVW, 0, DW)], 1)
    own = lax.dynamic_slice_in_dim(jnp.sum(gvec, 0)[0:6], w * DW, DW, 1)
    g_upb = lax.dynamic_slice_in_dim(gvec, w, 1, 0)[0, 6]
    g_qv = jnp.concatenate([gvec[:, 7, KVW : KVW + DW].reshape(D), gvec[:, 7, DW:KVW].reshape(D)])
    g_qv = lax.dynamic_slice_in_dim(g_qv, w * (2 * D // W), 2 * D // W)
    return (y.reshape(1, B, D), gx.reshape(1, B, D), gqkv, gout[DP - DW :].astype(F32), gup.astype(F32),
            gdown.astype(F32), g_qv, own[4], g_upb, own[5], own[0], own[1], own[2], own[3])


def finish_kernel(cfg, y, gx, gqkv, gout, gup, gdown, gvec, o_y, o_gx, o_qkv, o_out, o_up, o_down, o_qv, o_outb, o_upb,
                  o_downb, o_g1, o_s1, o_g2, o_s2):
    W, D, DW, MW, KVW = cfg.W, cfg.D, cfg.DW, cfg.MW, cfg.KVW
    o_y[0] = y[...]
    o_gx[0] = gx[...]
    for g in range(W):
        rows = gqkv[g].reshape(DW, MW).astype(F32)
        for third, a in enumerate((KVW, 0, DW)):
            o_qkv[:, third * D + g * DW : third * D + (g + 1) * DW] = rows[:, a : a + DW]
        o_up[:, g * cfg.FW : (g + 1) * cfg.FW] = gup[g].reshape(DW, cfg.FW).astype(F32)
    o_out[...] = gout[...].reshape(o_out.shape).astype(F32)
    o_down[...] = gdown[...].reshape(o_down.shape).astype(F32)
    o_qv[...] = gvec[6, 0 : 2 * DW]
    o_upb[...] = gvec[7, 0 : cfg.FW]
    for row, ref in enumerate((o_g1, o_s1, o_g2, o_s2, o_outb, o_downb)):
        ref[...] = gvec[row, 0:DW]


def finish(cfg, *arrays):
    B, D, DW, W, FW = cfg.B, cfg.D, cfg.DW, cfg.W, cfg.FW
    shapes = [(1, B, D)] * 2 + [(DW, 3 * D), (DW, D), (DW, W * FW), (FW, D), (2 * DW,), (DW,), (FW,)] + [(DW,)] * 5
    vm = pl.BlockSpec(memory_space=pltpu.VMEM)
    return pl.pallas_call(
        functools.partial(finish_kernel, cfg),
        out_shape=[jax.ShapeDtypeStruct(s, BF if i < 2 else F32) for i, s in enumerate(shapes)],
        in_specs=[vm] * len(arrays),
        out_specs=[vm] * len(shapes),
        name="results",
    )(*arrays)


def solution(mesh):
    tok, vec, mat = P("wa", "ctx", None), P("wa"), P("wa", None)
    return jax.shard_map(
        functools.partial(body, mesh.shape["ctx"], mesh.shape["wa"]),
        mesh=mesh,
        in_specs=(tok, vec, mat, mat, mat, mat) + (vec,) * 8 + (tok,),
        out_specs=(tok, tok, mat, mat, mat, mat) + (vec,) * 8,
        check_vma=False,
    )
```

```python
import functools
import math
from types import SimpleNamespace

import jax
import jax.numpy as jnp
from jax import lax
from jax.experimental import pallas as pl
from jax.experimental.pallas import tpu as pltpu
from jax.sharding import PartitionSpec as P

HEADS = 12
HEAD = 64
EPS = 1e-12
FLOOR = -1e30
MESH = pl.DeviceIdType.MESH
BF = jnp.bfloat16
F32 = jnp.float32

OUTB, DOWNB, GAIN1, SHIFT1, GAIN2, SHIFT2, QVB = range(7)
UPB, LEN = 8, 12
VROWS = 16
GROWS = 8

ALL = (0, 1, 2, 3)
SCHEDULE = dict(
    norm=((2, "down", (0,)), ),
    sent0=((3, "down", (0,)), (2, "down", (1,)), ),
    sent1=(),
    sent2=((2, "down", (2,)), ),
    sent3=(),
    arrived=((3, "down", (1,)), (2, "down", (3,)), (2, "up", (0,)), ),
    between=((4, "down", (0,)), (3, "down", (2,)), (2, "up", (1,)), ),
    after=((5, "down", (0,)), (4, "down", (1,)), (3, "down", (3,)), (3, "up", (0,)), (2, "up", (2,)), ),
    part=(),
    dq1=(),
    dq2=(),
    dq3=(),
    out=((5, "down", (1,)), (4, "down", (2,)), (3, "up", (1,)), (2, "up", (3,)), ),
    wait0=((6, "down", (0,)), (5, "down", (2,)), (4, "down", (3,)), (4, "up", (0,)), (3, "up", (2,)), ),
    wait1=((6, "down", (1,)), (5, "down", (3,)), (4, "up", (1,)), (3, "up", (3,)), ),
    wait2=(),
    wait3=((5, "up", (0,)), ),
    qkv=((6, "down", (2,)), (6, "down", (3,)), (6, "up", (0,)), (4, "up", (2,)), (4, "up", (3,)), ),
)


def dot(a, b):
    return lax.dot_general(a, b, (((1,), (0,)), ((), ())), preferred_element_type=F32)


def dot_nt(a, b):
    return lax.dot_general(a, b, (((1,), (1,)), ((), ())), preferred_element_type=F32)


def dot_tn(a, b):
    return lax.dot_general(a, b, (((0,), (0,)), ((), ())), preferred_element_type=F32)


def norm_stats(v):
    center = v - jnp.mean(v, -1, keepdims=True)
    rstd = lax.rsqrt(jnp.mean(center * center, -1, keepdims=True) + EPS)
    return center * rstd, rstd


def norm_back(dy, normed, rstd, gain):
    dn = dy * gain
    return rstd * (
        dn - jnp.mean(dn, -1, keepdims=True) - normed * jnp.mean(dn * normed, -1, keepdims=True)
    )


def col_sum(v):
    return jnp.sum(v, 0, keepdims=True)


def make_plan(cfg):
    C, W, B, D, FW, DW, DP, KVW, MW, R = (
        cfg.C, cfg.W, cfg.B, cfg.D, cfg.FW, cfg.DW, cfg.DP, cfg.KVW, cfg.MW, cfg.R)
    V = pltpu.VMEM
    dma = pltpu.SemaphoreType.DMA
    Q = W * B
    plan = dict(
        Xall=V((W, B, D), BF), Wc=V((D, MW), BF), Wq=V((DW, 3 * D), BF), Ws=V((W, DW, MW), BF), Vv=V((W, VROWS, DW), F32),
        Vs=V((8, D), F32), Outp=V((W, DP, D), BF), Upc=V((D, FW), BF), Dn=V((FW, D), BF), Cot=V((B, D), BF),
        QKVs=V((W, B, MW), BF), Rq=V((W, B, DP), BF), KV=V((R * Q, KVW), BF),
        Qm=V((cfg.HW, Q, DP), BF), Dm=V((cfg.HW, Q, DP), BF),
        mrow=V((8, Q), F32), lrow=V((8, Q), F32), bias=V((8, MW), F32), upb=V((8, cfg.FW), F32), drow=V((8, Q), F32), OT=V((DP, Q), F32), dQT=V((DP, Q), F32),
        Osend=V((W, B, DP), BF), Mix=V((W, B, DP), BF), MixT=V((W, B, DP), BF),
        N1f=V((B, D), F32), n1=V((B, D), F32), n2=V((B, D), F32), r1=V((B, 1), F32),
        N1all=V((W, B, D), BF), Hp=V((W, B, FW), F32), Gs=V((W, B, FW), BF),
        Fs=V((W, B, D), BF), Fr=V((3, B, D), BF), dR2=V((B, D), F32), dFall=V((W, B, D), BF),
        dHs=V((W, B, FW), BF), dNs=V((W, B, D), BF), dNr=V((3, B, D), BF), dR1=V((B, D), F32),
        dAall=V((W, B, D), BF), dOs=V((W, B, DP), BF), dOr=V((W, B, DP), BF),
        dKVf=V((Q, KVW), F32), dKVs=V((R - 1, Q, KVW), BF), dKVr=V((R - 1, Q, KVW), BF),
        dqs=V((W, B, MW), BF), dqr=V((W, B, MW), BF), dxs=V((W, B, D), BF), dxr=V((3, B, D), BF),
        gv=V((GROWS, D), F32),
    )
    sems = dict(
        x=4, wq=4, wf=12, vv=4, ow=4, uw=4, own=6,
        q=W, kv=W, kf=(R - 1) * W, o=W, mt=4, n=4, f=4, df=4, dn=4, da=4, do=W, dkv=R - 1, dq=W, dx=4,
    )
    recvs = dict(sems, kf=R * W)
    if cfg.fused:
        for name, (pieces, ch, cols, to_rows) in cfg.grads.items():
            plan["G" + name] = V((pieces, 2, 2, ch, cols), BF)
            plan["X" + name] = V((pieces, 3, ch, cols), BF)
            plan["T" + name] = V((pieces, ch, cols), BF)
            plan["Y" + name] = V((pieces, ch, cols), BF)
            plan["U" + name] = V((pieces, ch, cols), BF)
            plan["Z" + name] = V((pieces, ch, cols), BF)
            for kind in ("g1", "g2", "g3", "g4", "g5", "g6"):
                sems[kind + name] = 3 * pieces
                recvs[kind + name] = 3 * pieces
            if to_rows:
                plan["R" + name] = V((pieces, ch, cols), BF)
        plan.update(Va=V((4, GROWS, D), F32), Vb=V((3, GROWS, D), F32), Vt=V((W, GROWS, DW), F32),
                    Vw=V((W, GROWS, DW), F32))
        sems.update(v1=3, vw=W)
        recvs.update(v1=3, vw=W)
    for name, n in sems.items():
        plan["s_" + name] = dma((n,))
    for name, n in recvs.items():
        plan["r_" + name] = dma((n,))
    return plan


class Sums:
    def __init__(self, cfg, m, c, w, send, arrive):
        self.cfg, self.m, self.c, self.w, self.send, self.arrive = cfg, m, c, w, send, arrive
        self.x, self.near = lax.rem(c, 2), lax.rem(lax.div(c, 2), 2)
        self.partners = [(jnp.bitwise_xor(c, k), w) for k in (1, 2, 4, 3)]
        self.done = set()
        self.long = (self.one, self.two, self.three, self.four, self.five, self.six, self.seven)
        self.short = (self.quarters, self.quarters_sum, self.four, self.spread, self.spread_end)

    def stages(self, name):
        return self.long if name in ("up", "down", "out") else self.short

    def step(self, k, name, p):
        if self.cfg.fused:
            self.stages(name)[k - 1](name, p)
            self.done.add((k, name, p))

    def start(self, names):
        for name in names:
            for p in range(self.cfg.grads[name][0]):
                self.step(1, name, p)

    def run(self, place):
        for k, name, pieces in SCHEDULE[place]:
            for p in pieces:
                self.step(k, name, p)

    def finish(self, names, others, gap):
        order, last = [], []
        for name in names:
            n = len(self.stages(name))
            for p in range(self.cfg.grads[name][0]):
                ahead = 1 + sum((k, name, p) in self.done for k in range(1, n + 1))
                for k in range(ahead, n):
                    order.append((p + k - ahead, -k, len(order), (k, name, p)))
                last.append((n, name, p))
        others = list(others)
        for i, step in enumerate(sorted(order)):
            if others and i % gap == gap - 1:
                others.pop(0)()
            self.step(*step[3])
        for other in others:
            other()
        for step in last:
            if step not in self.done:
                self.step(*step)

    def ref(self, kind, name):
        return getattr(self.m, kind + name)

    def go(self, kind, name, p, src, dst, dev):
        self.send(src, dst, self.ref("s_" + kind, name).at[p], self.ref("r_" + kind, name).at[p], dev)

    def got(self, kind, name, p, dst):
        self.arrive(dst, self.ref("r_" + kind, name).at[p])

    def piece(self, name, k):
        return jnp.bitwise_xor(self.w, k) if self.cfg.grads[name][3] else k

    def one(self, name, k):
        p = self.piece(name, k)
        self.go("g1", name, k, self.ref("G", name).at[p, 1 - self.x], self.ref("X", name).at[k, pl.ds(0, 2)],
                self.partners[0])

    def two(self, name, k):
        g, other, t = self.ref("G", name), self.ref("X", name), self.ref("T", name)
        self.got("g1", name, k, other.at[k, pl.ds(0, 2)])
        far = 1 - self.near
        mine = g[self.piece(name, k), self.x, far].astype(F32)
        t[k] = (mine + other[k, far].astype(F32)).astype(BF)
        self.go("g2", name, k, t.at[k], self.ref("Y", name).at[k], self.partners[1])

    def three(self, name, k):
        g, other, y, u = (self.ref(kind, name) for kind in "GXYU")
        self.got("g2", name, k, y.at[k])
        n = self.near
        mine = g[self.piece(name, k), self.x, n].astype(F32)
        u[k] = (mine + other[k, n].astype(F32) + y[k].astype(F32)).astype(BF)
        self.go("g3", name, k, u.at[k], self.ref("Z", name).at[k], self.partners[2])

    def four(self, name, k):
        u, z, fin = (self.ref(kind, name) for kind in "UZF")
        self.got("g3", name, k, z.at[k])
        total = (u[k].astype(F32) + z[k].astype(F32)).astype(BF)
        if not self.cfg.grads[name][3] or k == 0:
            fin[self.piece(name, k), self.x, self.near] = total
            return
        done = self.ref("R", name)
        done[k] = total
        self.go("g4", name, k, done.at[k], fin.at[self.w, self.x, self.near], (self.c, jnp.bitwise_xor(self.w, k)))

    def owned(self, name, k):
        here = self.ref("F", name).at[self.piece(name, k), self.x, self.near]
        if self.cfg.grads[name][3] and k > 0:
            self.got("g4", name, k, here)
        return here

    def five(self, name, k):
        here = self.owned(name, k)
        self.go("g5", name, k, here, here, self.partners[1])

    def six(self, name, k):
        fin, p = self.ref("F", name), self.piece(name, k)
        self.got("g5", name, k, fin.at[p, self.x, 1 - self.near])
        self.go("g6", name, k, fin.at[p, self.x], fin.at[p, self.x], self.partners[0])

    def seven(self, name, k):
        self.got("g6", name, k, self.ref("F", name).at[self.piece(name, k), 1 - self.x])

    def three_others(self):
        x, n = self.x, self.near
        return ((1 - x, n, self.partners[0]), (x, 1 - n, self.partners[1]), (1 - x, 1 - n, self.partners[3]))

    def quarters(self, name, k):
        p = self.piece(name, k)
        for i, (x, n, dev) in enumerate(self.three_others()):
            self.go("g1", name, 3 * k + i, self.ref("G", name).at[p, x, n], self.ref("X", name).at[k, i], dev)

    def quarters_sum(self, name, k):
        total = self.ref("G", name)[self.piece(name, k), self.x, self.near].astype(F32)
        for i in range(3):
            other = self.ref("X", name).at[k, i]
            self.got("g1", name, 3 * k + i, other)
            total = total + other[...].astype(F32)
        u = self.ref("U", name)
        u[k] = total.astype(BF)
        self.go("g3", name, k, u.at[k], self.ref("Z", name).at[k], self.partners[2])

    def spread(self, name, k):
        here = self.owned(name, k)
        for i, (_, _, dev) in enumerate(self.three_others()):
            self.go("g5", name, 3 * k + i, here, here, dev)

    def spread_end(self, name, k):
        p = self.piece(name, k)
        for i, (x, n, _) in enumerate(self.three_others()):
            self.got("g5", name, 3 * k + i, self.ref("F", name).at[p, x, n])


def layer_kernel(cfg, names, n_in, *refs):
    (x_ref, cot_ref, qkv_ref, out_ref, up_ref, down_ref, len_ref, *vec_refs) = refs[:n_in]
    y_ref, gx_ref, gqkv_ref, gout_ref, gup_ref, gdown_ref, gvec_ref = refs[n_in : n_in + 7]
    m = SimpleNamespace(**dict(zip(names, refs[n_in + 7 :])))
    if cfg.fused:
        m.Fqkv, m.Fout, m.Fup, m.Fdown = gqkv_ref, gout_ref, gup_ref, gdown_ref
    C, W, B, D, DW, DP, KVW, MW, R, HW = (
        cfg.C, cfg.W, cfg.B, cfg.D, cfg.DW, cfg.DP, cfg.KVW, cfg.MW, cfg.R, cfg.HW)
    OFF = DP - DW
    Q = W * B
    c = lax.axis_index("ctx")
    w = lax.axis_index("wa")
    block_part = lax.rem(c, R)
    block_slot = lax.div(c, R)
    s = lax.div(c, R)
    low = lax.rem(c, R)
    g_att = lax.div(w, 2) * 2 + lax.rem(low, 2)
    r_att = lax.div(low, 2) * 2 + lax.rem(w, 2)

    def att_device(t, g, r):
        return (t * R + lax.div(r, 2) * 2 + lax.rem(g, 2), lax.div(g, 2) * 2 + lax.rem(r, 2))

    def is_me(dev):
        return jnp.logical_and(dev[0] == c, dev[1] == w)

    drains = []

    def remote(src, dst, ss, rs, dev):
        return pltpu.make_async_remote_copy(
            src_ref=src, dst_ref=dst, send_sem=ss, recv_sem=rs, device_id=dev, device_id_type=MESH)

    def send(src, dst, ss, rs, dev, pred=None):
        def go():
            remote(src, dst, ss, rs, dev).start()

        def end():
            remote(src, dst, ss, rs, dev).wait_send()

        if pred is None:
            go()
        else:
            pl.when(pred)(go)
        drains.append((pred, end))

    def arrive(dst, rs, pred=None):
        def go():
            remote(dst, dst, rs, rs, (c, w)).wait_recv()

        if pred is None:
            go()
        else:
            pl.when(pred)(go)

    barrier = pltpu.get_barrier_semaphore()

    def greet(i, carry):
        ci, wi = lax.div(i, W), lax.rem(i, W)

        @pl.when(jnp.logical_not(is_me((ci, wi))))
        def _():
            pl.semaphore_signal(barrier, inc=1, device_id=(ci, wi), device_id_type=MESH)

        return carry

    lax.fori_loop(0, C * W, greet, 0)

    def entered():
        pl.semaphore_wait(barrier, C * W - 1)

    def peer(k):
        return (c, jnp.bitwise_xor(w, k))

    def gather_start(buf, ss, rs):
        send(buf.at[w], buf.at[w], ss.at[2], rs.at[2], peer(2))
        send(buf.at[w], buf.at[w], ss.at[1], rs.at[1], peer(1))

    def gather_wait(buf, ss, rs, k):
        if k == 1:
            arrive(buf.at[jnp.bitwise_xor(w, 1)], rs.at[1])
        if k == 2:
            t = jnp.bitwise_xor(w, 2)
            arrive(buf.at[t], rs.at[2])
            send(buf.at[t], buf.at[t], ss.at[3], rs.at[3], peer(1))
        if k == 3:
            arrive(buf.at[jnp.bitwise_xor(w, 3)], rs.at[3])

    def scatter_sum(part, stage, recv, ss, rs, early=None, late=None):
        t3, t2, t1 = (jnp.bitwise_xor(w, k) for k in (3, 2, 1))
        stage[t3] = part(t3).astype(BF)
        send(stage.at[t3], recv.at[1], ss.at[1], rs.at[1], peer(1))
        mine2 = part(t2)
        stage[t1] = part(t1).astype(BF)
        send(stage.at[t1], recv.at[0], ss.at[0], rs.at[0], peer(1))
        if early:
            early()
        arrive(recv.at[1], rs.at[1])
        stage[t2] = (mine2 + recv[1].astype(F32)).astype(BF)
        send(stage.at[t2], recv.at[2], ss.at[2], rs.at[2], peer(2))
        own = part(w)
        arrive(recv.at[0], rs.at[0])
        own = own + recv[0].astype(F32)
        if late:
            late()
        arrive(recv.at[2], rs.at[2])
        return own + recv[2].astype(F32)

    def scatter_steps(part, stage, recv, ss, rs):
        t3, t2, t1 = (jnp.bitwise_xor(w, k) for k in (3, 2, 1))

        def first():
            stage[t3] = part(t3).astype(BF)
            send(stage.at[t3], recv.at[1], ss.at[1], rs.at[1], peer(1))
            stage[t1] = part(t1).astype(BF)
            send(stage.at[t1], recv.at[0], ss.at[0], rs.at[0], peer(1))

        def second():
            mine2 = part(t2)
            arrive(recv.at[1], rs.at[1])
            stage[t2] = (mine2 + recv[1].astype(F32)).astype(BF)
            send(stage.at[t2], recv.at[2], ss.at[2], rs.at[2], peer(2))

        def third():
            own = part(w)
            arrive(recv.at[0], rs.at[0])
            own = own + recv[0].astype(F32)
            arrive(recv.at[2], rs.at[2])
            return own + recv[2].astype(F32)

        return first, second, third

    def local(src, dst, sem):
        cp = pltpu.make_async_copy(src, dst, sem)
        cp.start()
        return cp

    rows_w = pl.ds(w * DW, DW)
    own = [
        local(qkv_ref, m.Wq, m.s_own.at[0]),
        local(x_ref, m.Xall.at[w], m.s_own.at[1]),
        local(out_ref, m.Outp.at[w, pl.ds(OFF, DW)], m.s_own.at[2]),
        local(up_ref.at[:, pl.ds(pl.multiple_of(w * cfg.FW, cfg.FW), cfg.FW)], m.Upc.at[rows_w], m.s_own.at[3]),
        local(down_ref, m.Dn, m.s_own.at[4]),
        local(cot_ref, m.Cot, m.s_own.at[5]),
    ]
    own[0].wait()
    for g in range(W):
        for i, third in enumerate((1, 2, 0)):
            a = third * D + g * DW
            m.Ws[g, :, i * DW : (i + 1) * DW] = m.Wq[:, a : a + DW]
        m.Ws[g, :, 3 * DW : MW] = jnp.zeros((DW, MW - 3 * DW), BF)
    row = 0
    for ref in vec_refs:
        v = ref[...].astype(F32)
        for i in range(v.shape[0] // DW):
            m.Vv[w, row : row + 1, :] = v[i * DW : (i + 1) * DW].reshape(1, DW)
            row += 1
    m.Vv[w, row:VROWS, :] = jnp.full((VROWS - row, DW), len_ref[0].astype(F32))
    own[1].wait()
    entered()

    def part_rows(t, part, parts):
        return pl.ds(pl.multiple_of(t * DW + part * (DW // parts), 16), DW // parts)

    quarter = lax.rem(c, 4)

    def near_me(k):
        return (jnp.bitwise_xor(c, k), w)

    for k in (2, 3):
        send(m.Ws.at[jnp.bitwise_xor(w, k), part_rows(0, quarter, 4)], m.Wc.at[part_rows(w, quarter, 4)],
             m.s_wq.at[k], m.r_wq.at[k], peer(k))
    gather_start(m.Xall, m.s_x, m.r_x)
    send(m.Ws.at[jnp.bitwise_xor(w, 1)], m.Wc.at[rows_w], m.s_wq.at[1], m.r_wq.at[1], peer(1))
    for k in (2, 3, 1):
        send(m.Vv.at[w], m.Vv.at[w], m.s_vv.at[k], m.r_vv.at[k], peer(k))
    m.Wc[rows_w, :] = m.Ws[w]
    for t in range(W):
        m.Outp[t, 0:OFF, :] = jnp.zeros((OFF, D), BF)
    m.bias[...] = jnp.zeros(m.bias.shape, F32)
    for cp in own[2:]:
        cp.wait()
    for k in (2, 3):
        rows = m.Wc.at[part_rows(jnp.bitwise_xor(w, k), quarter, 4)]
        arrive(rows, m.r_wq.at[k])
        for i in (1, 2, 3):
            e = 3 * (k - 2) + i - 1
            send(rows, rows, m.s_wf.at[e], m.r_wf.at[e], near_me(i))
    for k in (1, 2, 3):
        gather_wait(m.Xall, m.s_x, m.r_x, k)
    arrive(m.Wc.at[pl.ds(jnp.bitwise_xor(w, 1) * DW, DW)], m.r_wq.at[1])
    for k in (1, 2, 3):
        arrive(m.Vv.at[jnp.bitwise_xor(w, k)], m.r_vv.at[k])
    for k in (2, 3, 1):
        send(out_ref, m.Outp.at[w, pl.ds(OFF, DW)], m.s_ow.at[k], m.r_ow.at[k], peer(k))
    for k in (2, 3, 1):
        cols = pl.ds(pl.multiple_of(jnp.bitwise_xor(w, k) * cfg.FW, cfg.FW), cfg.FW)
        send(up_ref.at[:, cols], m.Upc.at[rows_w], m.s_uw.at[k], m.r_uw.at[k], peer(k))
    for k in (2, 3):
        for i in (1, 2, 3):
            e = 3 * (k - 2) + i - 1
            arrive(m.Wc.at[part_rows(jnp.bitwise_xor(w, k), jnp.bitwise_xor(quarter, i), 4)], m.r_wf.at[e])

    for t in range(W):
        m.Vs[0:6, t * DW : (t + 1) * DW] = m.Vv[t, 0:6, :]
        m.upb[0:1, t * DW : (t + 1) * DW] = m.Vv[w, UPB + t : UPB + t + 1, :]
    upper, odd = lax.div(w, 2), lax.rem(w, 2)
    m.bias[0:1, DW : 2 * DW] = m.Vv[W // 2 + upper, pl.ds(QVB + odd, 1), :]
    m.bias[0:1, 2 * DW : 3 * DW] = m.Vv[upper, pl.ds(QVB + odd, 1), :]
    bias = m.bias[0:1, :]

    def vec(row):
        return m.Vs[row : row + 1, :]

    kv_rows = pl.ds(pl.multiple_of(block_part * Q + block_slot * B, B), B)
    order = [lax.rem(s + 1 + k, W) for k in range(W)]
    for k, t in enumerate(order):
        m.QKVs[t] = (dot(m.Xall[t], m.Wc[...]) + bias).astype(BF)
        dev = att_device(t, w, block_part)
        send(m.QKVs.at[t, :, pl.ds(KVW, DP)], m.Rq.at[block_slot], m.s_q.at[k], m.r_q.at[block_slot], dev,
             jnp.logical_not(is_me(dev)))
    for k, t in enumerate(order):
        dev = att_device(t, w, block_part)
        send(m.QKVs.at[t, :, pl.ds(0, KVW)], m.KV.at[kv_rows], m.s_kv.at[k], m.r_kv.at[block_slot], dev,
             jnp.logical_not(is_me(dev)))

        @pl.when(is_me(dev))
        def _():
            m.Rq[block_slot] = m.QKVs[t, :, KVW:MW]
            m.KV[kv_rows, :] = m.QKVs[t, :, 0:KVW]

    lanes = lax.broadcasted_iota(jnp.int32, (1, DP), 1)

    def q_lane(h):
        return jnp.logical_and(lanes >= h * HEAD, lanes < (h + 1) * HEAD)

    def v_lane(h):
        return jnp.logical_and(lanes >= OFF + h * HEAD, lanes < OFF + (h + 1) * HEAD)

    for j in range(W):
        arrive(m.Rq.at[j], m.r_q.at[j], jnp.logical_not(is_me((j * R + r_att, g_att))))
        q = m.Rq[j] * jnp.asarray(HEAD**-0.5, BF)
        for h in range(HW):
            m.Qm[h, j * B : (j + 1) * B, :] = jnp.where(q_lane(h), q, jnp.zeros_like(q))

    KC = 2 * B
    PER_SET = Q // KC
    len_s = m.Vv[s, LEN : LEN + 1, 0:1]

    def alive(chunk):
        r, half = lax.div(chunk, PER_SET), lax.rem(chunk, PER_SET)
        row = lax.broadcasted_iota(jnp.int32, (KC, Q), 0)
        later = (row >= B).astype(jnp.int32)
        place = ((2 * half + later) * R + r) * B + row - later * B
        return place.astype(F32) < len_s

    m.mrow[...] = jnp.full(m.mrow.shape, FLOOR, F32)
    m.lrow[...] = jnp.zeros(m.lrow.shape, F32)
    m.OT[...] = jnp.zeros(m.OT.shape, F32)

    def attend(chunk, carry):
        rows = pl.ds(pl.multiple_of(chunk * KC, KC), KC)
        keys = m.KV[rows, 0:DP]
        values_t = m.KV[rows, KVW - DP : KVW].T
        live = alive(chunk)
        for h in range(HW):
            scores = jnp.where(live, dot_nt(keys, m.Qm[h]), FLOOR)
            top = m.mrow[h : h + 1, :]
            new_top = jnp.maximum(top, jnp.max(scores, 0, keepdims=True))
            prob = jnp.exp(scores - new_top)
            factor = jnp.exp(top - new_top)
            m.mrow[h : h + 1, :] = new_top
            m.lrow[h : h + 1, :] = m.lrow[h : h + 1, :] * factor + col_sum(prob)
            a, b = OFF + h * HEAD, OFF + (h + 1) * HEAD
            m.OT[a:b, :] = m.OT[a:b, :] * factor + dot(values_t[a:b, :], prob.astype(BF))
        return carry

    for i in range(PER_SET):
        pair = jnp.bitwise_xor(lax.div(s, 2), i)
        for e in range(2):
            j = 2 * pair + e
            rows = m.KV.at[pl.ds(pl.multiple_of(r_att * Q + j * B, B), B)]
            arrive(rows, m.r_kv.at[j], jnp.logical_not(is_me((j * R + r_att, g_att))))
            for k in range(1, R):
                send(rows, rows, m.s_kf.at[(k - 1) * W + 2 * i + e], m.r_kf.at[r_att * W + j],
                     att_device(s, g_att, lax.rem(r_att + k, R)))
        attend(r_att * PER_SET + pair, 0)

        def others(k, carry):
            r = lax.rem(r_att + k, R)
            for e in range(2):
                j = 2 * pair + e
                arrive(m.KV.at[pl.ds(pl.multiple_of(r * Q + j * B, B), B)], m.r_kf.at[r * W + j])
            return attend(r * PER_SET + pair, carry)

        lax.fori_loop(1, R, others, 0)
    for h in range(HW):
        a, b = OFF + h * HEAD, OFF + (h + 1) * HEAD
        m.OT[a:b, :] = m.OT[a:b, :] / m.lrow[h : h + 1, :]
    m.lrow[0:HW, :] = m.mrow[0:HW, :] + jnp.log(m.lrow[0:HW, :])
    for j in range(W):
        m.Osend[j] = m.OT[:, j * B : (j + 1) * B].T.astype(BF)
        dev = (j * R + r_att, s)
        send(m.Osend.at[j], m.Mix.at[g_att], m.s_o.at[j], m.r_o.at[g_att], dev, jnp.logical_not(is_me(dev)))

        @pl.when(is_me(dev))
        def _():
            m.Mix[g_att] = m.Osend[j]

    for k in (1, 2, 3):
        arrive(m.Outp.at[jnp.bitwise_xor(w, k), pl.ds(OFF, DW)], m.r_ow.at[k])
    resid = m.Xall[w].astype(F32) + vec(OUTB)
    for g in range(W):
        arrive(m.Mix.at[g], m.r_o.at[g], jnp.logical_not(is_me(att_device(w, g, block_part))))
        resid = resid + dot(m.Mix[g], m.Outp[g])
    n1, r1 = norm_stats(resid)
    m.n1[...] = n1
    m.r1[...] = r1
    n1_full = n1 * vec(GAIN1) + vec(SHIFT1)
    m.N1f[...] = n1_full
    m.N1all[w] = n1_full.astype(BF)
    gather_start(m.N1all, m.s_n, m.r_n)

    for k in (1, 2, 3):
        arrive(m.Upc.at[pl.ds(jnp.bitwise_xor(w, k) * DW, DW)], m.r_uw.at[k])
    up_bias = m.upb[0:1, :]

    def expand(t):
        h = dot(m.N1all[t], m.Upc[...]) + up_bias
        phi = 0.5 * (1.0 + lax.erf(h * (2.0**-0.5)))
        m.Gs[t] = (h * phi).astype(BF)
        m.Hp[t] = phi + h * ((2.0 * math.pi) ** -0.5) * jnp.exp(-0.5 * h * h)

    expand(w)
    for k in (1, 2, 3):
        gather_wait(m.N1all, m.s_n, m.r_n, k)
        expand(jnp.bitwise_xor(w, k))

    ffn = scatter_sum(lambda t: dot(m.Gs[t], m.Dn[...]), m.Fs, m.Fr, m.s_f, m.r_f)
    n2, r2 = norm_stats(m.N1f[...] + ffn + vec(DOWNB))
    m.n2[...] = n2
    y_ref[...] = (n2 * vec(GAIN2) + vec(SHIFT2)).astype(BF)

    place = c * B + lax.broadcasted_iota(jnp.int32, (B, D), 0)
    dy = jnp.where(place.astype(F32) < m.Vv[w, LEN : LEN + 1, 0:1], m.Cot[...].astype(F32), 0.0)
    d_r2 = norm_back(dy, n2, r2, vec(GAIN2))
    m.dR2[...] = d_r2
    m.dFall[w] = d_r2.astype(BF)
    gather_start(m.dFall, m.s_df, m.r_df)
    m.gv[2:3, :] = col_sum(dy * n2)
    m.gv[3:4, :] = col_sum(dy)
    m.gv[5:6, :] = col_sum(m.dFall[w].astype(F32))

    def shrink(t):
        m.dHs[t] = (dot_nt(m.dFall[t], m.Dn[...]) * m.Hp[t]).astype(BF)

    shrink(w)
    for k in (1, 2, 3):
        gather_wait(m.dFall, m.s_df, m.r_df, k)
        shrink(jnp.bitwise_xor(w, k))

    def flat(ref):
        return ref[...].reshape(Q, ref.shape[-1])

    def put_grad(name, plain, lhs, rhs, parts, lead=0):
        rows = lhs.shape[-1] // parts
        for i in range(parts):
            val = dot_tn(lhs[:, :, i * rows : (i + 1) * rows].reshape(Q, rows), flat(rhs)).astype(BF)
            if cfg.fused:
                _, ch, cols, _ = cfg.grads[name]
                n = (rows - lead) // (4 * ch)
                getattr(m, "G" + name)[i * n : (i + 1) * n] = val[lead:].reshape(n, 2, 2, ch, cols)
            else:
                plain[i * rows : (i + 1) * rows, :] = val

    pump = Sums(cfg, m, c, w, send, arrive)

    def early():
        put_grad("down", gdown_ref, m.Gs, m.dFall, 2)
        pump.start(("down",))

    def late():
        put_grad("up", gup_ref, m.N1all, m.dHs, 2)
        m.gv[6:7, :] = col_sum(flat(m.dHs).astype(F32))
        pump.run("norm")

    d_n1 = scatter_sum(
        lambda t: dot_nt(m.dHs[t], m.Upc[...]), m.dNs, m.dNr, m.s_dn, m.r_dn, early, late) + m.dR2[...]
    n1 = m.n1[...]
    d_r1 = norm_back(d_n1, n1, m.r1[...], vec(GAIN1))
    m.dR1[...] = d_r1
    d_a = d_r1.astype(BF)
    m.dAall[w] = d_a
    for g in range(W):
        m.dOs[g] = dot_nt(d_a, m.Outp[g]).astype(BF)
        dev = att_device(w, g, block_part)
        send(m.dOs.at[g], m.dOr.at[block_slot], m.s_do.at[g], m.r_do.at[block_slot], dev,
             jnp.logical_not(is_me(dev)))

        @pl.when(is_me(dev))
        def _():
            m.dOr[block_slot] = m.dOs[g]

    pump.start(("up",))
    gather_start(m.dAall, m.s_da, m.r_da)
    for k in (2, 3, 1):
        send(m.Mix.at[jnp.bitwise_xor(w, k)], m.MixT.at[w], m.s_mt.at[k], m.r_mt.at[k], peer(k))
    m.MixT[w] = m.Mix[w]
    m.gv[0:1, :] = col_sum(d_n1 * n1)
    m.gv[1:2, :] = col_sum(d_n1)
    m.gv[4:5, :] = col_sum(d_a.astype(F32))

    for j in range(W):
        pump.run("sent%d" % j)
        arrive(m.dOr.at[j], m.r_do.at[j], jnp.logical_not(is_me((j * R + r_att, s))))
        d_o = m.dOr[j]
        cols = slice(j * B, (j + 1) * B)
        for h in range(HW):
            m.Dm[h, cols, :] = jnp.where(v_lane(h), d_o, jnp.zeros_like(d_o))
        prod = m.OT[:, cols] * d_o.astype(F32).T
        for h in range(HW):
            m.drow[h : h + 1, cols] = col_sum(prod[OFF + h * HEAD : OFF + (h + 1) * HEAD, :])
    m.dQT[...] = jnp.zeros(m.dQT.shape, F32)
    pump.run("arrived")

    def attend_back(step, carry):
        chunk = lax.rem((r_att + 1) * PER_SET + step, R * PER_SET)
        rows = pl.ds(pl.multiple_of(chunk * KC, KC), KC)
        keys = m.KV[rows, 0:DP]
        values = m.KV[rows, KVW - DP : KVW]
        keys_t = keys.T
        live = alive(chunk)
        d_k = jnp.zeros((KC, DP), F32)
        d_v = jnp.zeros((KC, DP), F32)
        for h in range(HW):
            scores = dot_nt(keys, m.Qm[h])
            prob = jnp.where(live, jnp.exp(scores - m.lrow[h : h + 1, :]), 0.0)
            d_prob = dot_nt(values, m.Dm[h])
            d_s = (prob * (d_prob - m.drow[h : h + 1, :])).astype(BF)
            d_k = d_k + dot(d_s, m.Qm[h])
            d_v = d_v + dot(prob.astype(BF), m.Dm[h])
            a, b = h * HEAD, (h + 1) * HEAD
            m.dQT[a:b, :] = m.dQT[a:b, :] + dot(keys_t[a:b, :], d_s)
        lead = KVW - DP
        d_kv = jnp.concatenate([d_k[:, 0:lead], d_k[:, lead:] + d_v[:, 0 : DP - lead], d_v[:, DP - lead :]], 1)
        place, part = lax.div(step, PER_SET), lax.rem(step, PER_SET)
        rows = pl.ds(pl.multiple_of(part * KC, KC), KC)
        if carry is None:
            m.dKVf[rows, :] = d_kv
        else:
            m.dKVs[place, rows, :] = d_kv.astype(BF)
        return carry

    lax.fori_loop(0, (R - 1) * PER_SET, attend_back, 0)
    for k in range(1, R):
        send(m.dKVs.at[k - 1], m.dKVr.at[R - k - 1], m.s_dkv.at[k - 1], m.r_dkv.at[R - k - 1],
             att_device(s, g_att, lax.rem(r_att + k, R)))
    pump.run("between")
    lax.fori_loop((R - 1) * PER_SET, R * PER_SET, attend_back, None)
    pump.run("after")
    pump.run("part")
    for k in range(1, R):
        arrive(m.dKVr.at[k - 1], m.r_dkv.at[k - 1])
    for j in range(W):
        d_kv = m.dKVf[j * B : (j + 1) * B, :]
        for k in range(1, R):
            d_kv = d_kv + m.dKVr[k - 1, j * B : (j + 1) * B, :].astype(F32)
        m.dqs[j, :, 0:KVW] = d_kv.astype(BF)
        d_q = m.dQT[:, j * B : (j + 1) * B].T * (HEAD**-0.5)
        m.dqs[j, :, KVW:MW] = jnp.where(lanes < DW, d_q, 0.0).astype(BF)
        dev = (j * R + r_att, g_att)
        send(m.dqs.at[j], m.dqr.at[s], m.s_dq.at[j], m.r_dq.at[s], dev, jnp.logical_not(is_me(dev)))

        @pl.when(is_me(dev))
        def _():
            m.dqr[s] = m.dqs[j]

    for k in (1, 2, 3):
        pump.run("dq%d" % k)
        gather_wait(m.dAall, m.s_da, m.r_da, k)
        arrive(m.MixT.at[jnp.bitwise_xor(w, k)], m.r_mt.at[k])
    put_grad("out", gout_ref, m.MixT, m.dAall, 1, OFF)
    pump.start(("out",))
    pump.run("out")

    for t in range(W):
        pump.run("wait%d" % t)
        arrive(m.dqr.at[t], m.r_dq.at[t], jnp.logical_not(is_me(att_device(t, w, block_part))))

    put_grad("qkv", gqkv_ref, m.Xall, m.dqr, 2)
    pump.start(("qkv",))
    pump.run("qkv")

    m.gv[7:8, 0:MW] = col_sum(flat(m.dqr).astype(F32))
    m.gv[7:8, MW:D] = jnp.zeros((1, D - MW), F32)

    def d_x(t):
        return dot_nt(m.dqr[t], m.Wc[...])

    token_steps = scatter_steps(d_x, m.dxs, m.dxr, m.s_dx, m.r_dx)

    def vectors(i):
        if i:
            arrive(m.Vb.at[i - 1], m.r_v1.at[i - 1])
            m.Va[i] = m.Va[i - 1] + m.Vb[i - 1]
        else:
            m.Va[0] = m.gv[...]
        if i < 3:
            send(m.Va.at[i], m.Vb.at[i], m.s_v1.at[i], m.r_v1.at[i], pump.partners[i])

    def vectors_to_rows():
        vectors(3)
        total = m.Va[3]
        for t in range(W):
            m.Vt[t, 0:6, :] = total[0:6, t * DW : (t + 1) * DW]
            m.Vt[t, 6:7, :] = total[7:8, 2 * DW : 3 * DW]
            m.Vt[t, 7:8, :] = total[7:8, DW : 2 * DW]
        m.Vw[w] = m.Vt[w]
        for k in (2, 3, 1):
            send(m.Vt.at[jnp.bitwise_xor(w, k)], m.Vw.at[w], m.s_vw.at[k], m.r_vw.at[k], peer(k))
        gvec_ref[7:8, :] = total[6:7, :]

    def vectors_end():
        for k in (1, 2, 3):
            arrive(m.Vw.at[jnp.bitwise_xor(w, k)], m.r_vw.at[k])
        gvec_ref[0:6, 0:DW] = m.Vw[0, 0:6, :] + m.Vw[1, 0:6, :] + m.Vw[2, 0:6, :] + m.Vw[3, 0:6, :]
        for i in range(2):
            gvec_ref[6:7, i * DW : (i + 1) * DW] = m.Vw[2 * odd + i, pl.ds(6 + upper, 1), :]

    steps = [functools.partial(vectors, i) for i in range(3)] + [vectors_to_rows, vectors_end]

    if not cfg.fused:
        for step in token_steps[:-1]:
            step()
        d_x_sum = token_steps[-1]()
        gvec_ref[0] = m.gv[...]
    else:
        vector_steps = [functools.partial(vectors, i) for i in range(3)] + [vectors_to_rows, vectors_end]
        pump.finish(("qkv", "out", "up", "down"), [token_steps[0], vector_steps[0], token_steps[1]] + vector_steps[1:], 3)
        d_x_sum = token_steps[2]()
    gx_ref[...] = (m.dR1[...] + d_x_sum).astype(BF)

    for pred, end in drains:
        if pred is None:
            end()
        else:
            pl.when(pred)(end)


def body(C, W, tokens, lengths, qkv_weight, out_weight, up_weight, down_weight, qv_bias, out_bias, up_bias,
         down_bias, gain_one, shift_one, gain_two, shift_two, cotangent):
    _, B, D = tokens.shape
    FW = down_weight.shape[0]
    DW = D // W
    DP = -(-DW // 128) * 128
    KVW = 2 * DW
    MW = KVW + DP
    R = C // W
    cfg = SimpleNamespace(C=C, W=W, B=B, D=D, FW=FW, DW=DW, DP=DP, KVW=KVW, MW=MW, R=R, HW=HEADS // W)
    cfg.fused = R == 2 and C == 8 and DW % 64 == 0 and FW % (64 * W) == 0
    cfg.grads = dict(down=(W, FW // W // 4, D, False), up=(W, DW // 4, FW, True), qkv=(W, DW // 4, MW, True),
                     out=(1, DW // 4, D, False))
    w = lax.axis_index("wa")
    small = (out_bias, down_bias, gain_one, shift_one, gain_two, shift_two, qv_bias, up_bias)

    plan = make_plan(cfg)
    names = list(plan)
    vm = pl.BlockSpec(memory_space=pltpu.VMEM)
    hbm = pl.BlockSpec(memory_space=pl.ANY)
    if cfg.fused:
        outs = [(n, 2, 2, ch, cols) for n, ch, cols, _ in (cfg.grads[k] for k in ("qkv", "out", "up", "down"))]
        place = pltpu.VMEM
    else:
        outs = [(D, MW), (DP, D), (D, FW), (FW, D)]
        place = jax.ShapeDtypeStruct
    outs = [place(a, BF) for a in [(B, D), (B, D)] + outs] + [place((GROWS, D) if cfg.fused else (1, GROWS, D), F32)]
    args = (tokens.reshape(B, D), cotangent.reshape(B, D), qkv_weight, out_weight, up_weight, down_weight, lengths, *small)
    y, gx, gqkv, gout, gup, gdown, gvec = pl.pallas_call(
        functools.partial(layer_kernel, cfg, names, len(args)),
        out_shape=outs,
        in_specs=[hbm] * 6 + [pl.BlockSpec(memory_space=pltpu.SMEM)] + [vm] * len(small),
        out_specs=[vm] * len(outs),
        scratch_shapes=[plan[n] for n in names],
        compiler_params=pltpu.CompilerParams(collective_id=0, has_side_effects=True, vmem_limit_bytes=(52 if cfg.fused else 60) << 20),
        name="layer",
    )(*args)
    if cfg.fused:
        return finish(cfg, y, gx, gqkv, gout, gup, gdown, gvec)

    def to_rows(g):
        g = lax.psum(g, "ctx").reshape(W, DW, g.shape[1])
        return lax.all_to_all(g, "wa", 0, 0, tiled=True).transpose(1, 0, 2).reshape(DW, -1)

    gq = to_rows(gqkv).reshape(DW, W, MW).astype(F32)
    gup = to_rows(gup)
    gout, gdown, gvec = lax.psum((gout, gdown, gvec), "ctx")
    gvec = lax.all_gather(gvec, "wa", axis=0, tiled=True)
    gqkv = jnp.concatenate([gq[:, :, a : a + DW].reshape(DW, D) for a in (KVW, 0, DW)], 1)
    own = lax.dynamic_slice_in_dim(jnp.sum(gvec, 0)[0:6], w * DW, DW, 1)
    g_upb = lax.dynamic_slice_in_dim(gvec, w, 1, 0)[0, 6]
    g_qv = jnp.concatenate([gvec[:, 7, KVW : KVW + DW].reshape(D), gvec[:, 7, DW:KVW].reshape(D)])
    g_qv = lax.dynamic_slice_in_dim(g_qv, w * (2 * D // W), 2 * D // W)
    return (y.reshape(1, B, D), gx.reshape(1, B, D), gqkv, gout[DP - DW :].astype(F32), gup.astype(F32),
            gdown.astype(F32), g_qv, own[4], g_upb, own[5], own[0], own[1], own[2], own[3])


def finish_kernel(cfg, y, gx, gqkv, gout, gup, gdown, gvec, o_y, o_gx, o_qkv, o_out, o_up, o_down, o_qv, o_outb, o_upb,
                  o_downb, o_g1, o_s1, o_g2, o_s2):
    W, D, DW, MW, KVW = cfg.W, cfg.D, cfg.DW, cfg.MW, cfg.KVW
    o_y[0] = y[...]
    o_gx[0] = gx[...]
    for g in range(W):
        rows = gqkv[g].reshape(DW, MW).astype(F32)
        for third, a in enumerate((KVW, 0, DW)):
            o_qkv[:, third * D + g * DW : third * D + (g + 1) * DW] = rows[:, a : a + DW]
        o_up[:, g * cfg.FW : (g + 1) * cfg.FW] = gup[g].reshape(DW, cfg.FW).astype(F32)
    o_out[...] = gout[...].reshape(o_out.shape).astype(F32)
    o_down[...] = gdown[...].reshape(o_down.shape).astype(F32)
    o_qv[...] = gvec[6, 0 : 2 * DW]
    o_upb[...] = gvec[7, 0 : cfg.FW]
    for row, ref in enumerate((o_g1, o_s1, o_g2, o_s2, o_outb, o_downb)):
        ref[...] = gvec[row, 0:DW]


def finish(cfg, *arrays):
    B, D, DW, W, FW = cfg.B, cfg.D, cfg.DW, cfg.W, cfg.FW
    shapes = [(1, B, D)] * 2 + [(DW, 3 * D), (DW, D), (DW, W * FW), (FW, D), (2 * DW,), (DW,), (FW,)] + [(DW,)] * 5
    vm = pl.BlockSpec(memory_space=pltpu.VMEM)
    arrays = [pltpu.with_memory_space_constraint(a, pltpu.VMEM) for a in arrays]
    return pl.pallas_call(
        functools.partial(finish_kernel, cfg),
        out_shape=[jax.ShapeDtypeStruct(s, BF if i < 2 else F32) for i, s in enumerate(shapes)],
        in_specs=[vm] * len(arrays),
        out_specs=[vm] * len(shapes),
        compiler_params=pltpu.CompilerParams(vmem_limit_bytes=32 << 20),
        name="results",
    )(*arrays)


def solution(mesh):
    tok, vec, mat = P("wa", "ctx", None), P("wa"), P("wa", None)
    return jax.shard_map(
        functools.partial(body, mesh.shape["ctx"], mesh.shape["wa"]),
        mesh=mesh,
        in_specs=(tok, vec, mat, mat, mat, mat) + (vec,) * 8 + (tok,),
        out_specs=(tok, tok, mat, mat, mat, mat) + (vec,) * 8,
        check_vma=False,
    )
```

```python
import functools
import math
from types import SimpleNamespace

import jax
import jax.numpy as jnp
from jax import lax
from jax.experimental import pallas as pl
from jax.experimental.pallas import tpu as pltpu
from jax.sharding import PartitionSpec as P

HEADS = 12
HEAD = 64
EPS = 1e-12
FLOOR = -1e30
MESH = pl.DeviceIdType.MESH
BF = jnp.bfloat16
F32 = jnp.float32

OUTB, DOWNB, GAIN1, SHIFT1, GAIN2, SHIFT2, QVB = range(7)
UPB, LEN = 8, 12
VROWS = 16
GROWS = 8

ALL = (0, 1, 2, 3)
SCHEDULE = dict(
    early=(),
    norm=(
        (1, "up", 0), (1, "up", 1), (1, "up", 2), (1, "up", 3),
    ),
    sent=(),
    down=(
        (1, "down", 0), (1, "down", 1), (1, "down", 2), (1, "down", 3), (2, "down", 0), (2, "down", 1),
        (2, "down", 2), (2, "down", 3),
    ),
    sent0=(
        (3, "down", 0),
    ),
    sent1=(
        (3, "down", 1),
    ),
    sent2=(
        (3, "down", 2),
    ),
    sent3=(
        (3, "down", 3),
    ),
    arrived=(
        (2, "up", 0), (4, "down", 0), (5, "down", 0),
    ),
    between=(
        (4, "down", 1), (5, "down", 1), (2, "up", 1),
    ),
    after=(
        (4, "down", 2), (5, "down", 2), (3, "up", 0), (2, "up", 2),
    ),
    part=(),
    dq1=(),
    dq2=(),
    dq3=(),
    out=(
        (1, "out", 0), (6, "down", 0), (3, "up", 1), (2, "up", 3),
    ),
    wait0=(
        (4, "down", 3), (4, "up", 0), (3, "up", 2),
    ),
    wait1=(
        (6, "down", 1), (5, "down", 3), (4, "up", 1), (3, "up", 3),
    ),
    wait2=(),
    wait3=(
        (5, "up", 0),
    ),
    qkv=(
        (1, "qkv", 0), (1, "qkv", 1), (1, "qkv", 2), (1, "qkv", 3), (6, "down", 2), (6, "down", 3),
        (6, "up", 0), (4, "up", 2), (4, "up", 3), (2, "qkv", 0), (2, "out", 0),
    ),
    tail=(
        (5, "up", 1), (3, "qkv", 0), (0, "tokens", 0), (3, "out", 0), (2, "qkv", 1), (6, "up", 1),
        (0, "vectors", 0), (5, "up", 2), (4, "qkv", 0), (4, "out", 0), (1, "tokens", 0), (3, "qkv", 1),
        (2, "qkv", 2), (6, "up", 2), (1, "vectors", 0), (5, "out", 0), (5, "up", 3), (4, "qkv", 1),
        (2, "vectors", 0), (3, "qkv", 2), (2, "qkv", 3), (6, "out", 0), (3, "vectors", 0), (6, "up", 3),
        (4, "qkv", 2), (3, "qkv", 3), (4, "vectors", 0), (4, "qkv", 3),
    ),
)


def dot(a, b):
    return lax.dot_general(a, b, (((1,), (0,)), ((), ())), preferred_element_type=F32)


def dot_nt(a, b):
    return lax.dot_general(a, b, (((1,), (1,)), ((), ())), preferred_element_type=F32)


def dot_tn(a, b):
    return lax.dot_general(a, b, (((0,), (0,)), ((), ())), preferred_element_type=F32)


def norm_stats(v):
    center = v - jnp.mean(v, -1, keepdims=True)
    rstd = lax.rsqrt(jnp.mean(center * center, -1, keepdims=True) + EPS)
    return center * rstd, rstd


def norm_back(dy, normed, rstd, gain):
    dn = dy * gain
    return rstd * (
        dn - jnp.mean(dn, -1, keepdims=True) - normed * jnp.mean(dn * normed, -1, keepdims=True)
    )


def col_sum(v):
    return jnp.sum(v, 0, keepdims=True)


def make_plan(cfg):
    C, W, B, D, FW, DW, DP, KVW, MW, R = (
        cfg.C, cfg.W, cfg.B, cfg.D, cfg.FW, cfg.DW, cfg.DP, cfg.KVW, cfg.MW, cfg.R)
    V = pltpu.VMEM
    dma = pltpu.SemaphoreType.DMA
    Q, HB = W * B, B // 2
    plan = dict(
        Xall=V((W, B, D), BF), Wc=V((D, MW), BF), Wq=V((DW, 3 * D), BF), Ws=V((W, DW, MW), BF), Vv=V((W, VROWS, DW), F32),
        Vs=V((8, D), F32), Out=V((W, DW, D), BF), Upc=V((D, FW), BF), Dn=V((FW, D), BF), UpT=V((FW, D), BF), DnT=V((D, FW), BF),
        OutT=V((D, D), BF), WcT=V((MW, D), BF), Cot=V((B, D), BF),
        KVs=V((W, B, KVW), BF), Qs=V((W, HB, KVW), BF), Rq=V((W, HB, KVW), BF), wide=V((B, DP), BF), KV=V((R * Q, KVW), BF),
        Qm=V((cfg.HW, Q, DP), BF), Dm=V((cfg.HW, Q, DP), BF),
        mrow=V((8, Q), F32), lrow=V((8, Q), F32), bias=V((8, MW), F32), upb=V((8, cfg.FW), F32), drow=V((8, Q), F32), OT=V((DW, Q), F32), dQT=V((DW, Q), F32),
        Os=V((W, HB, KVW), BF), Mix=V((W, HB, KVW), BF), MixT=V((W, HB, KVW), BF), mixed=V((B, D), BF),
        Mt=V((W, B, DW), BF),
        N1f=V((B, D), F32), n1=V((B, D), F32), n2=V((B, D), F32), r1=V((B, 1), F32),
        N1all=V((W, B, D), BF), Hp=V((W, B, FW), F32), Gs=V((W, B, FW), BF),
        Fs=V((W, B, D), BF), Fr=V((3, B, D), BF), dR2=V((B, D), F32), dFall=V((W, B, D), BF),
        dHs=V((W, B, FW), BF), dNs=V((W, B, D), BF), dNr=V((3, B, D), BF), dR1=V((B, D), F32),
        dAall=V((W, B, D), BF), dOs=V((W, HB, KVW), BF), dOr=V((W, HB, KVW), BF),
        dKVf=V((Q, KVW), F32), dKVs=V((R - 1, Q, KVW), BF), dKVr=V((R - 1, Q, KVW), BF),
        dKVo=V((W, B, KVW), BF), dQs=V((W, HB, KVW), BF), dQr=V((W, HB, KVW), BF), dqr=V((W, B, MW), BF), dxs=V((W, B, D), BF), dxr=V((3, B, D), BF),
        gv=V((GROWS, D), F32),
    )
    sems = dict(
        x=4, wq=4, wf=12, vv=4, ow=4, uw=4, own=6,
        q=W, kv=W, kf=(R - 1) * W, o=W, mt=4, n=8, f=6, df=8, dn=6, da=4, do=W, dkv=R - 1, dq=W, dk=W, dx=4,
    )
    recvs = dict(sems, kf=R * W)
    if cfg.keep:
        plan["Pm"] = V((cfg.HW, R * Q, Q), F32)
    if cfg.fused:
        plan.update(GX=V((W, B, FW), BF), DX=V((W, B, D // 2), BF))
        sems.update(gx=6, fx=4)
        recvs.update(gx=6, fx=4)
        for name, (pieces, ch, cols, to_rows) in cfg.grads.items():
            plan["G" + name] = V((pieces, 2, ch, cols) if name == "down" else (pieces, 2, 2, ch, cols), BF)
            plan["X" + name] = V((pieces, 3, ch, cols), BF)
            plan["T" + name] = V((pieces, ch, cols), BF)
            plan["Y" + name] = V((pieces, ch, cols), BF)
            plan["U" + name] = V((pieces, ch, cols), BF)
            plan["Z" + name] = V((pieces, ch, cols), BF)
            for kind in ("g1", "g2", "g3", "g4", "g5", "g6"):
                sems[kind + name] = 3 * pieces
                recvs[kind + name] = 3 * pieces
            if to_rows:
                plan["R" + name] = V((pieces, ch, cols), BF)
        plan.update(Va=V((4, GROWS, D), F32), Vb=V((3, GROWS, D), F32), Vt=V((W, GROWS, DW), F32),
                    Vw=V((W, GROWS, DW), F32))
        sems.update(v1=3, vw=W)
        recvs.update(v1=3, vw=W)
    for name, n in sems.items():
        plan["s_" + name] = dma((n,))
    for name, n in recvs.items():
        plan["r_" + name] = dma((n,))
    return plan


class Sums:
    def __init__(self, cfg, m, c, w, send, arrive):
        self.cfg, self.m, self.c, self.w, self.send, self.arrive = cfg, m, c, w, send, arrive
        self.x, self.near = lax.rem(c, 2), lax.rem(lax.div(c, 2), 2)
        self.partners = [(jnp.bitwise_xor(c, k), w) for k in (1, 2, 4, 3)]
        self.long = (self.one, self.two, self.three, self.four, self.five, self.six, self.seven)
        self.halved = (self.nothing, self.pass_on, self.join) + self.long[3:]
        self.short = (self.quarters, self.quarters_sum, self.four, self.spread, self.spread_end)

    def stages(self, name):
        if name == "down":
            return self.halved
        return self.long if name in ("up", "down", "out") else self.short

    def step(self, k, name, p):
        if self.cfg.fused:
            self.stages(name)[k - 1](name, p)

    def run(self, place, others=None):
        if not self.cfg.fused:
            return
        for k, name, p in SCHEDULE[place]:
            if name in self.cfg.grads:
                self.step(k, name, p)
            else:
                others[name][k]()

    def finish(self):
        for name in ("down", "up", "out", "qkv"):
            for p in range(self.cfg.grads[name][0]):
                self.step(len(self.stages(name)), name, p)

    def ref(self, kind, name):
        return getattr(self.m, kind + name)

    def go(self, kind, name, p, src, dst, dev):
        self.send(src, dst, self.ref("s_" + kind, name).at[p], self.ref("r_" + kind, name).at[p], dev)

    def got(self, kind, name, p, dst):
        self.arrive(dst, self.ref("r_" + kind, name).at[p])

    def piece(self, name, k):
        return jnp.bitwise_xor(self.w, k) if self.cfg.grads[name][3] else k

    def nothing(self, name, k):
        pass

    def pass_on(self, name, k):
        g = self.ref("G", name).at[k, 1 - self.near]
        self.go("g2", name, k, g, self.ref("Y", name).at[k], self.partners[1])

    def join(self, name, k):
        y, u = self.ref("Y", name), self.ref("U", name)
        self.got("g2", name, k, y.at[k])
        u[k] = (self.ref("G", name)[k, self.near].astype(F32) + y[k].astype(F32)).astype(BF)
        self.go("g3", name, k, u.at[k], self.ref("Z", name).at[k], self.partners[2])

    def one(self, name, k):
        p = self.piece(name, k)
        self.go("g1", name, k, self.ref("G", name).at[p, 1 - self.x], self.ref("X", name).at[k, pl.ds(0, 2)],
                self.partners[0])

    def two(self, name, k):
        g, other, t = self.ref("G", name), self.ref("X", name), self.ref("T", name)
        self.got("g1", name, k, other.at[k, pl.ds(0, 2)])
        far = 1 - self.near
        mine = g[self.piece(name, k), self.x, far].astype(F32)
        t[k] = (mine + other[k, far].astype(F32)).astype(BF)
        self.go("g2", name, k, t.at[k], self.ref("Y", name).at[k], self.partners[1])

    def three(self, name, k):
        g, other, y, u = (self.ref(kind, name) for kind in "GXYU")
        self.got("g2", name, k, y.at[k])
        n = self.near
        mine = g[self.piece(name, k), self.x, n].astype(F32)
        u[k] = (mine + other[k, n].astype(F32) + y[k].astype(F32)).astype(BF)
        self.go("g3", name, k, u.at[k], self.ref("Z", name).at[k], self.partners[2])

    def four(self, name, k):
        u, z, fin = (self.ref(kind, name) for kind in "UZF")
        self.got("g3", name, k, z.at[k])
        total = (u[k].astype(F32) + z[k].astype(F32)).astype(BF)
        if not self.cfg.grads[name][3] or k == 0:
            fin[self.piece(name, k), self.x, self.near] = total
            return
        done = self.ref("R", name)
        done[k] = total
        self.go("g4", name, k, done.at[k], fin.at[self.w, self.x, self.near], (self.c, jnp.bitwise_xor(self.w, k)))

    def owned(self, name, k):
        here = self.ref("F", name).at[self.piece(name, k), self.x, self.near]
        if self.cfg.grads[name][3] and k > 0:
            self.got("g4", name, k, here)
        return here

    def five(self, name, k):
        here = self.owned(name, k)
        self.go("g5", name, k, here, here, self.partners[1])

    def six(self, name, k):
        fin, p = self.ref("F", name), self.piece(name, k)
        self.got("g5", name, k, fin.at[p, self.x, 1 - self.near])
        self.go("g6", name, k, fin.at[p, self.x], fin.at[p, self.x], self.partners[0])

    def seven(self, name, k):
        self.got("g6", name, k, self.ref("F", name).at[self.piece(name, k), 1 - self.x])

    def three_others(self):
        x, n = self.x, self.near
        return ((1 - x, n, self.partners[0]), (x, 1 - n, self.partners[1]), (1 - x, 1 - n, self.partners[3]))

    def quarters(self, name, k):
        p = self.piece(name, k)
        for i, (x, n, dev) in enumerate(self.three_others()):
            self.go("g1", name, 3 * k + i, self.ref("G", name).at[p, x, n], self.ref("X", name).at[k, i], dev)

    def quarters_sum(self, name, k):
        total = self.ref("G", name)[self.piece(name, k), self.x, self.near].astype(F32)
        for i in range(3):
            other = self.ref("X", name).at[k, i]
            self.got("g1", name, 3 * k + i, other)
            total = total + other[...].astype(F32)
        u = self.ref("U", name)
        u[k] = total.astype(BF)
        self.go("g3", name, k, u.at[k], self.ref("Z", name).at[k], self.partners[2])

    def spread(self, name, k):
        here = self.owned(name, k)
        for i, (_, _, dev) in enumerate(self.three_others()):
            self.go("g5", name, 3 * k + i, here, here, dev)

    def spread_end(self, name, k):
        p = self.piece(name, k)
        for i, (x, n, _) in enumerate(self.three_others()):
            self.got("g5", name, 3 * k + i, self.ref("F", name).at[p, x, n])


def layer_kernel(cfg, names, n_in, *refs):
    (x_ref, cot_ref, qkv_ref, out_ref, up_ref, down_ref, len_ref, *vec_refs) = refs[:n_in]
    y_ref, gx_ref, gqkv_ref, gout_ref, gup_ref, gdown_ref, gvec_ref = refs[n_in : n_in + 7]
    m = SimpleNamespace(**dict(zip(names, refs[n_in + 7 :])))
    if cfg.fused:
        m.Fqkv, m.Fout, m.Fup, m.Fdown = gqkv_ref, gout_ref, gup_ref, gdown_ref
    C, W, B, D, DW, DP, KVW, MW, R, HW = (
        cfg.C, cfg.W, cfg.B, cfg.D, cfg.DW, cfg.DP, cfg.KVW, cfg.MW, cfg.R, cfg.HW)
    OFF = DP - DW
    Q, HB = W * B, B // 2
    c = lax.axis_index("ctx")
    w = lax.axis_index("wa")
    block_part = lax.rem(c, R)
    block_slot = lax.div(c, R)
    s = lax.div(c, R)
    low = lax.rem(c, R)
    g_att = lax.div(w, 2) * 2 + lax.rem(low, 2)
    r_att = lax.div(low, 2) * 2 + lax.rem(w, 2)

    def att_device(t, g, r):
        return (t * R + lax.div(r, 2) * 2 + lax.rem(g, 2), lax.div(g, 2) * 2 + lax.rem(r, 2))

    def is_me(dev):
        return jnp.logical_and(dev[0] == c, dev[1] == w)

    drains = []

    def remote(src, dst, ss, rs, dev):
        return pltpu.make_async_remote_copy(
            src_ref=src, dst_ref=dst, send_sem=ss, recv_sem=rs, device_id=dev, device_id_type=MESH)

    def send(src, dst, ss, rs, dev, pred=None):
        def go():
            remote(src, dst, ss, rs, dev).start()

        def end():
            remote(src, dst, ss, rs, dev).wait_send()

        if pred is None:
            go()
        else:
            pl.when(pred)(go)
        drains.append((pred, end))

    def arrive(dst, rs, pred=None):
        def go():
            remote(dst, dst, rs, rs, (c, w)).wait_recv()

        if pred is None:
            go()
        else:
            pl.when(pred)(go)

    barrier = pltpu.get_barrier_semaphore()

    def greet(i, carry):
        ci, wi = lax.div(i, W), lax.rem(i, W)

        @pl.when(jnp.logical_not(is_me((ci, wi))))
        def _():
            pl.semaphore_signal(barrier, inc=1, device_id=(ci, wi), device_id_type=MESH)

        return carry

    lax.fori_loop(0, C * W, greet, 0)

    def entered():
        pl.semaphore_wait(barrier, C * W - 1)

    def peer(k):
        return (c, jnp.bitwise_xor(w, k))

    def gather_start(buf, ss, rs, parts=1):
        n = buf.shape[1] // parts
        for h in range(parts):
            rows = buf.at[w, pl.ds(h * n, n)]
            send(rows, rows, ss.at[2 * parts + h], rs.at[2 * parts + h], peer(2))
        send(buf.at[w], buf.at[w], ss.at[1], rs.at[1], peer(1))

    def gather_wait(buf, ss, rs, k, h=0, parts=1):
        n = buf.shape[1] // parts
        t = jnp.bitwise_xor(w, k)
        if k == 1:
            arrive(buf.at[t], rs.at[1])
            return
        rows = buf.at[t, pl.ds(h * n, n)]
        arrive(rows, rs.at[k * parts + h])
        if k == 2:
            send(rows, rows, ss.at[3 * parts + h], rs.at[3 * parts + h], peer(1))

    def take(ref, blocks):
        parts = [ref[t, rows, :] for t, rows in blocks]
        return jnp.concatenate(parts, 0) if len(parts) > 1 else parts[0]

    def put(ref, blocks, value):
        n = value.shape[0] // len(blocks)
        for i, (t, rows) in enumerate(blocks):
            ref[t, rows, :] = value[i * n : (i + 1) * n].astype(ref.dtype)

    def feed(buf, sems, work, part, stage, recv, sum_sems, idle, early=None, late=None):
        (ss, rs), (ss2, rs2) = sems, sum_sems
        t3, t2, t1 = (jnp.bitwise_xor(w, k) for k in (3, 2, 1))
        every = pl.ds(0, B)
        halves = [pl.ds(h * HB, HB) for h in range(2)]
        mine = [None, None]

        def across(h):
            rows = halves[h]
            arrive(recv.at[1, rows], rs2.at[2 + h])
            stage[t2, rows, :] = (mine[h] + recv[1, rows, :].astype(F32)).astype(BF)
            send(stage.at[t2, rows], recv.at[2, rows], ss2.at[4 + h], rs2.at[4 + h], peer(2))

        gather_start(buf, ss, rs, 2)
        work([(w, every)])
        gather_wait(buf, ss, rs, 1, 0, 2)
        work([(t1, every)])
        idle()
        for h, rows in enumerate(halves):
            gather_wait(buf, ss, rs, 2, h, 2)
            if h:
                across(0)
            gather_wait(buf, ss, rs, 3, h, 2)
            work([(t3, rows), (t2, rows)])
            both = part([(t3, rows), (t2, rows)])
            stage[t3, rows, :] = both[0:HB].astype(BF)
            send(stage.at[t3, rows], recv.at[1, rows], ss2.at[2 + h], rs2.at[2 + h], peer(1))
            mine[h] = both[HB:]
        stage[t1] = part([(t1, every)]).astype(BF)
        send(stage.at[t1], recv.at[0], ss2.at[0], rs2.at[0], peer(1))
        if early:
            early()
        across(1)
        own = part([(w, every)])
        arrive(recv.at[0], rs2.at[0])
        own = own + recv[0].astype(F32)
        if late:
            late()
        for h, rows in enumerate(halves):
            arrive(recv.at[2, rows], rs2.at[4 + h])
        return own + recv[2].astype(F32)

    def scatter_steps(part, stage, recv, ss, rs):
        t3, t2, t1 = (jnp.bitwise_xor(w, k) for k in (3, 2, 1))

        def first():
            stage[t3] = part(t3).astype(BF)
            send(stage.at[t3], recv.at[1], ss.at[1], rs.at[1], peer(1))
            stage[t1] = part(t1).astype(BF)
            send(stage.at[t1], recv.at[0], ss.at[0], rs.at[0], peer(1))

        def second():
            mine2 = part(t2)
            arrive(recv.at[1], rs.at[1])
            stage[t2] = (mine2 + recv[1].astype(F32)).astype(BF)
            send(stage.at[t2], recv.at[2], ss.at[2], rs.at[2], peer(2))

        def third():
            own = part(w)
            arrive(recv.at[0], rs.at[0])
            own = own + recv[0].astype(F32)
            arrive(recv.at[2], rs.at[2])
            return own + recv[2].astype(F32)

        return first, second, third

    def pack(ref, value):
        ref[:, 0:DW] = value[0:HB].astype(BF)
        ref[:, DW:KVW] = value[HB:B].astype(BF)

    def unpack(ref, lane, packed):
        ref[0:HB, lane : lane + DW] = packed[:, 0:DW]
        ref[HB:B, lane : lane + DW] = packed[:, DW:KVW]

    def local(src, dst, sem):
        cp = pltpu.make_async_copy(src, dst, sem)
        cp.start()
        return cp

    rows_w = pl.ds(w * DW, DW)
    own = [
        local(qkv_ref, m.Wq, m.s_own.at[0]),
        local(x_ref, m.Xall.at[w], m.s_own.at[1]),
        local(out_ref, m.Out.at[w], m.s_own.at[2]),
        local(up_ref.at[:, pl.ds(pl.multiple_of(w * cfg.FW, cfg.FW), cfg.FW)], m.Upc.at[rows_w], m.s_own.at[3]),
        local(down_ref, m.Dn, m.s_own.at[4]),
        local(cot_ref, m.Cot, m.s_own.at[5]),
    ]
    own[0].wait()
    for g in range(W):
        for i, third in enumerate((1, 2, 0)):
            a = third * D + g * DW
            m.Ws[g, :, i * DW : (i + 1) * DW] = m.Wq[:, a : a + DW]
        m.Ws[g, :, 3 * DW : MW] = jnp.zeros((DW, MW - 3 * DW), BF)
    row = 0
    for ref in vec_refs:
        v = ref[...].astype(F32)
        for i in range(v.shape[0] // DW):
            m.Vv[w, row : row + 1, :] = v[i * DW : (i + 1) * DW].reshape(1, DW)
            row += 1
    m.Vv[w, row:VROWS, :] = jnp.full((VROWS - row, DW), len_ref[0].astype(F32))
    own[1].wait()
    entered()

    def part_rows(t, part, parts):
        return pl.ds(pl.multiple_of(t * DW + part * (DW // parts), 16), DW // parts)

    quarter = lax.rem(c, 4)

    def near_me(k):
        return (jnp.bitwise_xor(c, k), w)

    for k in (2, 3):
        send(m.Ws.at[jnp.bitwise_xor(w, k), part_rows(0, quarter, 4)], m.Wc.at[part_rows(w, quarter, 4)],
             m.s_wq.at[k], m.r_wq.at[k], peer(k))
    gather_start(m.Xall, m.s_x, m.r_x)
    send(m.Ws.at[jnp.bitwise_xor(w, 1)], m.Wc.at[rows_w], m.s_wq.at[1], m.r_wq.at[1], peer(1))
    for k in (2, 3, 1):
        send(m.Vv.at[w], m.Vv.at[w], m.s_vv.at[k], m.r_vv.at[k], peer(k))
    m.Wc[rows_w, :] = m.Ws[w]
    m.wide[...] = jnp.zeros(m.wide.shape, BF)
    m.bias[...] = jnp.zeros(m.bias.shape, F32)
    for cp in own[2:]:
        cp.wait()
    m.DnT[...] = m.Dn[...].T
    for k in (2, 3):
        rows = m.Wc.at[part_rows(jnp.bitwise_xor(w, k), quarter, 4)]
        arrive(rows, m.r_wq.at[k])
        for i in (1, 2, 3):
            e = 3 * (k - 2) + i - 1
            send(rows, rows, m.s_wf.at[e], m.r_wf.at[e], near_me(i))
    for k in (1, 2, 3):
        gather_wait(m.Xall, m.s_x, m.r_x, k)
    arrive(m.Wc.at[pl.ds(jnp.bitwise_xor(w, 1) * DW, DW)], m.r_wq.at[1])
    for k in (1, 2, 3):
        arrive(m.Vv.at[jnp.bitwise_xor(w, k)], m.r_vv.at[k])
    gather_start(m.Out, m.s_ow, m.r_ow)
    for k in (2, 3, 1):
        cols = pl.ds(pl.multiple_of(jnp.bitwise_xor(w, k) * cfg.FW, cfg.FW), cfg.FW)
        send(up_ref.at[:, cols], m.Upc.at[rows_w], m.s_uw.at[k], m.r_uw.at[k], peer(k))
    for k in (2, 3):
        for i in (1, 2, 3):
            e = 3 * (k - 2) + i - 1
            arrive(m.Wc.at[part_rows(jnp.bitwise_xor(w, k), jnp.bitwise_xor(quarter, i), 4)], m.r_wf.at[e])

    for t in range(W):
        m.Vs[0:6, t * DW : (t + 1) * DW] = m.Vv[t, 0:6, :]
        m.upb[0:1, t * DW : (t + 1) * DW] = m.Vv[w, UPB + t : UPB + t + 1, :]
    upper, odd = lax.div(w, 2), lax.rem(w, 2)
    m.bias[0:1, DW : 2 * DW] = m.Vv[W // 2 + upper, pl.ds(QVB + odd, 1), :]
    m.bias[0:1, 2 * DW : 3 * DW] = m.Vv[upper, pl.ds(QVB + odd, 1), :]
    bias = m.bias[0:1, :]

    def vec(row):
        return m.Vs[row : row + 1, :]

    kv_rows = pl.ds(pl.multiple_of(block_part * Q + block_slot * B, B), B)
    order = [lax.rem(s + 1 + k, W) for k in range(W)]
    for k, t in enumerate(order):
        qkv = dot(m.Xall[t], m.Wc[...]) + bias
        m.KVs[t] = qkv[:, 0:KVW].astype(BF)
        pack(m.Qs.at[t], qkv[:, KVW : KVW + DW])
        dev = att_device(t, w, block_part)
        send(m.Qs.at[t], m.Rq.at[block_slot], m.s_q.at[k], m.r_q.at[block_slot], dev, jnp.logical_not(is_me(dev)))
    for k, t in enumerate(order):
        dev = att_device(t, w, block_part)
        send(m.KVs.at[t], m.KV.at[kv_rows], m.s_kv.at[k], m.r_kv.at[block_slot], dev, jnp.logical_not(is_me(dev)))

        @pl.when(is_me(dev))
        def _():
            m.Rq[block_slot] = m.Qs[t]
            m.KV[kv_rows, :] = m.KVs[t]

    lanes = lax.broadcasted_iota(jnp.int32, (1, DP), 1)

    def q_lane(h):
        return jnp.logical_and(lanes >= h * HEAD, lanes < (h + 1) * HEAD)

    def v_lane(h):
        return jnp.logical_and(lanes >= OFF + h * HEAD, lanes < OFF + (h + 1) * HEAD)

    for j in range(W):
        arrive(m.Rq.at[j], m.r_q.at[j], jnp.logical_not(is_me((j * R + r_att, g_att))))
        unpack(m.wide, 0, m.Rq.at[j])
        q = m.wide[...] * jnp.asarray(HEAD**-0.5, BF)
        for h in range(HW):
            m.Qm[h, j * B : (j + 1) * B, :] = jnp.where(q_lane(h), q, jnp.zeros_like(q))

    KC = 2 * B
    PER_SET = Q // KC
    len_s = m.Vv[s, LEN : LEN + 1, 0:1]

    def alive(chunk):
        r, half = lax.div(chunk, PER_SET), lax.rem(chunk, PER_SET)
        row = lax.broadcasted_iota(jnp.int32, (KC, Q), 0)
        later = (row >= B).astype(jnp.int32)
        place = ((2 * half + later) * R + r) * B + row - later * B
        return place.astype(F32) < len_s

    m.mrow[...] = jnp.full(m.mrow.shape, FLOOR, F32)
    m.lrow[...] = jnp.zeros(m.lrow.shape, F32)
    m.OT[...] = jnp.zeros(m.OT.shape, F32)

    def attend(chunk, carry):
        rows = pl.ds(pl.multiple_of(chunk * KC, KC), KC)
        keys = m.KV[rows, 0:DP]
        values_t = m.KV[rows, KVW - DP : KVW].T
        live = alive(chunk)
        for h in range(HW):
            scores = jnp.where(live, dot_nt(keys, m.Qm[h]), FLOOR)
            top = m.mrow[h : h + 1, :]
            new_top = jnp.maximum(top, jnp.max(scores, 0, keepdims=True))
            prob = jnp.exp(scores - new_top)
            factor = jnp.exp(top - new_top)
            m.mrow[h : h + 1, :] = new_top
            m.lrow[h : h + 1, :] = m.lrow[h : h + 1, :] * factor + col_sum(prob)
            a, b = h * HEAD, (h + 1) * HEAD
            m.OT[a:b, :] = m.OT[a:b, :] * factor + dot(values_t[OFF + a : OFF + b, :], prob.astype(BF))
        return carry

    for i in range(PER_SET):
        pair = jnp.bitwise_xor(lax.div(s, 2), i)
        for e in range(2):
            j = 2 * pair + e
            rows = m.KV.at[pl.ds(pl.multiple_of(r_att * Q + j * B, B), B)]
            arrive(rows, m.r_kv.at[j], jnp.logical_not(is_me((j * R + r_att, g_att))))
            for k in range(1, R):
                send(rows, rows, m.s_kf.at[(k - 1) * W + 2 * i + e], m.r_kf.at[r_att * W + j],
                     att_device(s, g_att, lax.rem(r_att + k, R)))
        attend(r_att * PER_SET + pair, 0)
        if i == 0:
            gather_wait(m.Out, m.s_ow, m.r_ow, 2)

        def others(k, carry):
            r = lax.rem(r_att + k, R)
            for e in range(2):
                j = 2 * pair + e
                arrive(m.KV.at[pl.ds(pl.multiple_of(r * Q + j * B, B), B)], m.r_kf.at[r * W + j])
            return attend(r * PER_SET + pair, carry)

        lax.fori_loop(1, R, others, 0)
    for h in range(HW):
        a, b = h * HEAD, (h + 1) * HEAD
        m.OT[a:b, :] = m.OT[a:b, :] / m.lrow[h : h + 1, :]
    m.lrow[0:HW, :] = m.mrow[0:HW, :] + jnp.log(m.lrow[0:HW, :])
    for j in range(W):
        pack(m.Os.at[j], m.OT[:, j * B : (j + 1) * B].T)
        dev = (j * R + r_att, s)
        send(m.Os.at[j], m.Mix.at[g_att], m.s_o.at[j], m.r_o.at[g_att], dev, jnp.logical_not(is_me(dev)))

        @pl.when(is_me(dev))
        def _():
            m.Mix[g_att] = m.Os[j]

    for k in (1, 3):
        gather_wait(m.Out, m.s_ow, m.r_ow, k)
    out_weight = m.Out[...].reshape(D, D)
    resid = m.Xall[w].astype(F32) + vec(OUTB)
    for g in range(W):
        arrive(m.Mix.at[g], m.r_o.at[g], jnp.logical_not(is_me(att_device(w, g, block_part))))
        unpack(m.mixed, g * DW, m.Mix.at[g])
    resid = resid + dot(m.mixed[...], out_weight)
    n1, r1 = norm_stats(resid)
    m.n1[...] = n1
    m.r1[...] = r1
    n1_full = n1 * vec(GAIN1) + vec(SHIFT1)
    m.N1f[...] = n1_full
    m.N1all[w] = n1_full.astype(BF)

    for k in (1, 2, 3):
        arrive(m.Upc.at[pl.ds(jnp.bitwise_xor(w, k) * DW, DW)], m.r_uw.at[k])
    up_bias = m.upb[0:1, :]

    activated = []

    def expand(blocks):
        h = dot(take(m.N1all, blocks), m.Upc[...]) + up_bias
        phi = 0.5 * (1.0 + lax.erf(h * (2.0**-0.5)))
        put(m.Gs, blocks, h * phi)
        put(m.Hp, blocks, phi + h * ((2.0 * math.pi) ** -0.5) * jnp.exp(-0.5 * h * h))
        if cfg.fused:
            for t, rows in blocks:
                i = len(activated)
                activated.append((t, rows))
                send(m.Gs.at[t, rows], m.GX.at[t, rows], m.s_gx.at[i], m.r_gx.at[i], near_me(1))

    def turn_weights():
        m.UpT[...] = m.Upc[...].T
        m.OutT[...] = m.Out[...].reshape(D, D).T

    ffn = feed(m.N1all, (m.s_n, m.r_n), expand, lambda blocks: dot(take(m.Gs, blocks), m.Dn[...]), m.Fs, m.Fr,
               (m.s_f, m.r_f), turn_weights)
    n2, r2 = norm_stats(m.N1f[...] + ffn + vec(DOWNB))
    m.n2[...] = n2
    y_ref[...] = (n2 * vec(GAIN2) + vec(SHIFT2)).astype(BF)

    place = c * B + lax.broadcasted_iota(jnp.int32, (B, D), 0)
    dy = jnp.where(place.astype(F32) < m.Vv[w, LEN : LEN + 1, 0:1], m.Cot[...].astype(F32), 0.0)
    d_r2 = norm_back(dy, n2, r2, vec(GAIN2))
    m.dR2[...] = d_r2
    m.dFall[w] = d_r2.astype(BF)

    def shrink(blocks):
        put(m.dHs, blocks, dot(take(m.dFall, blocks), m.DnT[...]) * take(m.Hp, blocks))

    def flat(ref):
        return ref[...].reshape(Q, ref.shape[-1])

    def put_grad(name, plain, lhs, rhs, parts):
        rows = lhs.shape[-1] // parts
        for i in range(parts):
            val = dot_tn(lhs[:, :, i * rows : (i + 1) * rows].reshape(Q, rows), flat(rhs)).astype(BF)
            if cfg.fused:
                _, ch, cols, _ = cfg.grads[name]
                n = rows // (4 * ch)
                getattr(m, "G" + name)[i * n : (i + 1) * n] = val.reshape(n, 2, 2, ch, cols)
            else:
                plain[i * rows : (i + 1) * rows, :] = val

    pump = Sums(cfg, m, c, w, send, arrive)

    side = lax.rem(c, 2)

    def half_cols(side):
        return pl.ds(pl.multiple_of(side * (D // 2), 128), D // 2)

    def down_half():
        for i, k in enumerate((0, 2)):
            rows = m.DX.at[jnp.bitwise_xor(w, k)]
            arrive(rows, m.r_fx.at[i])
            send(rows, rows, m.s_fx.at[2 + i], m.r_fx.at[2 + i], peer(1))
        for i, (t, rows) in enumerate(activated):
            arrive(m.GX.at[t, rows], m.r_gx.at[i])
        for i, k in enumerate((1, 3)):
            arrive(m.DX.at[jnp.bitwise_xor(w, k)], m.r_fx.at[2 + i])
        pieces, ch, cols, _ = cfg.grads["down"]
        n = cfg.FW // 2
        here = m.dFall[:, :, half_cols(side)].reshape(Q, cols)
        there = flat(m.DX)
        for i in range(2):
            at = slice(i * n, (i + 1) * n)
            val = dot_tn(m.Gs[:, :, at].reshape(Q, n), here) + dot_tn(m.GX[:, :, at].reshape(Q, n), there)
            m.Gdown[i * (pieces // 2) : (i + 1) * (pieces // 2)] = val.astype(BF).reshape(pieces // 2, 2, ch, cols)

    def early():
        if cfg.fused:
            for i, k in enumerate((0, 2)):
                t = jnp.bitwise_xor(w, k)
                send(m.dFall.at[t, :, half_cols(1 - side)], m.DX.at[t], m.s_fx.at[i], m.r_fx.at[i], near_me(1))
        else:
            put_grad("down", gdown_ref, m.Gs, m.dFall, 2)
        pump.run("early")

    def late():
        m.gv[2:3, :] = col_sum(dy * n2)
        m.gv[3:4, :] = col_sum(dy)
        m.gv[5:6, :] = col_sum(m.dFall[w].astype(F32))
        put_grad("up", gup_ref, m.N1all, m.dHs, 2)
        m.gv[6:7, :] = col_sum(flat(m.dHs).astype(F32))
        pump.run("norm")

    def turn_projection():
        m.WcT[...] = m.Wc[...].T

    d_n1 = feed(m.dFall, (m.s_df, m.r_df), shrink, lambda blocks: dot(take(m.dHs, blocks), m.UpT[...]), m.dNs, m.dNr,
                (m.s_dn, m.r_dn), turn_projection, early, late) + m.dR2[...]
    n1 = m.n1[...]
    d_r1 = norm_back(d_n1, n1, m.r1[...], vec(GAIN1))
    m.dR1[...] = d_r1
    d_a = d_r1.astype(BF)
    m.dAall[w] = d_a
    d_mixed = dot(d_a, m.OutT[...])
    for g in range(W):
        pack(m.dOs.at[g], d_mixed[:, g * DW : (g + 1) * DW])
        dev = att_device(w, g, block_part)
        send(m.dOs.at[g], m.dOr.at[block_slot], m.s_do.at[g], m.r_do.at[block_slot], dev,
             jnp.logical_not(is_me(dev)))

        @pl.when(is_me(dev))
        def _():
            m.dOr[block_slot] = m.dOs[g]

    pump.run("sent")
    gather_start(m.dAall, m.s_da, m.r_da)
    for k in (2, 3, 1):
        send(m.Mix.at[jnp.bitwise_xor(w, k)], m.MixT.at[w], m.s_mt.at[k], m.r_mt.at[k], peer(k))
    if cfg.fused:
        down_half()
    pump.run("down")
    m.MixT[w] = m.Mix[w]
    m.gv[0:1, :] = col_sum(d_n1 * n1)
    m.gv[1:2, :] = col_sum(d_n1)
    m.gv[4:5, :] = col_sum(d_a.astype(F32))

    m.wide[...] = jnp.zeros(m.wide.shape, BF)

    def weights_again(chunk, h):
        rows = pl.ds(pl.multiple_of(chunk * KC, KC), KC)
        scores = dot_nt(m.KV[rows, 0:DP], m.Qm[h])
        return jnp.where(alive(chunk), jnp.exp(scores - m.lrow[h : h + 1, :]), 0.0)

    if cfg.keep:

        def keep(chunk, carry):
            for h in range(HW):
                m.Pm[h, pl.ds(pl.multiple_of(chunk * KC, KC), KC), :] = weights_again(chunk, h)
            return carry

        lax.fori_loop(0, R * PER_SET, keep, 0)
    for j in range(W):
        pump.run("sent%d" % j)
        arrive(m.dOr.at[j], m.r_do.at[j], jnp.logical_not(is_me((j * R + r_att, s))))
        unpack(m.wide, OFF, m.dOr.at[j])
        d_o = m.wide[...]
        cols = slice(j * B, (j + 1) * B)
        for h in range(HW):
            m.Dm[h, cols, :] = jnp.where(v_lane(h), d_o, jnp.zeros_like(d_o))
        prod = m.OT[:, cols] * d_o.astype(F32).T[OFF:DP, :]
        for h in range(HW):
            m.drow[h : h + 1, cols] = col_sum(prod[h * HEAD : (h + 1) * HEAD, :])
    m.dQT[...] = jnp.zeros(m.dQT.shape, F32)
    pump.run("arrived")

    def attend_back(step, carry):
        chunk = lax.rem((r_att + 1) * PER_SET + step, R * PER_SET)
        rows = pl.ds(pl.multiple_of(chunk * KC, KC), KC)
        keys = m.KV[rows, 0:DP]
        values = m.KV[rows, KVW - DP : KVW]
        keys_t = keys.T
        d_k = jnp.zeros((KC, DP), F32)
        d_v = jnp.zeros((KC, DP), F32)
        for h in range(HW):
            prob = m.Pm[h, rows, :] if cfg.keep else weights_again(chunk, h)
            d_prob = dot_nt(values, m.Dm[h])
            d_s = (prob * (d_prob - m.drow[h : h + 1, :])).astype(BF)
            d_k = d_k + dot(d_s, m.Qm[h])
            d_v = d_v + dot(prob.astype(BF), m.Dm[h])
            a, b = h * HEAD, (h + 1) * HEAD
            m.dQT[a:b, :] = m.dQT[a:b, :] + dot(keys_t[a:b, :], d_s)
        lead = KVW - DP
        d_kv = jnp.concatenate([d_k[:, 0:lead], d_k[:, lead:] + d_v[:, 0 : DP - lead], d_v[:, DP - lead :]], 1)
        place, part = lax.div(step, PER_SET), lax.rem(step, PER_SET)
        rows = pl.ds(pl.multiple_of(part * KC, KC), KC)
        if carry is None:
            m.dKVf[rows, :] = d_kv
        else:
            m.dKVs[place, rows, :] = d_kv.astype(BF)
        return carry

    lax.fori_loop(0, (R - 1) * PER_SET, attend_back, 0)
    for k in range(1, R):
        send(m.dKVs.at[k - 1], m.dKVr.at[R - k - 1], m.s_dkv.at[k - 1], m.r_dkv.at[R - k - 1],
             att_device(s, g_att, lax.rem(r_att + k, R)))
    pump.run("between")
    lax.fori_loop((R - 1) * PER_SET, R * PER_SET, attend_back, None)
    pump.run("after")
    pump.run("part")
    for k in range(1, R):
        arrive(m.dKVr.at[k - 1], m.r_dkv.at[k - 1])
    for j in range(W):
        d_kv = m.dKVf[j * B : (j + 1) * B, :]
        for k in range(1, R):
            d_kv = d_kv + m.dKVr[k - 1, j * B : (j + 1) * B, :].astype(F32)
        m.dKVo[j] = d_kv.astype(BF)
        pack(m.dQs.at[j], m.dQT[:, j * B : (j + 1) * B].T * (HEAD**-0.5))
        dev = (j * R + r_att, g_att)
        away = jnp.logical_not(is_me(dev))
        send(m.dKVo.at[j], m.dqr.at[s, :, pl.ds(0, KVW)], m.s_dk.at[j], m.r_dk.at[s], dev, away)
        send(m.dQs.at[j], m.dQr.at[s], m.s_dq.at[j], m.r_dq.at[s], dev, away)

        @pl.when(is_me(dev))
        def _():
            m.dqr[s, :, 0:KVW] = m.dKVo[j]
            m.dQr[s] = m.dQs[j]

    for k in (1, 2, 3):
        pump.run("dq%d" % k)
        gather_wait(m.dAall, m.s_da, m.r_da, k)
        arrive(m.MixT.at[jnp.bitwise_xor(w, k)], m.r_mt.at[k])
    for t in range(W):
        unpack(m.Mt.at[t], 0, m.MixT.at[t])
        m.dqr[t, :, KVW + DW : MW] = jnp.zeros((B, MW - KVW - DW), BF)
    put_grad("out", gout_ref, m.Mt, m.dAall, 1)
    pump.run("out")

    for t in range(W):
        pump.run("wait%d" % t)
        away = jnp.logical_not(is_me(att_device(t, w, block_part)))
        arrive(m.dqr.at[t, :, pl.ds(0, KVW)], m.r_dk.at[t], away)
        arrive(m.dQr.at[t], m.r_dq.at[t], away)
        unpack(m.dqr.at[t], KVW, m.dQr.at[t])
    put_grad("qkv", gqkv_ref, m.Xall, m.dqr, 2)
    pump.run("qkv")

    m.gv[7:8, 0:MW] = col_sum(flat(m.dqr).astype(F32))
    m.gv[7:8, MW:D] = jnp.zeros((1, D - MW), F32)

    def d_x(t):
        return dot(m.dqr[t], m.WcT[...])

    token_steps = scatter_steps(d_x, m.dxs, m.dxr, m.s_dx, m.r_dx)

    def vectors(i):
        if i:
            arrive(m.Vb.at[i - 1], m.r_v1.at[i - 1])
            m.Va[i] = m.Va[i - 1] + m.Vb[i - 1]
        else:
            m.Va[0] = m.gv[...]
        if i < 3:
            send(m.Va.at[i], m.Vb.at[i], m.s_v1.at[i], m.r_v1.at[i], pump.partners[i])

    def vectors_to_rows():
        vectors(3)
        total = m.Va[3]
        for t in range(W):
            m.Vt[t, 0:6, :] = total[0:6, t * DW : (t + 1) * DW]
            m.Vt[t, 6:7, :] = total[7:8, 2 * DW : 3 * DW]
            m.Vt[t, 7:8, :] = total[7:8, DW : 2 * DW]
        m.Vw[w] = m.Vt[w]
        for k in (2, 3, 1):
            send(m.Vt.at[jnp.bitwise_xor(w, k)], m.Vw.at[w], m.s_vw.at[k], m.r_vw.at[k], peer(k))
        gvec_ref[7:8, :] = total[6:7, :]

    def vectors_end():
        for k in (1, 2, 3):
            arrive(m.Vw.at[jnp.bitwise_xor(w, k)], m.r_vw.at[k])
        gvec_ref[0:6, 0:DW] = m.Vw[0, 0:6, :] + m.Vw[1, 0:6, :] + m.Vw[2, 0:6, :] + m.Vw[3, 0:6, :]
        for i in range(2):
            gvec_ref[6:7, i * DW : (i + 1) * DW] = m.Vw[2 * odd + i, pl.ds(6 + upper, 1), :]

    steps = [functools.partial(vectors, i) for i in range(3)] + [vectors_to_rows, vectors_end]

    if not cfg.fused:
        for step in token_steps[:-1]:
            step()
        d_x_sum = token_steps[-1]()
        gvec_ref[0] = m.gv[...]
    else:
        vector_steps = [functools.partial(vectors, i) for i in range(3)] + [vectors_to_rows, vectors_end]
        pump.run("tail", dict(tokens=token_steps, vectors=vector_steps))
        pump.finish()
        d_x_sum = token_steps[2]()
    gx_ref[...] = (m.dR1[...] + d_x_sum).astype(BF)

    for pred, end in drains:
        if pred is None:
            end()
        else:
            pl.when(pred)(end)


def body(C, W, tokens, lengths, qkv_weight, out_weight, up_weight, down_weight, qv_bias, out_bias, up_bias,
         down_bias, gain_one, shift_one, gain_two, shift_two, cotangent):
    _, B, D = tokens.shape
    FW = down_weight.shape[0]
    DW = D // W
    DP = -(-DW // 128) * 128
    KVW = 2 * DW
    MW = KVW + DP
    R = C // W
    cfg = SimpleNamespace(C=C, W=W, B=B, D=D, FW=FW, DW=DW, DP=DP, KVW=KVW, MW=MW, R=R, HW=HEADS // W)
    cfg.fused = R == 2 and C == 8 and DW % 64 == 0 and FW % (64 * W) == 0
    cfg.keep = R == 2
    cfg.grads = dict(down=(W, FW // W // 2, D // 2, False), up=(W, DW // 4, FW, True), qkv=(W, DW // 4, MW, True),
                     out=(1, DW // 4, D, False))
    w = lax.axis_index("wa")
    small = (out_bias, down_bias, gain_one, shift_one, gain_two, shift_two, qv_bias, up_bias)

    plan = make_plan(cfg)
    names = list(plan)
    vm = pl.BlockSpec(memory_space=pltpu.VMEM)
    hbm = pl.BlockSpec(memory_space=pl.ANY)
    if cfg.fused:
        outs = [(n, 2, 2, ch, cols) for n, ch, cols, _ in (cfg.grads[k] for k in ("qkv", "out", "up", "down"))]
        place = pltpu.VMEM
    else:
        outs = [(D, MW), (DW, D), (D, FW), (FW, D)]
        place = jax.ShapeDtypeStruct
    outs = [place(a, BF) for a in [(B, D), (B, D)] + outs] + [place((GROWS, D) if cfg.fused else (1, GROWS, D), F32)]
    args = (tokens.reshape(B, D), cotangent.reshape(B, D), qkv_weight, out_weight, up_weight, down_weight, lengths, *small)
    y, gx, gqkv, gout, gup, gdown, gvec = pl.pallas_call(
        functools.partial(layer_kernel, cfg, names, len(args)),
        out_shape=outs,
        in_specs=[hbm] * 6 + [pl.BlockSpec(memory_space=pltpu.SMEM)] + [vm] * len(small),
        out_specs=[vm] * len(outs),
        scratch_shapes=[plan[n] for n in names],
        compiler_params=pltpu.CompilerParams(collective_id=0, has_side_effects=True, vmem_limit_bytes=(52 if cfg.fused else 60) << 20),
        name="layer",
    )(*args)
    if cfg.fused:
        return finish(cfg, y, gx, gqkv, gout, gup, gdown, gvec)

    def to_rows(g):
        g = lax.psum(g, "ctx").reshape(W, DW, g.shape[1])
        return lax.all_to_all(g, "wa", 0, 0, tiled=True).transpose(1, 0, 2).reshape(DW, -1)

    gq = to_rows(gqkv).reshape(DW, W, MW).astype(F32)
    gup = to_rows(gup)
    gout, gdown, gvec = lax.psum((gout, gdown, gvec), "ctx")
    gvec = lax.all_gather(gvec, "wa", axis=0, tiled=True)
    gqkv = jnp.concatenate([gq[:, :, a : a + DW].reshape(DW, D) for a in (KVW, 0, DW)], 1)
    own = lax.dynamic_slice_in_dim(jnp.sum(gvec, 0)[0:6], w * DW, DW, 1)
    g_upb = lax.dynamic_slice_in_dim(gvec, w, 1, 0)[0, 6]
    g_qv = jnp.concatenate([gvec[:, 7, KVW : KVW + DW].reshape(D), gvec[:, 7, DW:KVW].reshape(D)])
    g_qv = lax.dynamic_slice_in_dim(g_qv, w * (2 * D // W), 2 * D // W)
    return (y.reshape(1, B, D), gx.reshape(1, B, D), gqkv, gout.astype(F32), gup.astype(F32),
            gdown.astype(F32), g_qv, own[4], g_upb, own[5], own[0], own[1], own[2], own[3])


def finish_kernel(cfg, y, gx, gqkv, gout, gup, gdown, gvec, o_y, o_gx, o_qkv, o_out, o_up, o_down, o_qv, o_outb, o_upb,
                  o_downb, o_g1, o_s1, o_g2, o_s2):
    W, D, DW, MW, KVW = cfg.W, cfg.D, cfg.DW, cfg.MW, cfg.KVW
    o_y[0] = y[...]
    o_gx[0] = gx[...]
    for g in range(W):
        rows = gqkv[g].reshape(DW, MW).astype(F32)
        for third, a in enumerate((KVW, 0, DW)):
            o_qkv[:, third * D + g * DW : third * D + (g + 1) * DW] = rows[:, a : a + DW]
        o_up[:, g * cfg.FW : (g + 1) * cfg.FW] = gup[g].reshape(DW, cfg.FW).astype(F32)
    o_out[...] = gout[...].reshape(o_out.shape).astype(F32)
    for x in range(2):
        o_down[:, x * (D // 2) : (x + 1) * (D // 2)] = gdown[:, x].reshape(cfg.FW, D // 2).astype(F32)
    o_qv[...] = gvec[6, 0 : 2 * DW]
    o_upb[...] = gvec[7, 0 : cfg.FW]
    for row, ref in enumerate((o_g1, o_s1, o_g2, o_s2, o_outb, o_downb)):
        ref[...] = gvec[row, 0:DW]


def finish(cfg, *arrays):
    B, D, DW, W, FW = cfg.B, cfg.D, cfg.DW, cfg.W, cfg.FW
    shapes = [(1, B, D)] * 2 + [(DW, 3 * D), (DW, D), (DW, W * FW), (FW, D), (2 * DW,), (DW,), (FW,)] + [(DW,)] * 5
    vm = pl.BlockSpec(memory_space=pltpu.VMEM)
    arrays = [pltpu.with_memory_space_constraint(a, pltpu.VMEM) for a in arrays]
    return pl.pallas_call(
        functools.partial(finish_kernel, cfg),
        out_shape=[jax.ShapeDtypeStruct(s, BF if i < 2 else F32) for i, s in enumerate(shapes)],
        in_specs=[vm] * len(arrays),
        out_specs=[vm] * len(shapes),
        compiler_params=pltpu.CompilerParams(vmem_limit_bytes=32 << 20),
        name="results",
    )(*arrays)


def solution(mesh):
    tok, vec, mat = P("wa", "ctx", None), P("wa"), P("wa", None)
    return jax.shard_map(
        functools.partial(body, mesh.shape["ctx"], mesh.shape["wa"]),
        mesh=mesh,
        in_specs=(tok, vec, mat, mat, mat, mat) + (vec,) * 8 + (tok,),
        out_specs=(tok, tok, mat, mat, mat, mat) + (vec,) * 8,
        check_vma=False,
    )
```

```python
import functools
import math
from types import SimpleNamespace

import jax
import jax.numpy as jnp
from jax import lax
from jax.experimental import pallas as pl
from jax.experimental.pallas import tpu as pltpu
from jax.sharding import PartitionSpec as P

HEADS = 12
HEAD = 64
EPS = 1e-12
FLOOR = -1e30
MESH = pl.DeviceIdType.MESH
BF = jnp.bfloat16
F32 = jnp.float32

OUTB, DOWNB, GAIN1, SHIFT1, GAIN2, SHIFT2, QVB = range(7)
UPB, LEN = 8, 12
VROWS = 16
GROWS = 8

ALL = (0, 1, 2, 3)
SCHEDULE = dict(
    early=(),
    norm=(),
    sent=(
        (1, "up", 0), (1, "up", 1), (1, "up", 2), (1, "up", 3),
    ),
    down=(
        (1, "down", 0), (1, "down", 1), (1, "down", 2), (1, "down", 3), (2, "down", 0), (2, "down", 1),
        (2, "down", 2), (2, "down", 3),
    ),
    sent0=(
        (3, "down", 0),
    ),
    sent1=(),
    sent2=(),
    sent3=(
        (4, "down", 0),
    ),
    arrived=(
        (5, "down", 0), (3, "down", 1), (2, "up", 0),
    ),
    between=(
        (3, "down", 2), (2, "up", 1),
    ),
    after=(
        (4, "down", 1), (3, "down", 3), (3, "up", 0), (2, "up", 2),
    ),
    part=(),
    dq1=(),
    dq2=(),
    dq3=(
        (6, "down", 0),
    ),
    out=(
        (1, "out", 0), (5, "down", 1), (4, "down", 2), (3, "up", 1), (2, "up", 3),
    ),
    wait0=(
        (5, "down", 2), (4, "down", 3), (4, "up", 0), (3, "up", 2),
    ),
    wait1=(
        (6, "down", 1), (5, "down", 3), (4, "up", 1), (3, "up", 3),
    ),
    wait2=(),
    wait3=(
        (5, "up", 0),
    ),
    qkv=(
        (1, "qkv", 0), (1, "qkv", 1), (1, "qkv", 2), (1, "qkv", 3), (6, "down", 2), (6, "up", 0),
        (4, "up", 2), (4, "up", 3), (2, "qkv", 0), (2, "out", 0),
    ),
    tail=(
        (6, "down", 3), (5, "up", 1), (3, "qkv", 0), (0, "tokens", 0), (3, "out", 0), (2, "qkv", 1),
        (6, "up", 1), (0, "vectors", 0), (5, "up", 2), (4, "qkv", 0), (4, "out", 0), (1, "tokens", 0),
        (3, "qkv", 1), (2, "qkv", 2), (6, "up", 2), (1, "vectors", 0), (5, "out", 0), (5, "up", 3),
        (4, "qkv", 1), (2, "vectors", 0), (3, "qkv", 2), (2, "qkv", 3), (6, "out", 0), (3, "vectors", 0),
        (6, "up", 3), (4, "qkv", 2), (3, "qkv", 3), (4, "vectors", 0), (4, "qkv", 3),
    ),
)


def dot(a, b):
    return lax.dot_general(a, b, (((1,), (0,)), ((), ())), preferred_element_type=F32)


def dot_nt(a, b):
    return lax.dot_general(a, b, (((1,), (1,)), ((), ())), preferred_element_type=F32)


def dot_tn(a, b):
    return lax.dot_general(a, b, (((0,), (0,)), ((), ())), preferred_element_type=F32)


def norm_stats(v):
    center = v - jnp.mean(v, -1, keepdims=True)
    rstd = lax.rsqrt(jnp.mean(center * center, -1, keepdims=True) + EPS)
    return center * rstd, rstd


def norm_back(dy, normed, rstd, gain):
    dn = dy * gain
    return rstd * (
        dn - jnp.mean(dn, -1, keepdims=True) - normed * jnp.mean(dn * normed, -1, keepdims=True)
    )


def col_sum(v):
    return jnp.sum(v, 0, keepdims=True)


def make_plan(cfg):
    C, W, B, D, FW, DW, DP, KVW, MW, R = (
        cfg.C, cfg.W, cfg.B, cfg.D, cfg.FW, cfg.DW, cfg.DP, cfg.KVW, cfg.MW, cfg.R)
    V = pltpu.VMEM
    dma = pltpu.SemaphoreType.DMA
    Q, HB = W * B, B // 2
    plan = dict(
        Xall=V((W, B, D), BF), Wc=V((D, MW), BF), Wq=V((DW, 3 * D), BF), Ws=V((W, DW, MW), BF), Vv=V((W, VROWS, DW), F32),
        Vs=V((8, D), F32), Out=V((W, DW, D), BF), Upc=V((D, FW), BF), Dn=V((FW, D), BF), UpT=V((FW, D), BF), DnT=V((D, FW), BF),
        OutT=V((D, D), BF), WcT=V((MW, D), BF), Cot=V((B, D), BF),
        KVs=V((W, B, KVW), BF), Qs=V((W, HB, KVW), BF), Rq=V((W, HB, KVW), BF), wide=V((B, DP), BF), KV=V((R * Q, KVW), BF),
        Qm=V((cfg.HW, Q, DP), BF), Dm=V((cfg.HW, Q, DP), BF),
        mrow=V((8, Q), F32), lrow=V((8, Q), F32), bias=V((8, MW), F32), upb=V((8, cfg.FW), F32), drow=V((8, Q), F32), OT=V((DW, Q), F32), dQT=V((DW, Q), F32),
        Os=V((W, HB, KVW), BF), Mix=V((W, HB, KVW), BF), MixT=V((W, HB, KVW), BF), mixed=V((B, D), BF),
        Mt=V((W, B, DW), BF),
        N1f=V((B, D), F32), n1=V((B, D), F32), n2=V((B, D), F32), r1=V((B, 1), F32),
        N1all=V((W, B, D), BF), Hp=V((W, B, FW), F32), Gs=V((W, B, FW), BF),
        Fs=V((W, B, D), BF), Fr=V((3, B, D), BF), dR2=V((B, D), F32), dFall=V((W, B, D), BF),
        dHs=V((W, B, FW), BF), dNs=V((W, B, D), BF), dNr=V((3, B, D), BF), dR1=V((B, D), F32),
        dAall=V((W, B, D), BF), dOs=V((W, HB, KVW), BF), dOr=V((W, HB, KVW), BF),
        dKVf=V((Q, KVW), F32), dKVs=V((R - 1, Q, KVW), BF), dKVr=V((R - 1, Q, KVW), BF),
        dKVo=V((W, B, KVW), BF), dQs=V((W, HB, KVW), BF), dQr=V((W, HB, KVW), BF), dqr=V((W, B, MW), BF), dxs=V((W, B, D), BF), dxr=V((3, B, D), BF),
        gv=V((GROWS, D), F32),
    )
    sems = dict(
        x=4, wq=4, wf=12, vv=4, ow=4, uw=4, own=6,
        q=W, kv=W, kf=(R - 1) * W, o=W, mt=4, n=8, f=6, df=8, dn=6, da=4, do=W, dkv=R - 1, dq=W, dk=W, dx=4,
    )
    recvs = dict(sems, kf=R * W)
    if cfg.keep:
        plan["Pm"] = V((cfg.HW, R * Q, Q), F32)
    if cfg.fused:
        plan.update(GX=V((W, B, FW), BF), DX=V((W, B, D // 2), BF))
        sems.update(gx=6, fx=4)
        recvs.update(gx=6, fx=4)
        for name, (pieces, ch, cols, to_rows) in cfg.grads.items():
            plan["G" + name] = V((pieces, 2, ch, cols) if name == "down" else (pieces, 2, 2, ch, cols), BF)
            plan["X" + name] = V((pieces, 3, ch, cols), BF)
            plan["T" + name] = V((pieces, 2, ch, cols), BF)
            plan["Y" + name] = V((pieces, 2, ch, cols), BF)
            plan["U" + name] = V((pieces, 2, ch, cols), BF)
            plan["Z" + name] = V((pieces, 2, ch, cols), BF)
            for kind in ("g1", "g2", "g3", "g4", "g5", "g6"):
                sems[kind + name] = 3 * pieces
                recvs[kind + name] = 3 * pieces
            if to_rows:
                plan["R" + name] = V((pieces, 2, ch, cols), BF)
        plan.update(Va=V((4, GROWS, D), F32), Vb=V((3, GROWS, D), F32), Vt=V((W, GROWS, DW), F32),
                    Vw=V((W, GROWS, DW), F32))
        sems.update(v1=3, vw=W)
        recvs.update(v1=3, vw=W)
    for name, n in sems.items():
        plan["s_" + name] = dma((n,))
    for name, n in recvs.items():
        plan["r_" + name] = dma((n,))
    return plan


class Sums:
    def __init__(self, cfg, m, c, w, send, arrive):
        self.cfg, self.m, self.c, self.w, self.send, self.arrive = cfg, m, c, w, send, arrive
        self.x, self.near = lax.rem(c, 2), lax.rem(lax.div(c, 2), 2)
        self.partners = [(jnp.bitwise_xor(c, k), w) for k in (1, 2, 4, 3)]
        self.other_middle = (jnp.bitwise_xor(c, 6), w)
        self.middle = self.near != lax.div(c, 4)
        self.end = jnp.logical_not(self.middle)
        self.long = (self.one, self.two, self.three, self.four, self.five, self.six, self.seven)
        self.halved = (self.nothing,) + self.long[1:]
        self.short = (self.quarters, self.quarters_sum, self.quarters_total, self.spread, self.spread_end)

    def stages(self, name):
        if name == "down":
            return self.halved
        return self.long if name in ("up", "down", "out") else self.short

    def step(self, k, name, p):
        if self.cfg.fused:
            self.stages(name)[k - 1](name, p)

    def run(self, place, others=None):
        if not self.cfg.fused:
            return
        for k, name, p in SCHEDULE[place]:
            if name in self.cfg.grads:
                self.step(k, name, p)
            else:
                others[name][k]()

    def finish(self):
        for name in ("down", "up", "out", "qkv"):
            for p in range(self.cfg.grads[name][0]):
                self.step(len(self.stages(name)), name, p)

    def ref(self, kind, name):
        return getattr(self.m, kind + name)

    def go(self, kind, name, p, src, dst, dev, pred=None):
        self.send(src, dst, self.ref("s_" + kind, name).at[p], self.ref("r_" + kind, name).at[p], dev, pred)

    def got(self, kind, name, p, dst, pred=None):
        self.arrive(dst, self.ref("r_" + kind, name).at[p], pred)

    def piece(self, name, k):
        return jnp.bitwise_xor(self.w, k) if self.cfg.grads[name][3] else k

    def nothing(self, name, k):
        pass

    def half(self, name, k):
        if name == "down":
            return self.ref("G", name)[k].astype(F32)
        other = self.ref("X", name).at[k, pl.ds(0, 2)]
        self.got("g1", name, k, other)
        return self.ref("G", name)[self.piece(name, k), self.x].astype(F32) + other[...].astype(F32)

    def one(self, name, k):
        p = self.piece(name, k)
        self.go("g1", name, k, self.ref("G", name).at[p, 1 - self.x], self.ref("X", name).at[k, pl.ds(0, 2)],
                self.partners[0])

    def two(self, name, k):
        t = self.ref("T", name)

        @pl.when(self.end)
        def _():
            t[k] = self.half(name, k).astype(BF)

        self.go("g2", name, k, t.at[k], self.ref("Y", name).at[k], self.partners[1], self.end)

    def three(self, name, k):
        y, u = self.ref("Y", name), self.ref("U", name)

        @pl.when(self.middle)
        def _():
            mine = self.half(name, k)
            self.got("g2", name, k, y.at[k])
            u[k] = (mine + y[k].astype(F32)).astype(BF)

        self.go("g3", name, k, u.at[k], self.ref("Z", name).at[k], self.other_middle, self.middle)

    def four(self, name, k):
        u, z, fin = (self.ref(kind, name) for kind in "UZF")
        away = self.cfg.grads[name][3] and k > 0

        @pl.when(self.middle)
        def _():
            self.got("g3", name, k, z.at[k])
            total = (u[k].astype(F32) + z[k].astype(F32)).astype(BF)
            if away:
                self.ref("R", name)[k] = total
            else:
                fin[self.piece(name, k), self.x] = total

        if away:
            self.go("g4", name, k, self.ref("R", name).at[k], fin.at[self.w, self.x],
                    (self.c, jnp.bitwise_xor(self.w, k)), self.middle)

    def five(self, name, k):
        here = self.ref("F", name).at[self.piece(name, k), self.x]
        if self.cfg.grads[name][3] and k > 0:
            self.got("g4", name, k, here, self.middle)
        self.go("g5", name, k, here, here, self.partners[1], self.middle)
        self.go("g6", name, k, here, here, self.partners[0], self.middle)

    def six(self, name, k):
        here = self.ref("F", name).at[self.piece(name, k), self.x]
        self.got("g5", name, k, here, self.end)
        self.go("g6", name, k, here, here, self.partners[0], self.end)

    def seven(self, name, k):
        self.got("g6", name, k, self.ref("F", name).at[self.piece(name, k), 1 - self.x])

    def quarters_total(self, name, k):
        u, z, fin = (self.ref(kind, name) for kind in "UZF")
        self.got("g3", name, k, z.at[k, 0])
        total = (u[k, 0].astype(F32) + z[k, 0].astype(F32)).astype(BF)
        if not self.cfg.grads[name][3] or k == 0:
            fin[self.piece(name, k), self.x, self.near] = total
            return
        done = self.ref("R", name)
        done[k, 0] = total
        self.go("g4", name, k, done.at[k, 0], fin.at[self.w, self.x, self.near], (self.c, jnp.bitwise_xor(self.w, k)))

    def owned(self, name, k):
        here = self.ref("F", name).at[self.piece(name, k), self.x, self.near]
        if self.cfg.grads[name][3] and k > 0:
            self.got("g4", name, k, here)
        return here

    def three_others(self):
        x, n = self.x, self.near
        return ((1 - x, n, self.partners[0]), (x, 1 - n, self.partners[1]), (1 - x, 1 - n, self.partners[3]))

    def quarters(self, name, k):
        p = self.piece(name, k)
        for i, (x, n, dev) in enumerate(self.three_others()):
            self.go("g1", name, 3 * k + i, self.ref("G", name).at[p, x, n], self.ref("X", name).at[k, i], dev)

    def quarters_sum(self, name, k):
        total = self.ref("G", name)[self.piece(name, k), self.x, self.near].astype(F32)
        for i in range(3):
            other = self.ref("X", name).at[k, i]
            self.got("g1", name, 3 * k + i, other)
            total = total + other[...].astype(F32)
        u = self.ref("U", name)
        u[k, 0] = total.astype(BF)
        self.go("g3", name, k, u.at[k, 0], self.ref("Z", name).at[k, 0], self.partners[2])

    def spread(self, name, k):
        here = self.owned(name, k)
        for i, (_, _, dev) in enumerate(self.three_others()):
            self.go("g5", name, 3 * k + i, here, here, dev)

    def spread_end(self, name, k):
        p = self.piece(name, k)
        for i, (x, n, _) in enumerate(self.three_others()):
            self.got("g5", name, 3 * k + i, self.ref("F", name).at[p, x, n])


def layer_kernel(cfg, names, n_in, *refs):
    (x_ref, cot_ref, qkv_ref, out_ref, up_ref, down_ref, len_ref, *vec_refs) = refs[:n_in]
    y_ref, gx_ref, gqkv_ref, gout_ref, gup_ref, gdown_ref, gvec_ref = refs[n_in : n_in + 7]
    m = SimpleNamespace(**dict(zip(names, refs[n_in + 7 :])))
    if cfg.fused:
        m.Fqkv, m.Fout, m.Fup, m.Fdown = gqkv_ref, gout_ref, gup_ref, gdown_ref
    C, W, B, D, DW, DP, KVW, MW, R, HW = (
        cfg.C, cfg.W, cfg.B, cfg.D, cfg.DW, cfg.DP, cfg.KVW, cfg.MW, cfg.R, cfg.HW)
    OFF = DP - DW
    Q, HB = W * B, B // 2
    c = lax.axis_index("ctx")
    w = lax.axis_index("wa")
    block_part = lax.rem(c, R)
    block_slot = lax.div(c, R)
    s = lax.div(c, R)
    low = lax.rem(c, R)
    g_att = lax.div(w, 2) * 2 + lax.rem(low, 2)
    r_att = lax.div(low, 2) * 2 + lax.rem(w, 2)

    def att_device(t, g, r):
        return (t * R + lax.div(r, 2) * 2 + lax.rem(g, 2), lax.div(g, 2) * 2 + lax.rem(r, 2))

    def is_me(dev):
        return jnp.logical_and(dev[0] == c, dev[1] == w)

    drains = []

    def remote(src, dst, ss, rs, dev):
        return pltpu.make_async_remote_copy(
            src_ref=src, dst_ref=dst, send_sem=ss, recv_sem=rs, device_id=dev, device_id_type=MESH)

    def send(src, dst, ss, rs, dev, pred=None):
        def go():
            remote(src, dst, ss, rs, dev).start()

        def end():
            remote(src, dst, ss, rs, dev).wait_send()

        if pred is None:
            go()
        else:
            pl.when(pred)(go)
        drains.append((pred, end))

    def arrive(dst, rs, pred=None):
        def go():
            remote(dst, dst, rs, rs, (c, w)).wait_recv()

        if pred is None:
            go()
        else:
            pl.when(pred)(go)

    barrier = pltpu.get_barrier_semaphore()

    def greet(i, carry):
        ci, wi = lax.div(i, W), lax.rem(i, W)

        @pl.when(jnp.logical_not(is_me((ci, wi))))
        def _():
            pl.semaphore_signal(barrier, inc=1, device_id=(ci, wi), device_id_type=MESH)

        return carry

    lax.fori_loop(0, C * W, greet, 0)

    def entered():
        pl.semaphore_wait(barrier, C * W - 1)

    def peer(k):
        return (c, jnp.bitwise_xor(w, k))

    def gather_start(buf, ss, rs, parts=1):
        n = buf.shape[1] // parts
        for h in range(parts):
            rows = buf.at[w, pl.ds(h * n, n)]
            send(rows, rows, ss.at[2 * parts + h], rs.at[2 * parts + h], peer(2))
        send(buf.at[w], buf.at[w], ss.at[1], rs.at[1], peer(1))

    def gather_wait(buf, ss, rs, k, h=0, parts=1):
        n = buf.shape[1] // parts
        t = jnp.bitwise_xor(w, k)
        if k == 1:
            arrive(buf.at[t], rs.at[1])
            return
        rows = buf.at[t, pl.ds(h * n, n)]
        arrive(rows, rs.at[k * parts + h])
        if k == 2:
            send(rows, rows, ss.at[3 * parts + h], rs.at[3 * parts + h], peer(1))

    def take(ref, blocks):
        parts = [ref[t, rows, :] for t, rows in blocks]
        return jnp.concatenate(parts, 0) if len(parts) > 1 else parts[0]

    def put(ref, blocks, value):
        n = value.shape[0] // len(blocks)
        for i, (t, rows) in enumerate(blocks):
            ref[t, rows, :] = value[i * n : (i + 1) * n].astype(ref.dtype)

    def feed(buf, sems, work, part, stage, recv, sum_sems, idle, early=None, late=None):
        (ss, rs), (ss2, rs2) = sems, sum_sems
        t3, t2, t1 = (jnp.bitwise_xor(w, k) for k in (3, 2, 1))
        every = pl.ds(0, B)
        halves = [pl.ds(h * HB, HB) for h in range(2)]
        mine = [None, None]

        def across(h):
            rows = halves[h]
            arrive(recv.at[1, rows], rs2.at[2 + h])
            stage[t2, rows, :] = (mine[h] + recv[1, rows, :].astype(F32)).astype(BF)
            send(stage.at[t2, rows], recv.at[2, rows], ss2.at[4 + h], rs2.at[4 + h], peer(2))

        gather_start(buf, ss, rs, 2)
        work([(w, every)])
        gather_wait(buf, ss, rs, 1, 0, 2)
        work([(t1, every)])
        idle()
        for h, rows in enumerate(halves):
            gather_wait(buf, ss, rs, 2, h, 2)
            if h:
                across(0)
            gather_wait(buf, ss, rs, 3, h, 2)
            work([(t3, rows), (t2, rows)])
            both = part([(t3, rows), (t2, rows)])
            stage[t3, rows, :] = both[0:HB].astype(BF)
            send(stage.at[t3, rows], recv.at[1, rows], ss2.at[2 + h], rs2.at[2 + h], peer(1))
            mine[h] = both[HB:]
        stage[t1] = part([(t1, every)]).astype(BF)
        send(stage.at[t1], recv.at[0], ss2.at[0], rs2.at[0], peer(1))
        if early:
            early()
        across(1)
        own = part([(w, every)])
        arrive(recv.at[0], rs2.at[0])
        own = own + recv[0].astype(F32)
        if late:
            late()
        for h, rows in enumerate(halves):
            arrive(recv.at[2, rows], rs2.at[4 + h])
        return own + recv[2].astype(F32)

    def scatter_steps(part, stage, recv, ss, rs):
        t3, t2, t1 = (jnp.bitwise_xor(w, k) for k in (3, 2, 1))

        def first():
            stage[t3] = part(t3).astype(BF)
            send(stage.at[t3], recv.at[1], ss.at[1], rs.at[1], peer(1))
            stage[t1] = part(t1).astype(BF)
            send(stage.at[t1], recv.at[0], ss.at[0], rs.at[0], peer(1))

        def second():
            mine2 = part(t2)
            arrive(recv.at[1], rs.at[1])
            stage[t2] = (mine2 + recv[1].astype(F32)).astype(BF)
            send(stage.at[t2], recv.at[2], ss.at[2], rs.at[2], peer(2))

        def third():
            own = part(w)
            arrive(recv.at[0], rs.at[0])
            own = own + recv[0].astype(F32)
            arrive(recv.at[2], rs.at[2])
            return own + recv[2].astype(F32)

        return first, second, third

    def pack(ref, value):
        ref[:, 0:DW] = value[0:HB].astype(BF)
        ref[:, DW:KVW] = value[HB:B].astype(BF)

    def unpack(ref, lane, packed):
        ref[0:HB, lane : lane + DW] = packed[:, 0:DW]
        ref[HB:B, lane : lane + DW] = packed[:, DW:KVW]

    def local(src, dst, sem):
        cp = pltpu.make_async_copy(src, dst, sem)
        cp.start()
        return cp

    rows_w = pl.ds(w * DW, DW)
    own = [
        local(qkv_ref, m.Wq, m.s_own.at[0]),
        local(x_ref, m.Xall.at[w], m.s_own.at[1]),
        local(out_ref, m.Out.at[w], m.s_own.at[2]),
        local(up_ref.at[:, pl.ds(pl.multiple_of(w * cfg.FW, cfg.FW), cfg.FW)], m.Upc.at[rows_w], m.s_own.at[3]),
        local(down_ref, m.Dn, m.s_own.at[4]),
        local(cot_ref, m.Cot, m.s_own.at[5]),
    ]
    own[0].wait()
    for g in range(W):
        for i, third in enumerate((1, 2, 0)):
            a = third * D + g * DW
            m.Ws[g, :, i * DW : (i + 1) * DW] = m.Wq[:, a : a + DW]
        m.Ws[g, :, 3 * DW : MW] = jnp.zeros((DW, MW - 3 * DW), BF)
    row = 0
    for ref in vec_refs:
        v = ref[...].astype(F32)
        for i in range(v.shape[0] // DW):
            m.Vv[w, row : row + 1, :] = v[i * DW : (i + 1) * DW].reshape(1, DW)
            row += 1
    m.Vv[w, row:VROWS, :] = jnp.full((VROWS - row, DW), len_ref[0].astype(F32))
    own[1].wait()
    entered()

    def part_rows(t, part, parts):
        return pl.ds(pl.multiple_of(t * DW + part * (DW // parts), 16), DW // parts)

    quarter = lax.rem(c, 4)

    def near_me(k):
        return (jnp.bitwise_xor(c, k), w)

    for k in (2, 3):
        send(m.Ws.at[jnp.bitwise_xor(w, k), part_rows(0, quarter, 4)], m.Wc.at[part_rows(w, quarter, 4)],
             m.s_wq.at[k], m.r_wq.at[k], peer(k))
    gather_start(m.Xall, m.s_x, m.r_x)
    send(m.Ws.at[jnp.bitwise_xor(w, 1)], m.Wc.at[rows_w], m.s_wq.at[1], m.r_wq.at[1], peer(1))
    for k in (2, 3, 1):
        send(m.Vv.at[w], m.Vv.at[w], m.s_vv.at[k], m.r_vv.at[k], peer(k))
    m.Wc[rows_w, :] = m.Ws[w]
    m.wide[...] = jnp.zeros(m.wide.shape, BF)
    m.bias[...] = jnp.zeros(m.bias.shape, F32)
    for cp in own[2:]:
        cp.wait()
    m.DnT[...] = m.Dn[...].T
    for k in (2, 3):
        rows = m.Wc.at[part_rows(jnp.bitwise_xor(w, k), quarter, 4)]
        arrive(rows, m.r_wq.at[k])
        for i in (1, 2, 3):
            e = 3 * (k - 2) + i - 1
            send(rows, rows, m.s_wf.at[e], m.r_wf.at[e], near_me(i))
    for k in (1, 2, 3):
        gather_wait(m.Xall, m.s_x, m.r_x, k)
    arrive(m.Wc.at[pl.ds(jnp.bitwise_xor(w, 1) * DW, DW)], m.r_wq.at[1])
    for k in (1, 2, 3):
        arrive(m.Vv.at[jnp.bitwise_xor(w, k)], m.r_vv.at[k])
    gather_start(m.Out, m.s_ow, m.r_ow)
    for k in (2, 3, 1):
        cols = pl.ds(pl.multiple_of(jnp.bitwise_xor(w, k) * cfg.FW, cfg.FW), cfg.FW)
        send(up_ref.at[:, cols], m.Upc.at[rows_w], m.s_uw.at[k], m.r_uw.at[k], peer(k))
    for k in (2, 3):
        for i in (1, 2, 3):
            e = 3 * (k - 2) + i - 1
            arrive(m.Wc.at[part_rows(jnp.bitwise_xor(w, k), jnp.bitwise_xor(quarter, i), 4)], m.r_wf.at[e])

    for t in range(W):
        m.Vs[0:6, t * DW : (t + 1) * DW] = m.Vv[t, 0:6, :]
        m.upb[0:1, t * DW : (t + 1) * DW] = m.Vv[w, UPB + t : UPB + t + 1, :]
    upper, odd = lax.div(w, 2), lax.rem(w, 2)
    m.bias[0:1, DW : 2 * DW] = m.Vv[W // 2 + upper, pl.ds(QVB + odd, 1), :]
    m.bias[0:1, 2 * DW : 3 * DW] = m.Vv[upper, pl.ds(QVB + odd, 1), :]
    bias = m.bias[0:1, :]

    def vec(row):
        return m.Vs[row : row + 1, :]

    kv_rows = pl.ds(pl.multiple_of(block_part * Q + block_slot * B, B), B)
    order = [lax.rem(s + 1 + k, W) for k in range(W)]
    for k, t in enumerate(order):
        qkv = dot(m.Xall[t], m.Wc[...]) + bias
        m.KVs[t] = qkv[:, 0:KVW].astype(BF)
        pack(m.Qs.at[t], qkv[:, KVW : KVW + DW])
        dev = att_device(t, w, block_part)
        send(m.Qs.at[t], m.Rq.at[block_slot], m.s_q.at[k], m.r_q.at[block_slot], dev, jnp.logical_not(is_me(dev)))
    for k, t in enumerate(order):
        dev = att_device(t, w, block_part)
        send(m.KVs.at[t], m.KV.at[kv_rows], m.s_kv.at[k], m.r_kv.at[block_slot], dev, jnp.logical_not(is_me(dev)))

        @pl.when(is_me(dev))
        def _():
            m.Rq[block_slot] = m.Qs[t]
            m.KV[kv_rows, :] = m.KVs[t]

    lanes = lax.broadcasted_iota(jnp.int32, (1, DP), 1)

    def q_lane(h):
        return jnp.logical_and(lanes >= h * HEAD, lanes < (h + 1) * HEAD)

    def v_lane(h):
        return jnp.logical_and(lanes >= OFF + h * HEAD, lanes < OFF + (h + 1) * HEAD)

    for j in range(W):
        arrive(m.Rq.at[j], m.r_q.at[j], jnp.logical_not(is_me((j * R + r_att, g_att))))
        unpack(m.wide, 0, m.Rq.at[j])
        q = m.wide[...] * jnp.asarray(HEAD**-0.5, BF)
        for h in range(HW):
            m.Qm[h, j * B : (j + 1) * B, :] = jnp.where(q_lane(h), q, jnp.zeros_like(q))

    KC = 2 * B
    PER_SET = Q // KC
    len_s = m.Vv[s, LEN : LEN + 1, 0:1]

    def alive(chunk):
        r, half = lax.div(chunk, PER_SET), lax.rem(chunk, PER_SET)
        row = lax.broadcasted_iota(jnp.int32, (KC, Q), 0)
        later = (row >= B).astype(jnp.int32)
        place = ((2 * half + later) * R + r) * B + row - later * B
        return place.astype(F32) < len_s

    m.mrow[...] = jnp.full(m.mrow.shape, FLOOR, F32)
    m.lrow[...] = jnp.zeros(m.lrow.shape, F32)
    m.OT[...] = jnp.zeros(m.OT.shape, F32)

    def attend(chunk, carry):
        rows = pl.ds(pl.multiple_of(chunk * KC, KC), KC)
        keys = m.KV[rows, 0:DP]
        values_t = m.KV[rows, KVW - DP : KVW].T
        live = alive(chunk)
        for h in range(HW):
            scores = jnp.where(live, dot_nt(keys, m.Qm[h]), FLOOR)
            top = m.mrow[h : h + 1, :]
            new_top = jnp.maximum(top, jnp.max(scores, 0, keepdims=True))
            prob = jnp.exp(scores - new_top)
            factor = jnp.exp(top - new_top)
            m.mrow[h : h + 1, :] = new_top
            m.lrow[h : h + 1, :] = m.lrow[h : h + 1, :] * factor + col_sum(prob)
            a, b = h * HEAD, (h + 1) * HEAD
            m.OT[a:b, :] = m.OT[a:b, :] * factor + dot(values_t[OFF + a : OFF + b, :], prob.astype(BF))
        return carry

    for i in range(PER_SET):
        pair = jnp.bitwise_xor(lax.div(s, 2), i)
        for e in range(2):
            j = 2 * pair + e
            rows = m.KV.at[pl.ds(pl.multiple_of(r_att * Q + j * B, B), B)]
            arrive(rows, m.r_kv.at[j], jnp.logical_not(is_me((j * R + r_att, g_att))))
            for k in range(1, R):
                send(rows, rows, m.s_kf.at[(k - 1) * W + 2 * i + e], m.r_kf.at[r_att * W + j],
                     att_device(s, g_att, lax.rem(r_att + k, R)))
        attend(r_att * PER_SET + pair, 0)
        if i == 0:
            gather_wait(m.Out, m.s_ow, m.r_ow, 2)

        def others(k, carry):
            r = lax.rem(r_att + k, R)
            for e in range(2):
                j = 2 * pair + e
                arrive(m.KV.at[pl.ds(pl.multiple_of(r * Q + j * B, B), B)], m.r_kf.at[r * W + j])
            return attend(r * PER_SET + pair, carry)

        lax.fori_loop(1, R, others, 0)
    for h in range(HW):
        a, b = h * HEAD, (h + 1) * HEAD
        m.OT[a:b, :] = m.OT[a:b, :] / m.lrow[h : h + 1, :]
    m.lrow[0:HW, :] = m.mrow[0:HW, :] + jnp.log(m.lrow[0:HW, :])
    for j in range(W):
        pack(m.Os.at[j], m.OT[:, j * B : (j + 1) * B].T)
        dev = (j * R + r_att, s)
        send(m.Os.at[j], m.Mix.at[g_att], m.s_o.at[j], m.r_o.at[g_att], dev, jnp.logical_not(is_me(dev)))

        @pl.when(is_me(dev))
        def _():
            m.Mix[g_att] = m.Os[j]

    for k in (1, 3):
        gather_wait(m.Out, m.s_ow, m.r_ow, k)
    out_weight = m.Out[...].reshape(D, D)
    resid = m.Xall[w].astype(F32) + vec(OUTB)
    for g in range(W):
        arrive(m.Mix.at[g], m.r_o.at[g], jnp.logical_not(is_me(att_device(w, g, block_part))))
        unpack(m.mixed, g * DW, m.Mix.at[g])
    resid = resid + dot(m.mixed[...], out_weight)
    n1, r1 = norm_stats(resid)
    m.n1[...] = n1
    m.r1[...] = r1
    n1_full = n1 * vec(GAIN1) + vec(SHIFT1)
    m.N1f[...] = n1_full
    m.N1all[w] = n1_full.astype(BF)

    for k in (1, 2, 3):
        arrive(m.Upc.at[pl.ds(jnp.bitwise_xor(w, k) * DW, DW)], m.r_uw.at[k])
    up_bias = m.upb[0:1, :]

    activated = []

    def expand(blocks):
        h = dot(take(m.N1all, blocks), m.Upc[...]) + up_bias
        phi = 0.5 * (1.0 + lax.erf(h * (2.0**-0.5)))
        put(m.Gs, blocks, h * phi)
        put(m.Hp, blocks, phi + h * ((2.0 * math.pi) ** -0.5) * jnp.exp(-0.5 * h * h))
        if cfg.fused:
            for t, rows in blocks:
                i = len(activated)
                activated.append((t, rows))
                send(m.Gs.at[t, rows], m.GX.at[t, rows], m.s_gx.at[i], m.r_gx.at[i], near_me(1))

    def turn_weights():
        m.UpT[...] = m.Upc[...].T
        m.OutT[...] = m.Out[...].reshape(D, D).T

    ffn = feed(m.N1all, (m.s_n, m.r_n), expand, lambda blocks: dot(take(m.Gs, blocks), m.Dn[...]), m.Fs, m.Fr,
               (m.s_f, m.r_f), turn_weights)
    n2, r2 = norm_stats(m.N1f[...] + ffn + vec(DOWNB))
    m.n2[...] = n2
    y_ref[...] = (n2 * vec(GAIN2) + vec(SHIFT2)).astype(BF)

    place = c * B + lax.broadcasted_iota(jnp.int32, (B, D), 0)
    dy = jnp.where(place.astype(F32) < m.Vv[w, LEN : LEN + 1, 0:1], m.Cot[...].astype(F32), 0.0)
    d_r2 = norm_back(dy, n2, r2, vec(GAIN2))
    m.dR2[...] = d_r2
    m.dFall[w] = d_r2.astype(BF)

    def shrink(blocks):
        put(m.dHs, blocks, dot(take(m.dFall, blocks), m.DnT[...]) * take(m.Hp, blocks))

    def flat(ref):
        return ref[...].reshape(Q, ref.shape[-1])

    def put_grad(name, plain, lhs, rhs, parts):
        rows = lhs.shape[-1] // parts
        for i in range(parts):
            val = dot_tn(lhs[:, :, i * rows : (i + 1) * rows].reshape(Q, rows), flat(rhs)).astype(BF)
            if cfg.fused:
                _, ch, cols, _ = cfg.grads[name]
                n = rows // (4 * ch)
                getattr(m, "G" + name)[i * n : (i + 1) * n] = val.reshape(n, 2, 2, ch, cols)
            else:
                plain[i * rows : (i + 1) * rows, :] = val

    pump = Sums(cfg, m, c, w, send, arrive)

    side = lax.rem(c, 2)

    def half_cols(side):
        return pl.ds(pl.multiple_of(side * (D // 2), 128), D // 2)

    def down_half():
        for i, k in enumerate((0, 2)):
            rows = m.DX.at[jnp.bitwise_xor(w, k)]
            arrive(rows, m.r_fx.at[i])
            send(rows, rows, m.s_fx.at[2 + i], m.r_fx.at[2 + i], peer(1))
        for i, (t, rows) in enumerate(activated):
            arrive(m.GX.at[t, rows], m.r_gx.at[i])
        for i, k in enumerate((1, 3)):
            arrive(m.DX.at[jnp.bitwise_xor(w, k)], m.r_fx.at[2 + i])
        pieces, ch, cols, _ = cfg.grads["down"]
        n = cfg.FW // 2
        here = m.dFall[:, :, half_cols(side)].reshape(Q, cols)
        there = flat(m.DX)
        for i in range(2):
            at = slice(i * n, (i + 1) * n)
            val = dot_tn(m.Gs[:, :, at].reshape(Q, n), here) + dot_tn(m.GX[:, :, at].reshape(Q, n), there)
            m.Gdown[i * (pieces // 2) : (i + 1) * (pieces // 2)] = val.astype(BF).reshape(pieces // 2, 2, ch, cols)

    def early():
        if cfg.fused:
            for i, k in enumerate((0, 2)):
                t = jnp.bitwise_xor(w, k)
                send(m.dFall.at[t, :, half_cols(1 - side)], m.DX.at[t], m.s_fx.at[i], m.r_fx.at[i], near_me(1))
        else:
            put_grad("down", gdown_ref, m.Gs, m.dFall, 2)
        pump.run("early")

    def late():
        m.gv[2:3, :] = col_sum(dy * n2)
        m.gv[3:4, :] = col_sum(dy)
        m.gv[5:6, :] = col_sum(m.dFall[w].astype(F32))
        put_grad("up", gup_ref, m.N1all, m.dHs, 2)
        m.gv[6:7, :] = col_sum(flat(m.dHs).astype(F32))
        pump.run("norm")

    def turn_projection():
        m.WcT[...] = m.Wc[...].T

    d_n1 = feed(m.dFall, (m.s_df, m.r_df), shrink, lambda blocks: dot(take(m.dHs, blocks), m.UpT[...]), m.dNs, m.dNr,
                (m.s_dn, m.r_dn), turn_projection, early, late) + m.dR2[...]
    n1 = m.n1[...]
    d_r1 = norm_back(d_n1, n1, m.r1[...], vec(GAIN1))
    m.dR1[...] = d_r1
    d_a = d_r1.astype(BF)
    m.dAall[w] = d_a
    d_mixed = dot(d_a, m.OutT[...])
    for g in range(W):
        pack(m.dOs.at[g], d_mixed[:, g * DW : (g + 1) * DW])
        dev = att_device(w, g, block_part)
        send(m.dOs.at[g], m.dOr.at[block_slot], m.s_do.at[g], m.r_do.at[block_slot], dev,
             jnp.logical_not(is_me(dev)))

        @pl.when(is_me(dev))
        def _():
            m.dOr[block_slot] = m.dOs[g]

    pump.run("sent")
    gather_start(m.dAall, m.s_da, m.r_da)
    for k in (2, 3, 1):
        send(m.Mix.at[jnp.bitwise_xor(w, k)], m.MixT.at[w], m.s_mt.at[k], m.r_mt.at[k], peer(k))
    if cfg.fused:
        down_half()
    pump.run("down")
    m.MixT[w] = m.Mix[w]
    m.gv[0:1, :] = col_sum(d_n1 * n1)
    m.gv[1:2, :] = col_sum(d_n1)
    m.gv[4:5, :] = col_sum(d_a.astype(F32))

    m.wide[...] = jnp.zeros(m.wide.shape, BF)

    def weights_again(chunk, h):
        rows = pl.ds(pl.multiple_of(chunk * KC, KC), KC)
        scores = dot_nt(m.KV[rows, 0:DP], m.Qm[h])
        return jnp.where(alive(chunk), jnp.exp(scores - m.lrow[h : h + 1, :]), 0.0)

    if cfg.keep:

        def keep(chunk, carry):
            for h in range(HW):
                m.Pm[h, pl.ds(pl.multiple_of(chunk * KC, KC), KC), :] = weights_again(chunk, h)
            return carry

        lax.fori_loop(0, R * PER_SET, keep, 0)
    for j in range(W):
        pump.run("sent%d" % j)
        arrive(m.dOr.at[j], m.r_do.at[j], jnp.logical_not(is_me((j * R + r_att, s))))
        unpack(m.wide, OFF, m.dOr.at[j])
        d_o = m.wide[...]
        cols = slice(j * B, (j + 1) * B)
        for h in range(HW):
            m.Dm[h, cols, :] = jnp.where(v_lane(h), d_o, jnp.zeros_like(d_o))
        prod = m.OT[:, cols] * d_o.astype(F32).T[OFF:DP, :]
        for h in range(HW):
            m.drow[h : h + 1, cols] = col_sum(prod[h * HEAD : (h + 1) * HEAD, :])
    m.dQT[...] = jnp.zeros(m.dQT.shape, F32)
    pump.run("arrived")

    def attend_back(step, carry):
        chunk = lax.rem((r_att + 1) * PER_SET + step, R * PER_SET)
        rows = pl.ds(pl.multiple_of(chunk * KC, KC), KC)
        keys = m.KV[rows, 0:DP]
        values = m.KV[rows, KVW - DP : KVW]
        keys_t = keys.T
        d_k = jnp.zeros((KC, DP), F32)
        d_v = jnp.zeros((KC, DP), F32)
        for h in range(HW):
            prob = m.Pm[h, rows, :] if cfg.keep else weights_again(chunk, h)
            d_prob = dot_nt(values, m.Dm[h])
            d_s = (prob * (d_prob - m.drow[h : h + 1, :])).astype(BF)
            d_k = d_k + dot(d_s, m.Qm[h])
            d_v = d_v + dot(prob.astype(BF), m.Dm[h])
            a, b = h * HEAD, (h + 1) * HEAD
            m.dQT[a:b, :] = m.dQT[a:b, :] + dot(keys_t[a:b, :], d_s)
        lead = KVW - DP
        d_kv = jnp.concatenate([d_k[:, 0:lead], d_k[:, lead:] + d_v[:, 0 : DP - lead], d_v[:, DP - lead :]], 1)
        place, part = lax.div(step, PER_SET), lax.rem(step, PER_SET)
        rows = pl.ds(pl.multiple_of(part * KC, KC), KC)
        if carry is None:
            m.dKVf[rows, :] = d_kv
        else:
            m.dKVs[place, rows, :] = d_kv.astype(BF)
        return carry

    lax.fori_loop(0, (R - 1) * PER_SET, attend_back, 0)
    for k in range(1, R):
        send(m.dKVs.at[k - 1], m.dKVr.at[R - k - 1], m.s_dkv.at[k - 1], m.r_dkv.at[R - k - 1],
             att_device(s, g_att, lax.rem(r_att + k, R)))
    pump.run("between")
    lax.fori_loop((R - 1) * PER_SET, R * PER_SET, attend_back, None)
    pump.run("after")
    pump.run("part")
    for k in range(1, R):
        arrive(m.dKVr.at[k - 1], m.r_dkv.at[k - 1])
    for j in range(W):
        d_kv = m.dKVf[j * B : (j + 1) * B, :]
        for k in range(1, R):
            d_kv = d_kv + m.dKVr[k - 1, j * B : (j + 1) * B, :].astype(F32)
        m.dKVo[j] = d_kv.astype(BF)
        pack(m.dQs.at[j], m.dQT[:, j * B : (j + 1) * B].T * (HEAD**-0.5))
        dev = (j * R + r_att, g_att)
        away = jnp.logical_not(is_me(dev))
        send(m.dKVo.at[j], m.dqr.at[s, :, pl.ds(0, KVW)], m.s_dk.at[j], m.r_dk.at[s], dev, away)
        send(m.dQs.at[j], m.dQr.at[s], m.s_dq.at[j], m.r_dq.at[s], dev, away)

        @pl.when(is_me(dev))
        def _():
            m.dqr[s, :, 0:KVW] = m.dKVo[j]
            m.dQr[s] = m.dQs[j]

    for k in (1, 2, 3):
        pump.run("dq%d" % k)
        gather_wait(m.dAall, m.s_da, m.r_da, k)
        arrive(m.MixT.at[jnp.bitwise_xor(w, k)], m.r_mt.at[k])
    for t in range(W):
        unpack(m.Mt.at[t], 0, m.MixT.at[t])
        m.dqr[t, :, KVW + DW : MW] = jnp.zeros((B, MW - KVW - DW), BF)
    put_grad("out", gout_ref, m.Mt, m.dAall, 1)
    pump.run("out")

    for t in range(W):
        pump.run("wait%d" % t)
        away = jnp.logical_not(is_me(att_device(t, w, block_part)))
        arrive(m.dqr.at[t, :, pl.ds(0, KVW)], m.r_dk.at[t], away)
        arrive(m.dQr.at[t], m.r_dq.at[t], away)
        unpack(m.dqr.at[t], KVW, m.dQr.at[t])
    put_grad("qkv", gqkv_ref, m.Xall, m.dqr, 2)
    pump.run("qkv")

    m.gv[7:8, 0:MW] = col_sum(flat(m.dqr).astype(F32))
    m.gv[7:8, MW:D] = jnp.zeros((1, D - MW), F32)

    def d_x(t):
        return dot(m.dqr[t], m.WcT[...])

    token_steps = scatter_steps(d_x, m.dxs, m.dxr, m.s_dx, m.r_dx)

    def vectors(i):
        if i:
            arrive(m.Vb.at[i - 1], m.r_v1.at[i - 1])
            m.Va[i] = m.Va[i - 1] + m.Vb[i - 1]
        else:
            m.Va[0] = m.gv[...]
        if i < 3:
            send(m.Va.at[i], m.Vb.at[i], m.s_v1.at[i], m.r_v1.at[i], pump.partners[i])

    def vectors_to_rows():
        vectors(3)
        total = m.Va[3]
        for t in range(W):
            m.Vt[t, 0:6, :] = total[0:6, t * DW : (t + 1) * DW]
            m.Vt[t, 6:7, :] = total[7:8, 2 * DW : 3 * DW]
            m.Vt[t, 7:8, :] = total[7:8, DW : 2 * DW]
        m.Vw[w] = m.Vt[w]
        for k in (2, 3, 1):
            send(m.Vt.at[jnp.bitwise_xor(w, k)], m.Vw.at[w], m.s_vw.at[k], m.r_vw.at[k], peer(k))
        gvec_ref[7:8, :] = total[6:7, :]

    def vectors_end():
        for k in (1, 2, 3):
            arrive(m.Vw.at[jnp.bitwise_xor(w, k)], m.r_vw.at[k])
        gvec_ref[0:6, 0:DW] = m.Vw[0, 0:6, :] + m.Vw[1, 0:6, :] + m.Vw[2, 0:6, :] + m.Vw[3, 0:6, :]
        for i in range(2):
            gvec_ref[6:7, i * DW : (i + 1) * DW] = m.Vw[2 * odd + i, pl.ds(6 + upper, 1), :]

    steps = [functools.partial(vectors, i) for i in range(3)] + [vectors_to_rows, vectors_end]

    if not cfg.fused:
        for step in token_steps[:-1]:
            step()
        d_x_sum = token_steps[-1]()
        gvec_ref[0] = m.gv[...]
    else:
        vector_steps = [functools.partial(vectors, i) for i in range(3)] + [vectors_to_rows, vectors_end]
        pump.run("tail", dict(tokens=token_steps, vectors=vector_steps))
        pump.finish()
        d_x_sum = token_steps[2]()
    gx_ref[...] = (m.dR1[...] + d_x_sum).astype(BF)

    for pred, end in drains:
        if pred is None:
            end()
        else:
            pl.when(pred)(end)


def body(C, W, tokens, lengths, qkv_weight, out_weight, up_weight, down_weight, qv_bias, out_bias, up_bias,
         down_bias, gain_one, shift_one, gain_two, shift_two, cotangent):
    _, B, D = tokens.shape
    FW = down_weight.shape[0]
    DW = D // W
    DP = -(-DW // 128) * 128
    KVW = 2 * DW
    MW = KVW + DP
    R = C // W
    cfg = SimpleNamespace(C=C, W=W, B=B, D=D, FW=FW, DW=DW, DP=DP, KVW=KVW, MW=MW, R=R, HW=HEADS // W)
    cfg.fused = R == 2 and C == 8 and DW % 64 == 0 and FW % (64 * W) == 0
    cfg.keep = R == 2
    cfg.grads = dict(down=(W, FW // W // 2, D // 2, False), up=(W, DW // 4, FW, True), qkv=(W, DW // 4, MW, True),
                     out=(1, DW // 4, D, False))
    w = lax.axis_index("wa")
    small = (out_bias, down_bias, gain_one, shift_one, gain_two, shift_two, qv_bias, up_bias)

    plan = make_plan(cfg)
    names = list(plan)
    vm = pl.BlockSpec(memory_space=pltpu.VMEM)
    hbm = pl.BlockSpec(memory_space=pl.ANY)
    if cfg.fused:
        outs = [(n, 2, 2, ch, cols) for n, ch, cols, _ in (cfg.grads[k] for k in ("qkv", "out", "up", "down"))]
        place = pltpu.VMEM
    else:
        outs = [(D, MW), (DW, D), (D, FW), (FW, D)]
        place = jax.ShapeDtypeStruct
    outs = [place(a, BF) for a in [(B, D), (B, D)] + outs] + [place((GROWS, D) if cfg.fused else (1, GROWS, D), F32)]
    args = (tokens.reshape(B, D), cotangent.reshape(B, D), qkv_weight, out_weight, up_weight, down_weight, lengths, *small)
    y, gx, gqkv, gout, gup, gdown, gvec = pl.pallas_call(
        functools.partial(layer_kernel, cfg, names, len(args)),
        out_shape=outs,
        in_specs=[hbm] * 6 + [pl.BlockSpec(memory_space=pltpu.SMEM)] + [vm] * len(small),
        out_specs=[vm] * len(outs),
        scratch_shapes=[plan[n] for n in names],
        compiler_params=pltpu.CompilerParams(collective_id=0, has_side_effects=True, vmem_limit_bytes=(52 if cfg.fused else 60) << 20),
        name="layer",
    )(*args)
    if cfg.fused:
        return finish(cfg, y, gx, gqkv, gout, gup, gdown, gvec)

    def to_rows(g):
        g = lax.psum(g, "ctx").reshape(W, DW, g.shape[1])
        return lax.all_to_all(g, "wa", 0, 0, tiled=True).transpose(1, 0, 2).reshape(DW, -1)

    gq = to_rows(gqkv).reshape(DW, W, MW).astype(F32)
    gup = to_rows(gup)
    gout, gdown, gvec = lax.psum((gout, gdown, gvec), "ctx")
    gvec = lax.all_gather(gvec, "wa", axis=0, tiled=True)
    gqkv = jnp.concatenate([gq[:, :, a : a + DW].reshape(DW, D) for a in (KVW, 0, DW)], 1)
    own = lax.dynamic_slice_in_dim(jnp.sum(gvec, 0)[0:6], w * DW, DW, 1)
    g_upb = lax.dynamic_slice_in_dim(gvec, w, 1, 0)[0, 6]
    g_qv = jnp.concatenate([gvec[:, 7, KVW : KVW + DW].reshape(D), gvec[:, 7, DW:KVW].reshape(D)])
    g_qv = lax.dynamic_slice_in_dim(g_qv, w * (2 * D // W), 2 * D // W)
    return (y.reshape(1, B, D), gx.reshape(1, B, D), gqkv, gout.astype(F32), gup.astype(F32),
            gdown.astype(F32), g_qv, own[4], g_upb, own[5], own[0], own[1], own[2], own[3])


def finish_kernel(cfg, y, gx, gqkv, gout, gup, gdown, gvec, o_y, o_gx, o_qkv, o_out, o_up, o_down, o_qv, o_outb, o_upb,
                  o_downb, o_g1, o_s1, o_g2, o_s2):
    W, D, DW, MW, KVW = cfg.W, cfg.D, cfg.DW, cfg.MW, cfg.KVW
    o_y[0] = y[...]
    o_gx[0] = gx[...]
    for g in range(W):
        rows = gqkv[g].reshape(DW, MW).astype(F32)
        for third, a in enumerate((KVW, 0, DW)):
            o_qkv[:, third * D + g * DW : third * D + (g + 1) * DW] = rows[:, a : a + DW]
        o_up[:, g * cfg.FW : (g + 1) * cfg.FW] = gup[g].reshape(DW, cfg.FW).astype(F32)
    o_out[...] = gout[...].reshape(o_out.shape).astype(F32)
    for x in range(2):
        o_down[:, x * (D // 2) : (x + 1) * (D // 2)] = gdown[:, x].reshape(cfg.FW, D // 2).astype(F32)
    o_qv[...] = gvec[6, 0 : 2 * DW]
    o_upb[...] = gvec[7, 0 : cfg.FW]
    for row, ref in enumerate((o_g1, o_s1, o_g2, o_s2, o_outb, o_downb)):
        ref[...] = gvec[row, 0:DW]


def finish(cfg, *arrays):
    B, D, DW, W, FW = cfg.B, cfg.D, cfg.DW, cfg.W, cfg.FW
    shapes = [(1, B, D)] * 2 + [(DW, 3 * D), (DW, D), (DW, W * FW), (FW, D), (2 * DW,), (DW,), (FW,)] + [(DW,)] * 5
    vm = pl.BlockSpec(memory_space=pltpu.VMEM)
    arrays = [pltpu.with_memory_space_constraint(a, pltpu.VMEM) for a in arrays]
    return pl.pallas_call(
        functools.partial(finish_kernel, cfg),
        out_shape=[jax.ShapeDtypeStruct(s, BF if i < 2 else F32) for i, s in enumerate(shapes)],
        in_specs=[vm] * len(arrays),
        out_specs=[vm] * len(shapes),
        compiler_params=pltpu.CompilerParams(vmem_limit_bytes=32 << 20),
        name="results",
    )(*arrays)


def solution(mesh):
    tok, vec, mat = P("wa", "ctx", None), P("wa"), P("wa", None)
    return jax.shard_map(
        functools.partial(body, mesh.shape["ctx"], mesh.shape["wa"]),
        mesh=mesh,
        in_specs=(tok, vec, mat, mat, mat, mat) + (vec,) * 8 + (tok,),
        out_specs=(tok, tok, mat, mat, mat, mat) + (vec,) * 8,
        check_vma=False,
    )
```

```python
import functools
import math
from types import SimpleNamespace

import jax
import jax.numpy as jnp
from jax import lax
from jax.experimental import pallas as pl
from jax.experimental.pallas import tpu as pltpu
from jax.sharding import PartitionSpec as P

HEADS = 12
HEAD = 64
EPS = 1e-12
FLOOR = -1e30
MESH = pl.DeviceIdType.MESH
BF = jnp.bfloat16
F32 = jnp.float32

OUTB, DOWNB, GAIN1, SHIFT1, GAIN2, SHIFT2, QVB = range(7)
UPB, LEN = 8, 12
VROWS = 16
GROWS = 8

ALL = (0, 1, 2, 3)
SCHEDULE = dict(
    early=(),
    norm=(),
    sent=(
        (1, "up", 0), (1, "up", 1), (1, "up", 2), (1, "up", 3),
    ),
    down=(
        (1, "down", 0), (1, "down", 1), (1, "down", 2), (1, "down", 3), (2, "down", 0), (2, "down", 1),
        (2, "down", 2), (2, "down", 3),
    ),
    sent0=(
        (3, "down", 0),
    ),
    sent1=(),
    sent2=(),
    sent3=(
        (4, "down", 0),
    ),
    arrived=(
        (5, "down", 0), (3, "down", 1), (2, "up", 0),
    ),
    between=(
        (3, "down", 2), (2, "up", 1),
    ),
    after=(
        (4, "down", 1), (3, "down", 3), (3, "up", 0), (2, "up", 2),
    ),
    part=(),
    dq1=(),
    dq2=(),
    dq3=(
        (6, "down", 0),
    ),
    out=(
        (1, "out", 0), (5, "down", 1), (4, "down", 2), (3, "up", 1), (2, "up", 3),
    ),
    wait0=(
        (5, "down", 2), (4, "down", 3), (4, "up", 0), (3, "up", 2),
    ),
    wait1=(
        (6, "down", 1), (5, "down", 3), (4, "up", 1), (3, "up", 3),
    ),
    wait2=(),
    wait3=(
        (5, "up", 0),
    ),
    qkv=(
        (1, "qkv", 0), (1, "qkv", 1), (1, "qkv", 2), (1, "qkv", 3), (6, "down", 2), (6, "up", 0),
        (4, "up", 2), (4, "up", 3), (2, "qkv", 0), (2, "out", 0),
    ),
    tail=(
        (6, "down", 3), (5, "up", 1), (3, "qkv", 0), (0, "tokens", 0), (3, "out", 0), (2, "qkv", 1),
        (6, "up", 1), (0, "vectors", 0), (5, "up", 2), (4, "qkv", 0), (4, "out", 0), (1, "tokens", 0),
        (3, "qkv", 1), (2, "qkv", 2), (6, "up", 2), (1, "vectors", 0), (5, "out", 0), (5, "up", 3),
        (4, "qkv", 1), (2, "vectors", 0), (3, "qkv", 2), (2, "qkv", 3), (6, "out", 0), (3, "vectors", 0),
        (6, "up", 3), (4, "qkv", 2), (3, "qkv", 3), (4, "vectors", 0), (4, "qkv", 3),
    ),
)


def dot(a, b):
    return lax.dot_general(a, b, (((1,), (0,)), ((), ())), preferred_element_type=F32)


def dot_nt(a, b):
    return lax.dot_general(a, b, (((1,), (1,)), ((), ())), preferred_element_type=F32)


def dot_tn(a, b):
    return lax.dot_general(a, b, (((0,), (0,)), ((), ())), preferred_element_type=F32)


def norm_stats(v):
    center = v - jnp.mean(v, -1, keepdims=True)
    rstd = lax.rsqrt(jnp.mean(center * center, -1, keepdims=True) + EPS)
    return center * rstd, rstd


def norm_back(dy, normed, rstd, gain):
    dn = dy * gain
    return rstd * (
        dn - jnp.mean(dn, -1, keepdims=True) - normed * jnp.mean(dn * normed, -1, keepdims=True)
    )


def col_sum(v):
    return jnp.sum(v, 0, keepdims=True)


def make_plan(cfg):
    C, W, B, D, FW, DW, DP, KVW, MW, R = (
        cfg.C, cfg.W, cfg.B, cfg.D, cfg.FW, cfg.DW, cfg.DP, cfg.KVW, cfg.MW, cfg.R)
    V = pltpu.VMEM
    dma = pltpu.SemaphoreType.DMA
    Q, HB = W * B, B // 2
    plan = dict(
        Xall=V((W, B, D), BF), Wc=V((D, MW), BF), Wq=V((DW, 3 * D), BF), Ws=V((W, DW, MW), BF), Vv=V((W, VROWS, DW), F32),
        Vs=V((8, D), F32), Out=V((W, DW, D), BF), Upc=V((D, FW), BF), Dn=V((FW, D), BF), UpT=V((FW, D), BF), DnT=V((D, FW), BF),
        OutT=V((D, D), BF), WcT=V((MW, D), BF), Cot=V((B, D), BF),
        KVs=V((W, B, KVW), BF), Qs=V((W, HB, KVW), BF), Rq=V((W, HB, KVW), BF), wide=V((B, DP), BF), KV=V((R * Q, KVW), BF),
        Qm=V((cfg.HW, Q, DP), BF), Dm=V((cfg.HW, Q, DP), BF),
        mrow=V((8, Q), F32), lrow=V((8, Q), F32), bias=V((8, MW), F32), upb=V((8, cfg.FW), F32), drow=V((8, Q), F32), OT=V((DW, Q), F32), dQT=V((DW, Q), F32),
        Os=V((W, HB, KVW), BF), Mix=V((W, HB, KVW), BF), MixT=V((W, HB, KVW), BF), mixed=V((B, D), BF),
        Mt=V((W, B, DW), BF),
        N1f=V((B, D), F32), n1=V((B, D), F32), n2=V((B, D), F32), r1=V((B, 1), F32),
        N1all=V((W, B, D), BF), Hp=V((W, B, FW), F32), Gs=V((W, B, FW), BF),
        Fs=V((W, B, D), BF), Fr=V((3, B, D), BF), dR2=V((B, D), F32), dFall=V((W, B, D), BF),
        dHs=V((W, B, FW), BF), dNs=V((W, B, D), BF), dNr=V((3, B, D), BF), dR1=V((B, D), F32),
        dAall=V((W, B, D), BF), dOs=V((W, HB, KVW), BF), dOr=V((W, HB, KVW), BF),
        dKVf=V((Q, KVW), F32), dKVs=V((R - 1, Q, KVW), BF), dKVr=V((R - 1, Q, KVW), BF),
        dKVo=V((W, B, KVW), BF), dQs=V((W, HB, KVW), BF), dQr=V((W, HB, KVW), BF), dqr=V((W, B, MW), BF), dxs=V((W, B, D), BF), dxr=V((3, B, D), BF),
        gv=V((GROWS, D), F32),
    )
    sems = dict(
        x=4, wq=4, wf=12, vv=4, ow=4, uw=4, own=6,
        q=W, kv=W, kf=(R - 1) * W, o=W, mt=4, n=8, f=6, df=8, dn=6, da=4, do=W, dkv=R - 1, dq=W, dk=W, dx=4,
    )
    recvs = dict(sems, kf=R * W)
    if cfg.keep:
        plan["Pm"] = V((cfg.HW, R * Q, Q), F32)
    if cfg.fused:
        plan.update(GX=V((W, B, FW), BF), DX=V((W, B, D // 2), BF))
        sems.update(gx=6, fx=4)
        recvs.update(gx=6, fx=4)
        for name, (pieces, ch, cols, to_rows) in cfg.grads.items():
            plan["G" + name] = V((pieces, 2, ch, cols) if name == "down" else (pieces, 2, 2, ch, cols), BF)
            plan["X" + name] = V((pieces, 3, ch, cols), BF)
            plan["T" + name] = V((pieces, 2, ch, cols), BF)
            plan["Y" + name] = V((pieces, 2, ch, cols), BF)
            plan["U" + name] = V((pieces, 2, ch, cols), BF)
            plan["Z" + name] = V((pieces, 2, ch, cols), BF)
            for kind in ("g1", "g2", "g3", "g4", "g5", "g6"):
                sems[kind + name] = 3 * pieces
                recvs[kind + name] = 3 * pieces
            if to_rows:
                plan["R" + name] = V((pieces, 2, ch, cols), BF)
        plan.update(Va=V((4, GROWS, D), F32), Vb=V((3, GROWS, D), F32), Vt=V((W, GROWS, DW), F32),
                    Vw=V((W, GROWS, DW), F32))
        sems.update(v1=3, vw=W)
        recvs.update(v1=3, vw=W)
    for name, n in sems.items():
        plan["s_" + name] = dma((n,))
    for name, n in recvs.items():
        plan["r_" + name] = dma((n,))
    return plan


class Sums:
    def __init__(self, cfg, m, c, w, send, arrive):
        self.cfg, self.m, self.c, self.w, self.send, self.arrive = cfg, m, c, w, send, arrive
        self.x, self.near = lax.rem(c, 2), lax.rem(lax.div(c, 2), 2)
        self.partners = [(jnp.bitwise_xor(c, k), w) for k in (1, 2, 4, 3)]
        self.other_middle = (jnp.bitwise_xor(c, 6), w)
        self.middle = self.near != lax.div(c, 4)
        self.end = jnp.logical_not(self.middle)
        self.long = (self.one, self.two, self.three, self.four, self.five, self.six, self.seven)
        self.halved = (self.nothing,) + self.long[1:]
        self.short = (self.quarters, self.quarters_sum, self.quarters_total, self.spread, self.spread_end)

    def stages(self, name):
        if name == "down":
            return self.halved
        return self.long if name in ("up", "down", "out") else self.short

    def step(self, k, name, p):
        if self.cfg.fused:
            self.stages(name)[k - 1](name, p)

    def run(self, place, others=None):
        if not self.cfg.fused:
            return
        for k, name, p in SCHEDULE[place]:
            if name in self.cfg.grads:
                self.step(k, name, p)
            else:
                others[name][k]()

    def finish(self):
        for name in ("down", "up", "out", "qkv"):
            for p in range(self.cfg.grads[name][0]):
                self.step(len(self.stages(name)), name, p)

    def ref(self, kind, name):
        return getattr(self.m, kind + name)

    def go(self, kind, name, p, src, dst, dev, pred=None):
        self.send(src, dst, self.ref("s_" + kind, name).at[p], self.ref("r_" + kind, name).at[p], dev, pred)

    def got(self, kind, name, p, dst, pred=None):
        self.arrive(dst, self.ref("r_" + kind, name).at[p], pred)

    def piece(self, name, k):
        return jnp.bitwise_xor(self.w, k) if self.cfg.grads[name][3] else k

    def nothing(self, name, k):
        pass

    def half(self, name, k):
        if name == "down":
            return self.ref("G", name)[k].astype(F32)
        other = self.ref("X", name).at[k, pl.ds(0, 2)]
        self.got("g1", name, k, other)
        return self.ref("G", name)[self.piece(name, k), self.x].astype(F32) + other[...].astype(F32)

    def one(self, name, k):
        p = self.piece(name, k)
        self.go("g1", name, k, self.ref("G", name).at[p, 1 - self.x], self.ref("X", name).at[k, pl.ds(0, 2)],
                self.partners[0])

    def two(self, name, k):
        t = self.ref("T", name)

        @pl.when(self.end)
        def _():
            t[k] = self.half(name, k).astype(BF)

        self.go("g2", name, k, t.at[k], self.ref("Y", name).at[k], self.partners[1], self.end)

    def three(self, name, k):
        y, u = self.ref("Y", name), self.ref("U", name)

        @pl.when(self.middle)
        def _():
            mine = self.half(name, k)
            self.got("g2", name, k, y.at[k])
            u[k] = (mine + y[k].astype(F32)).astype(BF)

        self.go("g3", name, k, u.at[k], self.ref("Z", name).at[k], self.other_middle, self.middle)

    def four(self, name, k):
        u, z, fin = (self.ref(kind, name) for kind in "UZF")
        away = self.cfg.grads[name][3] and k > 0

        @pl.when(self.middle)
        def _():
            self.got("g3", name, k, z.at[k])
            total = (u[k].astype(F32) + z[k].astype(F32)).astype(BF)
            if away:
                self.ref("R", name)[k] = total
            else:
                fin[self.piece(name, k), self.x] = total

        if away:
            self.go("g4", name, k, self.ref("R", name).at[k], fin.at[self.w, self.x],
                    (self.c, jnp.bitwise_xor(self.w, k)), self.middle)

    def five(self, name, k):
        here = self.ref("F", name).at[self.piece(name, k), self.x]
        if self.cfg.grads[name][3] and k > 0:
            self.got("g4", name, k, here, self.middle)
        self.go("g5", name, k, here, here, self.partners[1], self.middle)
        self.go("g6", name, k, here, here, self.partners[0], self.middle)

    def six(self, name, k):
        here = self.ref("F", name).at[self.piece(name, k), self.x]
        self.got("g5", name, k, here, self.end)
        self.go("g6", name, k, here, here, self.partners[0], self.end)

    def seven(self, name, k):
        self.got("g6", name, k, self.ref("F", name).at[self.piece(name, k), 1 - self.x])

    def quarters_total(self, name, k):
        u, z, fin = (self.ref(kind, name) for kind in "UZF")
        self.got("g3", name, k, z.at[k, 0])
        total = (u[k, 0].astype(F32) + z[k, 0].astype(F32)).astype(BF)
        if not self.cfg.grads[name][3] or k == 0:
            fin[self.piece(name, k), self.x, self.near] = total
            return
        done = self.ref("R", name)
        done[k, 0] = total
        self.go("g4", name, k, done.at[k, 0], fin.at[self.w, self.x, self.near], (self.c, jnp.bitwise_xor(self.w, k)))

    def owned(self, name, k):
        here = self.ref("F", name).at[self.piece(name, k), self.x, self.near]
        if self.cfg.grads[name][3] and k > 0:
            self.got("g4", name, k, here)
        return here

    def three_others(self):
        x, n = self.x, self.near
        return ((1 - x, n, self.partners[0]), (x, 1 - n, self.partners[1]), (1 - x, 1 - n, self.partners[3]))

    def quarters(self, name, k):
        p = self.piece(name, k)
        for i, (x, n, dev) in enumerate(self.three_others()):
            self.go("g1", name, 3 * k + i, self.ref("G", name).at[p, x, n], self.ref("X", name).at[k, i], dev)

    def quarters_sum(self, name, k):
        total = self.ref("G", name)[self.piece(name, k), self.x, self.near].astype(F32)
        for i in range(3):
            other = self.ref("X", name).at[k, i]
            self.got("g1", name, 3 * k + i, other)
            total = total + other[...].astype(F32)
        u = self.ref("U", name)
        u[k, 0] = total.astype(BF)
        self.go("g3", name, k, u.at[k, 0], self.ref("Z", name).at[k, 0], self.partners[2])

    def spread(self, name, k):
        here = self.owned(name, k)
        for i, (_, _, dev) in enumerate(self.three_others()):
            self.go("g5", name, 3 * k + i, here, here, dev)

    def spread_end(self, name, k):
        p = self.piece(name, k)
        for i, (x, n, _) in enumerate(self.three_others()):
            self.got("g5", name, 3 * k + i, self.ref("F", name).at[p, x, n])


def layer_kernel(cfg, names, n_in, *refs):
    (x_ref, cot_ref, qkv_ref, out_ref, up_ref, down_ref, len_ref, *vec_refs) = refs[:n_in]
    y_ref, gx_ref, gqkv_ref, gout_ref, gup_ref, gdown_ref, gvec_ref = refs[n_in : n_in + 7]
    m = SimpleNamespace(**dict(zip(names, refs[n_in + 7 :])))
    if cfg.fused:
        m.Fqkv, m.Fout, m.Fup, m.Fdown = gqkv_ref, gout_ref, gup_ref, gdown_ref
    C, W, B, D, DW, DP, KVW, MW, R, HW = (
        cfg.C, cfg.W, cfg.B, cfg.D, cfg.DW, cfg.DP, cfg.KVW, cfg.MW, cfg.R, cfg.HW)
    OFF = DP - DW
    Q, HB = W * B, B // 2
    c = lax.axis_index("ctx")
    w = lax.axis_index("wa")
    block_part = lax.rem(c, R)
    block_slot = lax.div(c, R)
    s = lax.div(c, R)
    low = lax.rem(c, R)
    g_att = lax.div(w, 2) * 2 + lax.rem(low, 2)
    r_att = lax.div(low, 2) * 2 + lax.rem(w, 2)

    def att_device(t, g, r):
        return (t * R + lax.div(r, 2) * 2 + lax.rem(g, 2), lax.div(g, 2) * 2 + lax.rem(r, 2))

    def is_me(dev):
        return jnp.logical_and(dev[0] == c, dev[1] == w)

    drains = []

    def remote(src, dst, ss, rs, dev):
        return pltpu.make_async_remote_copy(
            src_ref=src, dst_ref=dst, send_sem=ss, recv_sem=rs, device_id=dev, device_id_type=MESH)

    def send(src, dst, ss, rs, dev, pred=None):
        def go():
            remote(src, dst, ss, rs, dev).start()

        def end():
            remote(src, dst, ss, rs, dev).wait_send()

        if pred is None:
            go()
        else:
            pl.when(pred)(go)
        drains.append((pred, end))

    def arrive(dst, rs, pred=None):
        def go():
            remote(dst, dst, rs, rs, (c, w)).wait_recv()

        if pred is None:
            go()
        else:
            pl.when(pred)(go)

    barrier = pltpu.get_barrier_semaphore()

    def greet(i, carry):
        ci, wi = lax.div(i, W), lax.rem(i, W)

        @pl.when(jnp.logical_not(is_me((ci, wi))))
        def _():
            pl.semaphore_signal(barrier, inc=1, device_id=(ci, wi), device_id_type=MESH)

        return carry

    lax.fori_loop(0, C * W, greet, 0)

    def entered():
        pl.semaphore_wait(barrier, C * W - 1)

    def peer(k):
        return (c, jnp.bitwise_xor(w, k))

    def gather_start(buf, ss, rs, parts=1):
        n = buf.shape[1] // parts
        for h in range(parts):
            rows = buf.at[w, pl.ds(h * n, n)]
            send(rows, rows, ss.at[2 * parts + h], rs.at[2 * parts + h], peer(2))
        send(buf.at[w], buf.at[w], ss.at[1], rs.at[1], peer(1))

    def gather_wait(buf, ss, rs, k, h=0, parts=1):
        n = buf.shape[1] // parts
        t = jnp.bitwise_xor(w, k)
        if k == 1:
            arrive(buf.at[t], rs.at[1])
            return
        rows = buf.at[t, pl.ds(h * n, n)]
        arrive(rows, rs.at[k * parts + h])
        if k == 2:
            send(rows, rows, ss.at[3 * parts + h], rs.at[3 * parts + h], peer(1))

    def take(ref, blocks):
        parts = [ref[t, rows, :] for t, rows in blocks]
        return jnp.concatenate(parts, 0) if len(parts) > 1 else parts[0]

    def put(ref, blocks, value):
        n = value.shape[0] // len(blocks)
        for i, (t, rows) in enumerate(blocks):
            ref[t, rows, :] = value[i * n : (i + 1) * n].astype(ref.dtype)

    def feed(buf, sems, work, part, stage, recv, sum_sems, idle, early=None, late=None):
        (ss, rs), (ss2, rs2) = sems, sum_sems
        t3, t2, t1 = (jnp.bitwise_xor(w, k) for k in (3, 2, 1))
        every = pl.ds(0, B)
        halves = [pl.ds(h * HB, HB) for h in range(2)]
        mine = [None, None]

        def across(h):
            rows = halves[h]
            arrive(recv.at[1, rows], rs2.at[2 + h])
            stage[t2, rows, :] = (mine[h] + recv[1, rows, :].astype(F32)).astype(BF)
            send(stage.at[t2, rows], recv.at[2, rows], ss2.at[4 + h], rs2.at[4 + h], peer(2))

        gather_start(buf, ss, rs, 2)
        work([(w, every)])
        gather_wait(buf, ss, rs, 1, 0, 2)
        work([(t1, every)])
        idle()
        for h, rows in enumerate(halves):
            gather_wait(buf, ss, rs, 2, h, 2)
            if h:
                across(0)
            gather_wait(buf, ss, rs, 3, h, 2)
            work([(t3, rows), (t2, rows)])
            both = part([(t3, rows), (t2, rows)])
            stage[t3, rows, :] = both[0:HB].astype(BF)
            send(stage.at[t3, rows], recv.at[1, rows], ss2.at[2 + h], rs2.at[2 + h], peer(1))
            mine[h] = both[HB:]
        stage[t1] = part([(t1, every)]).astype(BF)
        send(stage.at[t1], recv.at[0], ss2.at[0], rs2.at[0], peer(1))
        if early:
            early()
        across(1)
        own = part([(w, every)])
        arrive(recv.at[0], rs2.at[0])
        own = own + recv[0].astype(F32)
        if late:
            late()
        for h, rows in enumerate(halves):
            arrive(recv.at[2, rows], rs2.at[4 + h])
        return own + recv[2].astype(F32)

    def scatter_steps(part, stage, recv, ss, rs):
        t3, t2, t1 = (jnp.bitwise_xor(w, k) for k in (3, 2, 1))

        def first():
            stage[t3] = part(t3).astype(BF)
            send(stage.at[t3], recv.at[1], ss.at[1], rs.at[1], peer(1))
            stage[t1] = part(t1).astype(BF)
            send(stage.at[t1], recv.at[0], ss.at[0], rs.at[0], peer(1))

        def second():
            mine2 = part(t2)
            arrive(recv.at[1], rs.at[1])
            stage[t2] = (mine2 + recv[1].astype(F32)).astype(BF)
            send(stage.at[t2], recv.at[2], ss.at[2], rs.at[2], peer(2))

        def third():
            own = part(w)
            arrive(recv.at[0], rs.at[0])
            own = own + recv[0].astype(F32)
            arrive(recv.at[2], rs.at[2])
            return own + recv[2].astype(F32)

        return first, second, third

    def pack(ref, value):
        ref[:, 0:DW] = value[0:HB].astype(BF)
        ref[:, DW:KVW] = value[HB:B].astype(BF)

    def unpack(ref, lane, packed):
        ref[0:HB, lane : lane + DW] = packed[:, 0:DW]
        ref[HB:B, lane : lane + DW] = packed[:, DW:KVW]

    def local(src, dst, sem):
        cp = pltpu.make_async_copy(src, dst, sem)
        cp.start()
        return cp

    rows_w = pl.ds(w * DW, DW)
    own = [
        local(qkv_ref, m.Wq, m.s_own.at[0]),
        local(x_ref, m.Xall.at[w], m.s_own.at[1]),
        local(out_ref, m.Out.at[w], m.s_own.at[2]),
        local(up_ref.at[:, pl.ds(pl.multiple_of(w * cfg.FW, cfg.FW), cfg.FW)], m.Upc.at[rows_w], m.s_own.at[3]),
        local(down_ref, m.Dn, m.s_own.at[4]),
        local(cot_ref, m.Cot, m.s_own.at[5]),
    ]
    own[0].wait()
    for g in range(W):
        for i, third in enumerate((1, 2, 0)):
            a = third * D + g * DW
            m.Ws[g, :, i * DW : (i + 1) * DW] = m.Wq[:, a : a + DW]
        m.Ws[g, :, 3 * DW : MW] = jnp.zeros((DW, MW - 3 * DW), BF)
    row = 0
    for ref in vec_refs:
        v = ref[...].astype(F32)
        for i in range(v.shape[0] // DW):
            m.Vv[w, row : row + 1, :] = v[i * DW : (i + 1) * DW].reshape(1, DW)
            row += 1
    m.Vv[w, row:VROWS, :] = jnp.full((VROWS - row, DW), len_ref[0].astype(F32))
    own[1].wait()
    entered()

    def part_rows(t, part, parts):
        return pl.ds(pl.multiple_of(t * DW + part * (DW // parts), 16), DW // parts)

    quarter = lax.rem(c, 4)

    def near_me(k):
        return (jnp.bitwise_xor(c, k), w)

    for k in (2, 3):
        send(m.Ws.at[jnp.bitwise_xor(w, k), part_rows(0, quarter, 4)], m.Wc.at[part_rows(w, quarter, 4)],
             m.s_wq.at[k], m.r_wq.at[k], peer(k))
    gather_start(m.Xall, m.s_x, m.r_x)
    send(m.Ws.at[jnp.bitwise_xor(w, 1)], m.Wc.at[rows_w], m.s_wq.at[1], m.r_wq.at[1], peer(1))
    for k in (2, 3, 1):
        send(m.Vv.at[w], m.Vv.at[w], m.s_vv.at[k], m.r_vv.at[k], peer(k))
    m.Wc[rows_w, :] = m.Ws[w]
    m.wide[...] = jnp.zeros(m.wide.shape, BF)
    m.bias[...] = jnp.zeros(m.bias.shape, F32)
    for cp in own[2:]:
        cp.wait()
    m.DnT[...] = m.Dn[...].T
    for k in (2, 3):
        rows = m.Wc.at[part_rows(jnp.bitwise_xor(w, k), quarter, 4)]
        arrive(rows, m.r_wq.at[k])
        for i in (1, 2, 3):
            e = 3 * (k - 2) + i - 1
            send(rows, rows, m.s_wf.at[e], m.r_wf.at[e], near_me(i))
    for k in (1, 2, 3):
        gather_wait(m.Xall, m.s_x, m.r_x, k)
    arrive(m.Wc.at[pl.ds(jnp.bitwise_xor(w, 1) * DW, DW)], m.r_wq.at[1])
    for k in (1, 2, 3):
        arrive(m.Vv.at[jnp.bitwise_xor(w, k)], m.r_vv.at[k])
    gather_start(m.Out, m.s_ow, m.r_ow)
    for k in (2, 3, 1):
        cols = pl.ds(pl.multiple_of(jnp.bitwise_xor(w, k) * cfg.FW, cfg.FW), cfg.FW)
        send(up_ref.at[:, cols], m.Upc.at[rows_w], m.s_uw.at[k], m.r_uw.at[k], peer(k))
    for k in (2, 3):
        for i in (1, 2, 3):
            e = 3 * (k - 2) + i - 1
            arrive(m.Wc.at[part_rows(jnp.bitwise_xor(w, k), jnp.bitwise_xor(quarter, i), 4)], m.r_wf.at[e])

    for t in range(W):
        m.Vs[0:6, t * DW : (t + 1) * DW] = m.Vv[t, 0:6, :]
        m.upb[0:1, t * DW : (t + 1) * DW] = m.Vv[w, UPB + t : UPB + t + 1, :]
    upper, odd = lax.div(w, 2), lax.rem(w, 2)
    m.bias[0:1, DW : 2 * DW] = m.Vv[W // 2 + upper, pl.ds(QVB + odd, 1), :]
    m.bias[0:1, 2 * DW : 3 * DW] = m.Vv[upper, pl.ds(QVB + odd, 1), :]
    bias = m.bias[0:1, :]

    def vec(row):
        return m.Vs[row : row + 1, :]

    kv_rows = pl.ds(pl.multiple_of(block_part * Q + block_slot * B, B), B)
    order = [lax.rem(s + 1 + k, W) for k in range(W)]
    for k, t in enumerate(order):
        qkv = dot(m.Xall[t], m.Wc[...]) + bias
        m.KVs[t] = qkv[:, 0:KVW].astype(BF)
        pack(m.Qs.at[t], qkv[:, KVW : KVW + DW])
        dev = att_device(t, w, block_part)
        send(m.Qs.at[t], m.Rq.at[block_slot], m.s_q.at[k], m.r_q.at[block_slot], dev, jnp.logical_not(is_me(dev)))
    for k, t in enumerate(order):
        dev = att_device(t, w, block_part)
        send(m.KVs.at[t], m.KV.at[kv_rows], m.s_kv.at[k], m.r_kv.at[block_slot], dev, jnp.logical_not(is_me(dev)))

        @pl.when(is_me(dev))
        def _():
            m.Rq[block_slot] = m.Qs[t]
            m.KV[kv_rows, :] = m.KVs[t]

    lanes = lax.broadcasted_iota(jnp.int32, (1, DP), 1)

    def q_lane(h):
        return jnp.logical_and(lanes >= h * HEAD, lanes < (h + 1) * HEAD)

    def v_lane(h):
        return jnp.logical_and(lanes >= OFF + h * HEAD, lanes < OFF + (h + 1) * HEAD)

    for j in range(W):
        arrive(m.Rq.at[j], m.r_q.at[j], jnp.logical_not(is_me((j * R + r_att, g_att))))
        unpack(m.wide, 0, m.Rq.at[j])
        q = m.wide[...] * jnp.asarray(HEAD**-0.5, BF)
        for h in range(HW):
            m.Qm[h, j * B : (j + 1) * B, :] = jnp.where(q_lane(h), q, jnp.zeros_like(q))

    KC = 2 * B
    PER_SET = Q // KC
    len_s = m.Vv[s, LEN : LEN + 1, 0:1]

    def alive(chunk):
        r, half = lax.div(chunk, PER_SET), lax.rem(chunk, PER_SET)
        row = lax.broadcasted_iota(jnp.int32, (KC, Q), 0)
        later = (row >= B).astype(jnp.int32)
        place = ((2 * half + later) * R + r) * B + row - later * B
        return place.astype(F32) < len_s

    m.mrow[...] = jnp.full(m.mrow.shape, FLOOR, F32)
    m.lrow[...] = jnp.zeros(m.lrow.shape, F32)
    m.OT[...] = jnp.zeros(m.OT.shape, F32)

    def attend(chunk, carry):
        rows = pl.ds(pl.multiple_of(chunk * KC, KC), KC)
        keys = m.KV[rows, 0:DP]
        values_t = m.KV[rows, KVW - DP : KVW].T
        live = alive(chunk)
        for h in range(HW):
            scores = jnp.where(live, dot_nt(keys, m.Qm[h]), FLOOR)
            top = m.mrow[h : h + 1, :]
            new_top = jnp.maximum(top, jnp.max(scores, 0, keepdims=True))
            prob = jnp.exp(scores - new_top)
            factor = jnp.exp(top - new_top)
            m.mrow[h : h + 1, :] = new_top
            m.lrow[h : h + 1, :] = m.lrow[h : h + 1, :] * factor + col_sum(prob)
            a, b = h * HEAD, (h + 1) * HEAD
            m.OT[a:b, :] = m.OT[a:b, :] * factor + dot(values_t[OFF + a : OFF + b, :], prob.astype(BF))
        return carry

    for i in range(PER_SET):
        pair = jnp.bitwise_xor(lax.div(s, 2), i)
        for e in range(2):
            j = 2 * pair + e
            rows = m.KV.at[pl.ds(pl.multiple_of(r_att * Q + j * B, B), B)]
            arrive(rows, m.r_kv.at[j], jnp.logical_not(is_me((j * R + r_att, g_att))))
            for k in range(1, R):
                send(rows, rows, m.s_kf.at[(k - 1) * W + 2 * i + e], m.r_kf.at[r_att * W + j],
                     att_device(s, g_att, lax.rem(r_att + k, R)))
        attend(r_att * PER_SET + pair, 0)
        if i == 0:
            gather_wait(m.Out, m.s_ow, m.r_ow, 2)

        def others(k, carry):
            r = lax.rem(r_att + k, R)
            for e in range(2):
                j = 2 * pair + e
                arrive(m.KV.at[pl.ds(pl.multiple_of(r * Q + j * B, B), B)], m.r_kf.at[r * W + j])
            return attend(r * PER_SET + pair, carry)

        lax.fori_loop(1, R, others, 0)
    for h in range(HW):
        a, b = h * HEAD, (h + 1) * HEAD
        m.OT[a:b, :] = m.OT[a:b, :] / m.lrow[h : h + 1, :]
    m.lrow[0:HW, :] = m.mrow[0:HW, :] + jnp.log(m.lrow[0:HW, :])
    for j in range(W):
        pack(m.Os.at[j], m.OT[:, j * B : (j + 1) * B].T)
        dev = (j * R + r_att, s)
        send(m.Os.at[j], m.Mix.at[g_att], m.s_o.at[j], m.r_o.at[g_att], dev, jnp.logical_not(is_me(dev)))

        @pl.when(is_me(dev))
        def _():
            m.Mix[g_att] = m.Os[j]

    for k in (1, 3):
        gather_wait(m.Out, m.s_ow, m.r_ow, k)
    out_weight = m.Out[...].reshape(D, D)
    resid = m.Xall[w].astype(F32) + vec(OUTB)
    for g in range(W):
        arrive(m.Mix.at[g], m.r_o.at[g], jnp.logical_not(is_me(att_device(w, g, block_part))))
        unpack(m.mixed, g * DW, m.Mix.at[g])
    resid = resid + dot(m.mixed[...], out_weight)
    n1, r1 = norm_stats(resid)
    m.n1[...] = n1
    m.r1[...] = r1
    n1_full = n1 * vec(GAIN1) + vec(SHIFT1)
    m.N1f[...] = n1_full
    m.N1all[w] = n1_full.astype(BF)

    for k in (1, 2, 3):
        arrive(m.Upc.at[pl.ds(jnp.bitwise_xor(w, k) * DW, DW)], m.r_uw.at[k])
    up_bias = m.upb[0:1, :]

    activated = []

    def expand(blocks):
        h = dot(take(m.N1all, blocks), m.Upc[...]) + up_bias
        phi = 0.5 * (1.0 + lax.erf(h * (2.0**-0.5)))
        put(m.Gs, blocks, h * phi)
        put(m.Hp, blocks, phi + h * ((2.0 * math.pi) ** -0.5) * jnp.exp(-0.5 * h * h))
        if cfg.fused:
            for t, rows in blocks:
                i = len(activated)
                activated.append((t, rows))
                send(m.Gs.at[t, rows], m.GX.at[t, rows], m.s_gx.at[i], m.r_gx.at[i], near_me(1))

    def turn_weights():
        m.UpT[...] = m.Upc[...].T
        m.OutT[...] = m.Out[...].reshape(D, D).T

    ffn = feed(m.N1all, (m.s_n, m.r_n), expand, lambda blocks: dot(take(m.Gs, blocks), m.Dn[...]), m.Fs, m.Fr,
               (m.s_f, m.r_f), turn_weights)
    n2, r2 = norm_stats(m.N1f[...] + ffn + vec(DOWNB))
    m.n2[...] = n2
    y_ref[...] = (n2 * vec(GAIN2) + vec(SHIFT2)).astype(BF)

    place = c * B + lax.broadcasted_iota(jnp.int32, (B, D), 0)
    dy = jnp.where(place.astype(F32) < m.Vv[w, LEN : LEN + 1, 0:1], m.Cot[...].astype(F32), 0.0)
    d_r2 = norm_back(dy, n2, r2, vec(GAIN2))
    m.dR2[...] = d_r2
    m.dFall[w] = d_r2.astype(BF)

    def shrink(blocks):
        put(m.dHs, blocks, dot(take(m.dFall, blocks), m.DnT[...]) * take(m.Hp, blocks))

    def flat(ref):
        return ref[...].reshape(Q, ref.shape[-1])

    def put_grad(name, plain, lhs, rhs, parts):
        rows = lhs.shape[-1] // parts
        for i in range(parts):
            val = dot_tn(lhs[:, :, i * rows : (i + 1) * rows].reshape(Q, rows), flat(rhs)).astype(BF)
            if cfg.fused:
                _, ch, cols, _ = cfg.grads[name]
                n = rows // (4 * ch)
                getattr(m, "G" + name)[i * n : (i + 1) * n] = val.reshape(n, 2, 2, ch, cols)
            else:
                plain[i * rows : (i + 1) * rows, :] = val

    pump = Sums(cfg, m, c, w, send, arrive)

    side = lax.rem(c, 2)

    def half_cols(side):
        return pl.ds(pl.multiple_of(side * (D // 2), 128), D // 2)

    def down_half():
        for i, k in enumerate((0, 2)):
            rows = m.DX.at[jnp.bitwise_xor(w, k)]
            arrive(rows, m.r_fx.at[i])
            send(rows, rows, m.s_fx.at[2 + i], m.r_fx.at[2 + i], peer(1))
        for i, (t, rows) in enumerate(activated):
            arrive(m.GX.at[t, rows], m.r_gx.at[i])
        for i, k in enumerate((1, 3)):
            arrive(m.DX.at[jnp.bitwise_xor(w, k)], m.r_fx.at[2 + i])
        pieces, ch, cols, _ = cfg.grads["down"]
        n = cfg.FW // 2
        here = m.dFall[:, :, half_cols(side)].reshape(Q, cols)
        there = flat(m.DX)
        for i in range(2):
            at = slice(i * n, (i + 1) * n)
            val = dot_tn(m.Gs[:, :, at].reshape(Q, n), here) + dot_tn(m.GX[:, :, at].reshape(Q, n), there)
            m.Gdown[i * (pieces // 2) : (i + 1) * (pieces // 2)] = val.astype(BF).reshape(pieces // 2, 2, ch, cols)

    def early():
        if cfg.fused:
            for i, k in enumerate((0, 2)):
                t = jnp.bitwise_xor(w, k)
                send(m.dFall.at[t, :, half_cols(1 - side)], m.DX.at[t], m.s_fx.at[i], m.r_fx.at[i], near_me(1))
        else:
            put_grad("down", gdown_ref, m.Gs, m.dFall, 2)
        pump.run("early")

    def late():
        m.gv[2:3, :] = col_sum(dy * n2)
        m.gv[3:4, :] = col_sum(dy)
        m.gv[5:6, :] = col_sum(m.dFall[w].astype(F32))
        put_grad("up", gup_ref, m.N1all, m.dHs, 2)
        m.gv[6:7, :] = col_sum(flat(m.dHs).astype(F32))
        pump.run("norm")

    def turn_projection():
        m.WcT[...] = m.Wc[...].T

    d_n1 = feed(m.dFall, (m.s_df, m.r_df), shrink, lambda blocks: dot(take(m.dHs, blocks), m.UpT[...]), m.dNs, m.dNr,
                (m.s_dn, m.r_dn), turn_projection, early, late) + m.dR2[...]
    n1 = m.n1[...]
    d_r1 = norm_back(d_n1, n1, m.r1[...], vec(GAIN1))
    m.dR1[...] = d_r1
    d_a = d_r1.astype(BF)
    m.dAall[w] = d_a
    d_mixed = dot(d_a, m.OutT[...])
    for g in range(W):
        pack(m.dOs.at[g], d_mixed[:, g * DW : (g + 1) * DW])
        dev = att_device(w, g, block_part)
        send(m.dOs.at[g], m.dOr.at[block_slot], m.s_do.at[g], m.r_do.at[block_slot], dev,
             jnp.logical_not(is_me(dev)))

        @pl.when(is_me(dev))
        def _():
            m.dOr[block_slot] = m.dOs[g]

    pump.run("sent")
    gather_start(m.dAall, m.s_da, m.r_da)
    for k in (2, 3, 1):
        send(m.Mix.at[jnp.bitwise_xor(w, k)], m.MixT.at[w], m.s_mt.at[k], m.r_mt.at[k], peer(k))
    if cfg.fused:
        down_half()
    pump.run("down")
    m.MixT[w] = m.Mix[w]
    m.gv[0:1, :] = col_sum(d_n1 * n1)
    m.gv[1:2, :] = col_sum(d_n1)
    m.gv[4:5, :] = col_sum(d_a.astype(F32))

    m.wide[...] = jnp.zeros(m.wide.shape, BF)

    def weights_again(chunk, h):
        rows = pl.ds(pl.multiple_of(chunk * KC, KC), KC)
        scores = dot_nt(m.KV[rows, 0:DP], m.Qm[h])
        return jnp.where(alive(chunk), jnp.exp(scores - m.lrow[h : h + 1, :]), 0.0)

    if cfg.keep:

        def keep(chunk, carry):
            for h in range(HW):
                m.Pm[h, pl.ds(pl.multiple_of(chunk * KC, KC), KC), :] = weights_again(chunk, h)
            return carry

        lax.fori_loop(0, R * PER_SET, keep, 0)
    for j in range(W):
        pump.run("sent%d" % j)
        arrive(m.dOr.at[j], m.r_do.at[j], jnp.logical_not(is_me((j * R + r_att, s))))
        unpack(m.wide, OFF, m.dOr.at[j])
        d_o = m.wide[...]
        cols = slice(j * B, (j + 1) * B)
        for h in range(HW):
            m.Dm[h, cols, :] = jnp.where(v_lane(h), d_o, jnp.zeros_like(d_o))
        prod = m.OT[:, cols] * d_o.astype(F32).T[OFF:DP, :]
        for h in range(HW):
            m.drow[h : h + 1, cols] = col_sum(prod[h * HEAD : (h + 1) * HEAD, :])
    m.dQT[...] = jnp.zeros(m.dQT.shape, F32)
    pump.run("arrived")

    def attend_back(step, carry):
        chunk = lax.rem((r_att + 1) * PER_SET + step, R * PER_SET)
        rows = pl.ds(pl.multiple_of(chunk * KC, KC), KC)
        keys = m.KV[rows, 0:DP]
        values = m.KV[rows, KVW - DP : KVW]
        keys_t = keys.T
        d_k = jnp.zeros((KC, DP), F32)
        d_v = jnp.zeros((KC, DP), F32)
        for h in range(HW):
            prob = m.Pm[h, rows, :] if cfg.keep else weights_again(chunk, h)
            d_prob = dot_nt(values, m.Dm[h])
            d_s = (prob * (d_prob - m.drow[h : h + 1, :])).astype(BF)
            d_k = d_k + dot(d_s, m.Qm[h])
            d_v = d_v + dot(prob.astype(BF), m.Dm[h])
            a, b = h * HEAD, (h + 1) * HEAD
            m.dQT[a:b, :] = m.dQT[a:b, :] + dot(keys_t[a:b, :], d_s)
        lead = KVW - DP
        d_kv = jnp.concatenate([d_k[:, 0:lead], d_k[:, lead:] + d_v[:, 0 : DP - lead], d_v[:, DP - lead :]], 1)
        place, part = lax.div(step, PER_SET), lax.rem(step, PER_SET)
        rows = pl.ds(pl.multiple_of(part * KC, KC), KC)
        if carry is None:
            m.dKVf[rows, :] = d_kv
        else:
            m.dKVs[place, rows, :] = d_kv.astype(BF)
        return carry

    lax.fori_loop(0, (R - 1) * PER_SET, attend_back, 0)
    for k in range(1, R):
        send(m.dKVs.at[k - 1], m.dKVr.at[R - k - 1], m.s_dkv.at[k - 1], m.r_dkv.at[R - k - 1],
             att_device(s, g_att, lax.rem(r_att + k, R)))
    pump.run("between")
    lax.fori_loop((R - 1) * PER_SET, R * PER_SET, attend_back, None)
    pump.run("after")
    pump.run("part")
    for k in range(1, R):
        arrive(m.dKVr.at[k - 1], m.r_dkv.at[k - 1])
    for j in range(W):
        d_kv = m.dKVf[j * B : (j + 1) * B, :]
        for k in range(1, R):
            d_kv = d_kv + m.dKVr[k - 1, j * B : (j + 1) * B, :].astype(F32)
        m.dKVo[j] = d_kv.astype(BF)
        pack(m.dQs.at[j], m.dQT[:, j * B : (j + 1) * B].T * (HEAD**-0.5))
        dev = (j * R + r_att, g_att)
        away = jnp.logical_not(is_me(dev))
        send(m.dKVo.at[j], m.dqr.at[s, :, pl.ds(0, KVW)], m.s_dk.at[j], m.r_dk.at[s], dev, away)
        send(m.dQs.at[j], m.dQr.at[s], m.s_dq.at[j], m.r_dq.at[s], dev, away)

        @pl.when(is_me(dev))
        def _():
            m.dqr[s, :, 0:KVW] = m.dKVo[j]
            m.dQr[s] = m.dQs[j]

    for k in (1, 2, 3):
        pump.run("dq%d" % k)
        gather_wait(m.dAall, m.s_da, m.r_da, k)
        arrive(m.MixT.at[jnp.bitwise_xor(w, k)], m.r_mt.at[k])
    for t in range(W):
        unpack(m.Mt.at[t], 0, m.MixT.at[t])
        m.dqr[t, :, KVW + DW : MW] = jnp.zeros((B, MW - KVW - DW), BF)
    put_grad("out", gout_ref, m.Mt, m.dAall, 1)
    pump.run("out")

    for t in range(W):
        pump.run("wait%d" % t)
        away = jnp.logical_not(is_me(att_device(t, w, block_part)))
        arrive(m.dqr.at[t, :, pl.ds(0, KVW)], m.r_dk.at[t], away)
        arrive(m.dQr.at[t], m.r_dq.at[t], away)
        unpack(m.dqr.at[t], KVW, m.dQr.at[t])
    put_grad("qkv", gqkv_ref, m.Xall, m.dqr, 2)
    pump.run("qkv")

    m.gv[7:8, 0:MW] = col_sum(flat(m.dqr).astype(F32))
    m.gv[7:8, MW:D] = jnp.zeros((1, D - MW), F32)

    def d_x(t):
        return dot(m.dqr[t], m.WcT[...])

    token_steps = scatter_steps(d_x, m.dxs, m.dxr, m.s_dx, m.r_dx)

    def vectors(i):
        if i:
            arrive(m.Vb.at[i - 1], m.r_v1.at[i - 1])
            m.Va[i] = m.Va[i - 1] + m.Vb[i - 1]
        else:
            m.Va[0] = m.gv[...]
        if i < 3:
            send(m.Va.at[i], m.Vb.at[i], m.s_v1.at[i], m.r_v1.at[i], pump.partners[i])

    def vectors_to_rows():
        vectors(3)
        total = m.Va[3]
        for t in range(W):
            m.Vt[t, 0:6, :] = total[0:6, t * DW : (t + 1) * DW]
            m.Vt[t, 6:7, :] = total[7:8, 2 * DW : 3 * DW]
            m.Vt[t, 7:8, :] = total[7:8, DW : 2 * DW]
        m.Vw[w] = m.Vt[w]
        for k in (2, 3, 1):
            send(m.Vt.at[jnp.bitwise_xor(w, k)], m.Vw.at[w], m.s_vw.at[k], m.r_vw.at[k], peer(k))
        gvec_ref[7:8, :] = total[6:7, :]

    def vectors_end():
        for k in (1, 2, 3):
            arrive(m.Vw.at[jnp.bitwise_xor(w, k)], m.r_vw.at[k])
        gvec_ref[0:6, 0:DW] = m.Vw[0, 0:6, :] + m.Vw[1, 0:6, :] + m.Vw[2, 0:6, :] + m.Vw[3, 0:6, :]
        for i in range(2):
            gvec_ref[6:7, i * DW : (i + 1) * DW] = m.Vw[2 * odd + i, pl.ds(6 + upper, 1), :]

    steps = [functools.partial(vectors, i) for i in range(3)] + [vectors_to_rows, vectors_end]

    if not cfg.fused:
        for step in token_steps[:-1]:
            step()
        d_x_sum = token_steps[-1]()
        gvec_ref[0] = m.gv[...]
    else:
        vector_steps = [functools.partial(vectors, i) for i in range(3)] + [vectors_to_rows, vectors_end]
        pump.run("tail", dict(tokens=token_steps, vectors=vector_steps))
        pump.finish()
        d_x_sum = token_steps[2]()
    gx_ref[...] = (m.dR1[...] + d_x_sum).astype(BF)

    for pred, end in drains:
        if pred is None:
            end()
        else:
            pl.when(pred)(end)


def body(C, W, tokens, lengths, qkv_weight, out_weight, up_weight, down_weight, qv_bias, out_bias, up_bias,
         down_bias, gain_one, shift_one, gain_two, shift_two, cotangent):
    _, B, D = tokens.shape
    FW = down_weight.shape[0]
    DW = D // W
    DP = -(-DW // 128) * 128
    KVW = 2 * DW
    MW = KVW + DP
    R = C // W
    cfg = SimpleNamespace(C=C, W=W, B=B, D=D, FW=FW, DW=DW, DP=DP, KVW=KVW, MW=MW, R=R, HW=HEADS // W)
    cfg.fused = R == 2 and C == 8 and DW % 64 == 0 and FW % (64 * W) == 0
    cfg.keep = R == 2
    cfg.grads = dict(down=(W, FW // W // 2, D // 2, False), up=(W, DW // 4, FW, True), qkv=(W, DW // 4, MW, True),
                     out=(1, DW // 4, D, False))
    w = lax.axis_index("wa")
    small = (out_bias, down_bias, gain_one, shift_one, gain_two, shift_two, qv_bias, up_bias)

    plan = make_plan(cfg)
    names = list(plan)
    vm = pl.BlockSpec(memory_space=pltpu.VMEM)
    hbm = pl.BlockSpec(memory_space=pl.ANY)
    if cfg.fused:
        outs = [(n, 2, 2, ch, cols) for n, ch, cols, _ in (cfg.grads[k] for k in ("qkv", "out", "up", "down"))]
        place = pltpu.VMEM
    else:
        outs = [(D, MW), (DW, D), (D, FW), (FW, D)]
        place = jax.ShapeDtypeStruct
    outs = [place(a, BF) for a in [(B, D), (B, D)] + outs] + [place((GROWS, D) if cfg.fused else (1, GROWS, D), F32)]
    args = (tokens.reshape(B, D), cotangent.reshape(B, D), qkv_weight, out_weight, up_weight, down_weight, lengths, *small)
    y, gx, gqkv, gout, gup, gdown, gvec = pl.pallas_call(
        functools.partial(layer_kernel, cfg, names, len(args)),
        out_shape=outs,
        in_specs=[hbm] * 6 + [pl.BlockSpec(memory_space=pltpu.SMEM)] + [vm] * len(small),
        out_specs=[vm] * len(outs),
        scratch_shapes=[plan[n] for n in names],
        compiler_params=pltpu.CompilerParams(collective_id=0, has_side_effects=True, vmem_limit_bytes=(52 if cfg.fused else 60) << 20),
        name="layer",
    )(*args)
    if cfg.fused:
        return finish(cfg, y, gx, gqkv, gout, gup, gdown, gvec)

    def to_rows(g):
        g = lax.psum(g, "ctx").reshape(W, DW, g.shape[1])
        return lax.all_to_all(g, "wa", 0, 0, tiled=True).transpose(1, 0, 2).reshape(DW, -1)

    gq = to_rows(gqkv).reshape(DW, W, MW).astype(F32)
    gup = to_rows(gup)
    gout, gdown, gvec = lax.psum((gout, gdown, gvec), "ctx")
    gvec = lax.all_gather(gvec, "wa", axis=0, tiled=True)
    gqkv = jnp.concatenate([gq[:, :, a : a + DW].reshape(DW, D) for a in (KVW, 0, DW)], 1)
    own = lax.dynamic_slice_in_dim(jnp.sum(gvec, 0)[0:6], w * DW, DW, 1)
    g_upb = lax.dynamic_slice_in_dim(gvec, w, 1, 0)[0, 6]
    g_qv = jnp.concatenate([gvec[:, 7, KVW : KVW + DW].reshape(D), gvec[:, 7, DW:KVW].reshape(D)])
    g_qv = lax.dynamic_slice_in_dim(g_qv, w * (2 * D // W), 2 * D // W)
    return (y.reshape(1, B, D), gx.reshape(1, B, D), gqkv, gout.astype(F32), gup.astype(F32),
            gdown.astype(F32), g_qv, own[4], g_upb, own[5], own[0], own[1], own[2], own[3])


def finish_kernel(cfg, y, gx, gqkv, gout, gup, gdown, gvec, o_y, o_gx, o_qkv, o_out, o_up, o_down, o_qv, o_outb, o_upb,
                  o_downb, o_g1, o_s1, o_g2, o_s2, f_qkv, f_out, f_up, f_down, sems):
    W, D, DW, MW, KVW = cfg.W, cfg.D, cfg.DW, cfg.MW, cfg.KVW
    copies = [pltpu.make_async_copy(a, b, sems.at[i]) for i, (a, b) in enumerate(
        ((f_down, o_down), (f_up, o_up), (f_qkv, o_qkv), (f_out, o_out)))]
    for x in range(2):
        f_down[:, x * (D // 2) : (x + 1) * (D // 2)] = gdown[:, x].reshape(cfg.FW, D // 2).astype(F32)
    copies[0].start()
    for g in range(W):
        f_up[:, g * cfg.FW : (g + 1) * cfg.FW] = gup[g].reshape(DW, cfg.FW).astype(F32)
    copies[1].start()
    for g in range(W):
        rows = gqkv[g].reshape(DW, MW).astype(F32)
        for third, a in enumerate((KVW, 0, DW)):
            f_qkv[:, third * D + g * DW : third * D + (g + 1) * DW] = rows[:, a : a + DW]
    copies[2].start()
    f_out[...] = gout[...].reshape(f_out.shape).astype(F32)
    copies[3].start()
    o_y[0] = y[...]
    o_gx[0] = gx[...]
    o_qv[...] = gvec[6, 0 : 2 * DW]
    o_upb[...] = gvec[7, 0 : cfg.FW]
    for row, ref in enumerate((o_g1, o_s1, o_g2, o_s2, o_outb, o_downb)):
        ref[...] = gvec[row, 0:DW]
    for cp in copies:
        cp.wait()


def finish(cfg, *arrays):
    B, D, DW, W, FW = cfg.B, cfg.D, cfg.DW, cfg.W, cfg.FW
    shapes = [(1, B, D)] * 2 + [(DW, 3 * D), (DW, D), (DW, W * FW), (FW, D), (2 * DW,), (DW,), (FW,)] + [(DW,)] * 5
    vm = pl.BlockSpec(memory_space=pltpu.VMEM)
    arrays = [pltpu.with_memory_space_constraint(a, pltpu.VMEM) for a in arrays]
    return pl.pallas_call(
        functools.partial(finish_kernel, cfg),
        out_shape=[jax.ShapeDtypeStruct(s, BF if i < 2 else F32) for i, s in enumerate(shapes)],
        in_specs=[vm] * len(arrays),
        out_specs=[vm] * 2 + [pl.BlockSpec(memory_space=pl.ANY)] * 4 + [vm] * 8,
        scratch_shapes=[pltpu.VMEM(s, F32) for s in shapes[2:6]] + [pltpu.SemaphoreType.DMA((4,))],
        compiler_params=pltpu.CompilerParams(vmem_limit_bytes=32 << 20),
        name="results",
    )(*arrays)


def solution(mesh):
    tok, vec, mat = P("wa", "ctx", None), P("wa"), P("wa", None)
    return jax.shard_map(
        functools.partial(body, mesh.shape["ctx"], mesh.shape["wa"]),
        mesh=mesh,
        in_specs=(tok, vec, mat, mat, mat, mat) + (vec,) * 8 + (tok,),
        out_specs=(tok, tok, mat, mat, mat, mat) + (vec,) * 8,
        check_vma=False,
    )
```
